32 devices in a mesh: blk: 4 (over z), uly: 8 (over y, x, core).
Axes of the slice: x: 2, y: 2, z: 4, core: 2. Of those that a mesh axis runs over, the one named last changes fastest.
Arguments:
- queries: bfloat16 [4096, 4096], P(('blk', 'uly')), may hold values from -6 to 6
- keys: bfloat16 [4096, 1024], P(('blk', 'uly')), may hold values from -6 to 6
- values: bfloat16 [4096, 1024], P(('blk', 'uly')), may hold values from -6 to 6
- grad_out: bfloat16 [4096, 4096], P(('blk', 'uly')), may hold values from -6 to 6
- row_delta: float32 [4096, 32], P(('blk', 'uly')), may hold values from -18 to 18
- doc_ids: int32 [4096], replicated, may hold values from 0 to 63, never falling along the last dimension, each value on 1 to 128 neighbouring positions
- doc_lang: int32 [64], replicated, may hold values from 0 to 3
- tile_list: int32 [8, 32, 2], replicated, may hold values from 0 to 31, as said below
Outputs:
- grad_queries: bfloat16 [4096, 4096], P(('blk', 'uly'))
- grad_keys: bfloat16 [4096, 1024], P(('blk', 'uly'))
- grad_values: bfloat16 [4096, 1024], P(('blk', 'uly'))
The draws below stay inside these ranges and needn't reach their ends.
Inputs may be any that keep to these rules, and one draw needn't show every extreme that they name: `doc_ids`: document ids never fall, rise by one where a new document begins, and a document holds at most 128 tokens. `tile_list`: each listed tile of query tile a is at most a and not before the first tile of the block of 8 tiles that precedes the block of a; entries may repeat.
All inputs are finite; a program needn't handle non-finite values.
Results may differ from the reference program's by a relative error of at most 0.0059.
Values may be sent and summed in bfloat16 or wider, within the bound.
A program may use at most 128 MiB of HBM per device.

```python
import math
import jax
import jax.numpy as jnp
import numpy as np
from jax import lax

H = 32
DH = 128
G = 8
BLOCK = 128
LIST = 2
LANGS = 4
ROWS = 1024
SEQ = 4096
DOCS = 64


def draw_queries(key, part):
    drawn = jax.random.normal(jax.random.fold_in(key, 1), (SEQ, H * DH), jnp.float32)
    return jnp.clip(drawn, -6.0, 6.0).astype(jnp.bfloat16)


def draw_keys(key, part):
    drawn = jax.random.normal(jax.random.fold_in(key, 3), (SEQ, G * DH), jnp.float32)
    return jnp.clip(drawn, -6.0, 6.0).astype(jnp.bfloat16)


def draw_tile_list(key, part):
    tile_total = SEQ // BLOCK
    tiles_block = ROWS // BLOCK
    query_tile = jnp.arange(tile_total, dtype=jnp.int32)
    lowest = jnp.maximum((query_tile // tiles_block - 1) * tiles_block, 0)
    spread = query_tile - lowest + 1
    random_bits = jax.random.randint(jax.random.fold_in(key, 31), (G, tile_total, LIST), 0, 1 << 30)
    chosen = lowest[None, :, None] + random_bits % spread[None, :, None]
    chosen = chosen.at[:, tile_total - 1, 0].set(tile_total - 1)
    return chosen.astype(jnp.int32)


def touch_ends(result, rng, least, high):
    place = [jax.random.randint(jax.random.fold_in(rng, axis), (), 0, length) for axis, length in enumerate(result.shape)]
    longest = result.shape.index(max(result.shape))
    neighbour = place[:longest] + [(place[longest] + 1) % result.shape[longest]] + place[longest + 1:]
    return result.at[tuple(place)].set(least).at[tuple(neighbour)].set(high)


def level_of(key, dims, pieces, low, high):
    def one(position, blocks):
        steps = jax.random.uniform(jax.random.fold_in(jax.random.fold_in(key, 6), position), (blocks,), jnp.float32, low / len(pieces), high / len(pieces))
        return jnp.repeat(jnp.exp(steps), dims[position] // blocks).reshape((-1,) + (1,) * (len(dims) - position - 1))

    gain = one(*pieces[0])
    for cut in pieces[1:]:
        gain = gain * one(*cut)
    return gain


def length_profile(number_of, total, reach, skew):
    weights = [(1 << 20) // math.isqrt(standing ** skew) + 1 for standing in range(2, number_of + 1)]
    rest, given = total - reach - (number_of - 1), [1] * (number_of - 1)
    while rest > 0:
        free = [i for i in range(number_of - 1) if given[i] < reach]
        mass, remaining = sum([weights[i] for i in free]), rest
        for i in free:
            extra = min(reach - given[i], max(1, remaining * weights[i] // mass), rest)
            given[i] = given[i] + extra
            rest = rest - extra
    return np.array([reach] + given)


def uneven_parts(key, count, total, limit, slope):
    if count == 2:
        one = jax.random.randint(key, (), max(1, total - limit), min(limit, total - 1) + 1)
        return jnp.stack([one, total - one])
    sizes = jnp.asarray(length_profile(count, total, limit, slope), jnp.int32)
    couples = (count - 1) // 2
    donor, sink = sizes[1:1 + 2 * couples:2], sizes[2:2 + 2 * couples:2]
    margin = jnp.minimum(donor - 1, limit - sink)
    moved = jax.random.randint(jax.random.fold_in(key, 1), (couples,), 0, 1 << 20) % (margin + 1)
    sizes = sizes.at[1:1 + 2 * couples:2].set(donor - moved).at[2:2 + 2 * couples:2].set(sink + moved)
    return sizes[jax.random.permutation(jax.random.fold_in(key, 2), count)]


def noise(key, extent, width, reach, pieces=(), held_as=jnp.bfloat16):
    values = width * jax.random.normal(key, extent, jnp.float32)
    if pieces:
        values = values * level_of(key, extent, pieces, -0.22, 0.18)
    return jnp.clip(values, -reach, reach).astype(held_as)


def setup_inputs(seed: int = 0) -> dict:
    splits = jax.random.split(jax.random.key(seed), 9)
    queries = draw_queries(jax.random.fold_in(splits[8], 71), 0)
    keys = draw_keys(jax.random.fold_in(splits[8], 71), 0)
    values = noise(splits[2], (SEQ, G * DH), 1.0, 6.0, ((0, 32),))
    grad_out = noise(splits[3], (SEQ, H * DH), 1.0, 6.0, ((0, 32),))
    row_delta = noise(splits[4], (SEQ, H), 3.0, 18.0, ((0, 32),), jnp.float32)
    doc_ids = jnp.searchsorted(jnp.cumsum(uneven_parts(splits[5], DOCS, SEQ, BLOCK, 1)), jnp.arange(SEQ), side="right").astype(jnp.int32)
    doc_lang = touch_ends(jax.random.randint(splits[6], (DOCS,), 0, LANGS), jax.random.fold_in(splits[6], 1), 0, LANGS - 1).astype(jnp.int32)
    tile_list = draw_tile_list(jax.random.fold_in(splits[8], 71), 0)
    return dict(queries=queries, keys=keys, values=values, grad_out=grad_out, row_delta=row_delta, doc_ids=doc_ids, doc_lang=doc_lang, tile_list=tile_list)


MASKED = -1e30


def candidates(list_group, query_tiles):
    band_tiles = query_tiles[:, None] + jnp.arange(-1, 1, dtype=jnp.int32)[None, :]
    listed = jnp.take(list_group, query_tiles, axis=0, mode="clip")
    list_count = listed.shape[1]
    in_band = jnp.any(listed[:, :, None] == band_tiles[:, None, :], axis=2)
    earlier = jnp.tril(jnp.ones((list_count, list_count), jnp.bool_), -1)
    repeated = jnp.any((listed[:, :, None] == listed[:, None, :]) & earlier[None], axis=2)
    candidate = jnp.concatenate([band_tiles, listed], axis=1)
    usable = jnp.concatenate([band_tiles >= 0, jnp.logical_not(in_band | repeated)], axis=1)
    marked = jnp.any(candidate[:, :, None] == listed[:, None, :], axis=2)
    return candidate, usable, marked


def allowed_tiles(candidate, usable, marked, query_tiles, doc_ids, position_lang):
    offsets = jnp.arange(BLOCK, dtype=jnp.int32)
    query_pos = query_tiles[:, None] * BLOCK + offsets[None, :]
    key_pos = jnp.maximum(candidate, 0)[:, :, None] * BLOCK + offsets[None, None, :]
    query_doc = jnp.take(doc_ids, query_pos, mode="clip")
    key_doc = jnp.take(doc_ids, key_pos, mode="clip")
    query_lang = jnp.take(position_lang, query_pos, mode="clip")
    key_lang = jnp.take(position_lang, key_pos, mode="clip")
    causal = key_pos[:, :, None, :] <= query_pos[:, None, :, None]
    same_doc = key_doc[:, :, None, :] == query_doc[:, None, :, None]
    same_lang = key_lang[:, :, None, :] == query_lang[:, None, :, None]
    return usable[:, :, None, None] & causal & (same_doc | (same_lang & marked[:, :, None, None]))


def tile_setup(list_group, first_query, window_first, slot_count, tile_group, doc_ids, position_lang):
    query_tiles = first_query + jnp.arange(tile_group, dtype=jnp.int32)
    candidate, usable, marked = candidates(list_group, query_tiles)
    window_slot = candidate - window_first
    usable = usable & (window_slot >= 0) & (window_slot < slot_count)
    window_slot = jnp.clip(window_slot, 0, slot_count - 1)
    allowed = allowed_tiles(candidate, usable, marked, query_tiles, doc_ids, position_lang)
    return window_slot, allowed


def tile_stats(query_part, key_part, allowed, scaling):
    scores = scaling * jnp.einsum("qid,qcjd->qcij", query_part.astype(jnp.float32), key_part.astype(jnp.float32))
    masked = jnp.where(allowed, scores, MASKED)
    row_top = jnp.max(masked, axis=(1, 3))
    row_total = jnp.sum(jnp.where(allowed, jnp.exp(masked - row_top[:, None, :, None]), 0.0), axis=(1, 3))
    return row_top + jnp.log(row_total)


def tile_grads(query_part, dout_part, key_part, value_part, log_total, delta_part, allowed, scaling):
    scores = scaling * jnp.einsum("qid,qcjd->qcij", query_part.astype(jnp.float32), key_part.astype(jnp.float32))
    weights = jnp.where(allowed, jnp.exp(scores - log_total[:, None, :, None]), 0.0)
    weights_low = weights.astype(jnp.bfloat16)
    grad_value = jnp.einsum("qcij,qid->qcjd", weights_low.astype(jnp.float32), dout_part.astype(jnp.float32))
    grad_weights = jnp.einsum("qid,qcjd->qcij", dout_part.astype(jnp.float32), value_part.astype(jnp.float32))
    grad_scores = (weights * (grad_weights - delta_part[:, None, :, None])).astype(jnp.bfloat16)
    grad_query = scaling * jnp.einsum("qcij,qcjd->qid", grad_scores.astype(jnp.float32), key_part.astype(jnp.float32))
    grad_key = scaling * jnp.einsum("qcij,qid->qcjd", grad_scores.astype(jnp.float32), query_part.astype(jnp.float32))
    return grad_query, grad_key, grad_value


def stats_pass(query_one, key_tiles, list_group, first_tile, window_first, doc_ids, position_lang, tile_group, scaling):
    slot_count = key_tiles.shape[0]
    tile_count = query_one.shape[0] // BLOCK

    def stats_step(tile_start):
        window_slot, allowed = tile_setup(list_group, first_tile + tile_start, window_first, slot_count, tile_group,
                                          doc_ids, position_lang)
        query_part = lax.dynamic_slice_in_dim(query_one, tile_start * BLOCK, tile_group * BLOCK).reshape(tile_group, BLOCK, DH)
        key_part = jnp.take(key_tiles, window_slot, axis=0)
        return tile_stats(query_part, key_part, allowed, scaling)

    tile_starts = jnp.arange(tile_count // tile_group, dtype=jnp.int32) * tile_group
    return lax.map(stats_step, tile_starts).reshape(tile_count * BLOCK)


def grad_pass(query_one, dout_one, lse_one, delta_one, key_tiles, value_tiles, list_group, first_tile, window_first,
              doc_ids, position_lang, tile_group, scaling):
    slot_count = key_tiles.shape[0]
    tile_count = query_one.shape[0] // BLOCK

    def scan_step(carried, tile_start):
        key_sum, value_sum = carried
        window_slot, allowed = tile_setup(list_group, first_tile + tile_start, window_first, slot_count, tile_group,
                                          doc_ids, position_lang)
        row_start = tile_start * BLOCK
        row_span = tile_group * BLOCK
        query_part = lax.dynamic_slice_in_dim(query_one, row_start, row_span).reshape(tile_group, BLOCK, DH)
        dout_part = lax.dynamic_slice_in_dim(dout_one, row_start, row_span).reshape(tile_group, BLOCK, DH)
        lse_part = lax.dynamic_slice_in_dim(lse_one, row_start, row_span).reshape(tile_group, BLOCK)
        delta_part = lax.dynamic_slice_in_dim(delta_one, row_start, row_span).reshape(tile_group, BLOCK)
        key_part = jnp.take(key_tiles, window_slot, axis=0)
        value_part = jnp.take(value_tiles, window_slot, axis=0)
        grad_query, grad_key, grad_value = tile_grads(query_part, dout_part, key_part, value_part, lse_part, delta_part,
                                                      allowed, scaling)
        flat_slot = window_slot.reshape(-1)
        key_sum = key_sum.at[flat_slot].add(grad_key.reshape(-1, BLOCK, DH))
        value_sum = value_sum.at[flat_slot].add(grad_value.reshape(-1, BLOCK, DH))
        return (key_sum, value_sum), grad_query

    zero_tiles = jnp.zeros((slot_count, BLOCK, DH), jnp.float32)
    tile_starts = jnp.arange(tile_count // tile_group, dtype=jnp.int32) * tile_group
    sums, grad_query = lax.scan(scan_step, (zero_tiles, zero_tiles), tile_starts)
    return grad_query.reshape(-1, DH), sums[0].reshape(-1, DH), sums[1].reshape(-1, DH)


def reference(queries, keys, values, grad_out, row_delta, doc_ids, doc_lang, tile_list):
    seq_count = queries.shape[0]
    repeat_count = H // G
    scaling = float(DH) ** -0.5
    tile_total = seq_count // BLOCK
    tile_group = math.gcd(tile_total, 32)
    position_lang = jnp.take(doc_lang, doc_ids, mode="clip").astype(jnp.int32)

    def key_head(group_id):
        key_one = lax.dynamic_slice_in_dim(keys, group_id * DH, DH, axis=1)
        value_one = lax.dynamic_slice_in_dim(values, group_id * DH, DH, axis=1)
        list_group = lax.dynamic_index_in_dim(tile_list, group_id, 0, keepdims=False)
        key_tiles = key_one.reshape(tile_total, BLOCK, DH)
        value_tiles = value_one.reshape(tile_total, BLOCK, DH)
        key_total = jnp.zeros((seq_count, DH), jnp.float32)
        value_total = jnp.zeros((seq_count, DH), jnp.float32)
        query_grads = []
        for member in range(repeat_count):
            head = group_id * repeat_count + member
            query_one = lax.dynamic_slice_in_dim(queries, head * DH, DH, axis=1)
            dout_one = lax.dynamic_slice_in_dim(grad_out, head * DH, DH, axis=1)
            delta_one = lax.dynamic_index_in_dim(row_delta, head, 1, keepdims=False)
            zero_index = jnp.zeros((), jnp.int32)
            log_total = stats_pass(query_one, key_tiles, list_group, zero_index, zero_index, doc_ids, position_lang,
                                   tile_group, scaling)
            grad_query, head_key, head_value = grad_pass(query_one, dout_one, log_total, delta_one, key_tiles, value_tiles,
                                                         list_group, zero_index, zero_index, doc_ids, position_lang,
                                                         tile_group, scaling)
            key_total = key_total + lax.optimization_barrier(head_key.astype(jnp.bfloat16)).astype(jnp.float32)
            value_total = value_total + lax.optimization_barrier(head_value.astype(jnp.bfloat16)).astype(jnp.float32)
            query_grads.append(grad_query.astype(jnp.bfloat16))
        return jnp.stack(query_grads), key_total.astype(jnp.bfloat16), value_total.astype(jnp.bfloat16)

    grad_query, grad_key, grad_value = lax.map(key_head, jnp.arange(G, dtype=jnp.int32))
    grad_queries = grad_query.transpose(2, 0, 1, 3).reshape(seq_count, H * DH)
    grad_keys = grad_key.transpose(1, 0, 2).reshape(seq_count, G * DH)
    grad_values = grad_value.transpose(1, 0, 2).reshape(seq_count, G * DH)
    return grad_queries, grad_keys, grad_values
```

```python
import functools

import jax
import jax.numpy as jnp
from jax import lax
from jax.experimental import pallas as pl
from jax.experimental.pallas import tpu as pltpu
from jax.sharding import PartitionSpec as P

DH = 128
BLOCK = 128
LANGS = 4
MASKED = -1e30
MESH = pl.DeviceIdType.MESH
LOOK = 7
CHUNKS = 4
SPLIT = 8
HALF = 4
LOG2_E = 1.4426950408889634
VMEM_LIMIT = 56 * 1024 * 1024


def greet(b, u, n_blk, n_uly):
    barrier = pltpu.get_barrier_semaphore()
    for p in range(1, n_uly):
        pl.semaphore_signal(
            barrier, inc=1, device_id=(b, lax.rem(u + p, n_uly)), device_id_type=MESH
        )

    @pl.when(b > 0)
    def _():
        pl.semaphore_signal(barrier, inc=1, device_id=(b - 1, u), device_id_type=MESH)

    @pl.when(b < n_blk - 1)
    def _():
        pl.semaphore_signal(barrier, inc=1, device_id=(b + 1, u), device_id_type=MESH)

    ends = jnp.where(b > 0, 1, 0) + jnp.where(b < n_blk - 1, 1, 0)
    pl.semaphore_wait(barrier, n_uly - 1 + ends)


def aligned(start, size):
    return pl.ds(pl.multiple_of(start, size), size)


def partner(u, s, n):
    found, bit = 0, 1
    while bit < n:
        found = found + bit * lax.rem(lax.div(u, bit) + lax.div(s, bit), 2)
        bit *= 2
    return found


def fused_kernel(
    n_blk,
    n_uly,
    list_count,
    heads_here,
    repeat_count,
    list_hbm,
    lang_hbm,
    docs_hbm,
    q_ref,
    do_ref,
    k_ref,
    v_ref,
    dl_ref,
    dq_ref,
    dk_ref,
    dv_ref,
    q_all,
    do_all,
    dl_all,
    window,
    list_ref,
    lang_ref,
    code_ref,
    key_codes,
    acc,
    dq_all,
    back,
    returned,
    total,
    landing,
    in_send,
    in_recv,
    local_sem,
    z_send,
    z_recv,
    back_send,
    back_recv,
    out_send,
    out_recv,
    out_local,
    table_sem,
):
    b, u = lax.axis_index("blk"), lax.axis_index("uly")
    tiles_here = n_uly
    width = heads_here * DH
    copies = repeat_count // heads_here
    direct = copies == 1
    f32 = jnp.float32
    my_cols = aligned(u * width, width)
    my_group = aligned(u * DH, DH)
    peer_of = functools.partial(partner, u, n=n_uly)

    def pieces(peer):
        group = lax.div(peer * heads_here, repeat_count)
        kv_cols = aligned(group * DH, DH)
        q_cols = aligned(peer * width, width)
        return (
            (k_ref.at[:, kv_cols], window.at[tiles_here + u, 0]),
            (v_ref.at[:, kv_cols], window.at[tiles_here + u, 1]),
            (dl_ref.at[peer], dl_all.at[u]),
            (q_ref.at[:, q_cols], q_all.at[u]),
            (do_ref.at[:, q_cols], do_all.at[u]),
        )

    def out_pieces(peer):
        if direct:
            ends = (dk_ref.at[:, my_group], dv_ref.at[:, my_group])
        else:
            ends = (landing.at[0, u], landing.at[1, u])
        return (
            (total.at[peer, 0], ends[0]),
            (total.at[peer, 1], ends[1]),
            (dq_all.at[peer], dq_ref.at[:, my_cols]),
        )

    def remote(parts, kind, s, send, recv):
        peer = peer_of(s)
        src, dst = parts(peer)[kind]
        return pltpu.make_async_remote_copy(
            src_ref=src,
            dst_ref=dst,
            send_sem=send.at[kind, s],
            recv_sem=recv.at[kind, s],
            device_id=(b, peer),
            device_id_type=MESH,
        )

    def inward(kind, s):
        return remote(pieces, kind, s, in_send, in_recv)

    def outward(kind, s):
        return remote(out_pieces, kind, s, out_send, out_recv)

    def local(kind):
        src, dst = pieces(u)[kind]
        return pltpu.make_async_copy(src, dst, local_sem.at[kind])

    def out_own(kind):
        src, dst = out_pieces(u)[kind]
        return pltpu.make_async_copy(src, dst, out_local.at[kind])

    def forward(a):
        return pltpu.make_async_remote_copy(
            src_ref=window.at[tiles_here + a],
            dst_ref=window.at[a],
            send_sem=z_send.at[a],
            recv_sem=z_recv.at[a],
            device_id=(lax.rem(b + 1, n_blk), u),
            device_id_type=MESH,
        )

    def backward(a):
        return pltpu.make_async_remote_copy(
            src_ref=back.at[a],
            dst_ref=returned.at[a],
            send_sem=back_send.at[a],
            recv_sem=back_recv.at[a],
            device_id=(lax.rem(b + n_blk - 1, n_blk), u),
            device_id_type=MESH,
        )

    def each(first, last, body):
        lax.fori_loop(first, last, lambda s, _: (body(s), 0)[1], 0)

    has_next = b < n_blk - 1
    has_prev = b > 0

    tables = (
        pltpu.make_async_copy(list_hbm, list_ref, table_sem.at[0]),
        pltpu.make_async_copy(lang_hbm, lang_ref, table_sem.at[1]),
        pltpu.make_async_copy(
            docs_hbm.at[aligned(jnp.maximum(b - 1, 0) * tiles_here, tiles_here), :],
            code_ref.at[pl.ds(0, tiles_here), :],
            table_sem.at[2],
        ),
        pltpu.make_async_copy(
            docs_hbm.at[aligned(b * tiles_here, tiles_here), :],
            code_ref.at[pl.ds(tiles_here, tiles_here), :],
            table_sem.at[3],
        ),
    )
    for kind in range(5):
        local(kind).start()
    for table in tables:
        table.start()
    greet(b, u, n_blk, n_uly)

    def send_keys(s):
        inward(0, s).start()
        inward(1, s).start()

    def send_rows(s):
        inward(2, s).start()
        inward(3, s).start()
        inward(4, s).start()

    each(1, n_uly, send_keys)
    each(1, min(LOOK, n_uly - 1) + 1, send_rows)
    local(0).wait()
    local(1).wait()

    @pl.when(has_next)
    def _():
        forward(u).start()

    for table in tables:
        table.wait()
    docs = code_ref[...]

    def look_up(d, lang):
        return lang + jnp.where(docs == d, lang_ref[d], 0)

    lang = lax.fori_loop(0, lang_ref.shape[0], look_up, jnp.zeros_like(docs))
    code_ref[...] = docs * LANGS + lang

    def prepare(t):
        key_codes[t] = jnp.broadcast_to(code_ref[pl.ds(t, 1), :], (BLOCK, BLOCK)).T
        acc[t] = jnp.zeros(acc.shape[1:], f32)

    each(0, 2 * tiles_here, prepare)

    @pl.when(b == 0)
    def _():
        window[0:tiles_here] = jnp.zeros((tiles_here,) + window.shape[1:], window.dtype)

    def pass_on(s):
        inward(0, s).wait_recv()
        inward(1, s).wait_recv()

        @pl.when(has_next)
        def _():
            forward(peer_of(s)).start()

    each(1, n_uly, pass_on)

    @pl.when(has_prev)
    def _():
        each(0, tiles_here, lambda a: forward(a).wait_recv())

    local(2).wait()
    local(3).wait()
    local(4).wait()

    scaling = float(DH) ** (-0.5)
    across = (((1,), (1,)), ((), ()))
    gap = lax.broadcasted_iota(jnp.int32, (BLOCK, BLOCK), 0) - lax.broadcasted_iota(
        jnp.int32, (BLOCK, BLOCK), 1
    )
    group_here = lax.div(u * heads_here, repeat_count)

    def tile_work(a):
        tile = b * tiles_here + a
        listed = [list_ref[group_here, l, tile] for l in range(list_count)]
        cands = [tile - 1, tile] + listed
        own_slot = tiles_here + a
        window_first = (b - 1) * tiles_here
        query_code = code_ref[pl.ds(own_slot, 1), :]
        query_lang = query_code & (LANGS - 1)
        slots = []
        biases = []
        for c, cand in enumerate(cands):
            usable = cand >= 0
            for other in cands[: c if c >= 2 else 0]:
                usable = usable & (cand != other)
            marked = cand == listed[0]
            for other in listed[1:]:
                marked = marked | (cand == other)
            if c < 2:
                slot = own_slot - 1 + c
            else:
                slot = jnp.clip(cand - window_first, 0, 2 * tiles_here - 1)
            limit = jnp.where(usable, (tile - cand) * BLOCK, -2 * BLOCK)
            seen_lang = jnp.where(marked, query_lang, -1)
            key_code = key_codes[slot]
            allowed = (gap <= limit) & (
                (key_code == query_code) | ((key_code & (LANGS - 1)) == seen_lang)
            )
            slots.append(slot)
            biases.append(jnp.where(allowed, 0.0, MASKED))

        def stacked(rows):
            return jnp.concatenate([rows[:, h * DH : (h + 1) * DH] for h in range(heads_here)], 0)

        bias = jnp.concatenate(biases, axis=0)
        bias = jnp.concatenate([bias] * heads_here, axis=1)
        key_part = jnp.concatenate([window[s, 0] for s in slots], axis=0)
        value_part = jnp.concatenate([window[s, 1] for s in slots], axis=0)
        query_part = stacked(q_all[a])
        dout_part = stacked(do_all[a])
        delta_tile = dl_all[a]
        delta = jnp.concatenate([delta_tile[h : h + 1, :] for h in range(heads_here)], axis=1)
        scores = lax.dot_general(key_part, query_part, across, preferred_element_type=f32)
        scores = scores * scaling + bias
        top = jnp.max(scores, axis=0, keepdims=True)
        raised = jnp.exp(scores - top)
        weights = raised * (1.0 / jnp.sum(raised, axis=0, keepdims=True))
        grad_weights = lax.dot_general(value_part, dout_part, across, preferred_element_type=f32)
        grad_scores = (weights * (grad_weights - delta)).astype(jnp.bfloat16)
        grad_query = scaling * lax.dot_general(
            grad_scores, key_part, (((0,), (0,)), ((), ())), preferred_element_type=f32
        )
        for h in range(heads_here):
            dq_all[a, :, h * DH : (h + 1) * DH] = grad_query[h * BLOCK : (h + 1) * BLOCK].astype(
                dq_all.dtype
            )
        grad_key = scaling * jnp.dot(grad_scores, query_part, preferred_element_type=f32)
        grad_value = jnp.dot(weights.astype(jnp.bfloat16), dout_part, preferred_element_type=f32)
        parts = (grad_key, grad_value)
        for c in range(2):
            for k in range(2):
                acc[slots[c], k] += parts[k][c * BLOCK : (c + 1) * BLOCK]

        def spread(t):
            for k in range(2):
                more = acc[t, k]
                for c in range(2, 2 + list_count):
                    piece = parts[k][c * BLOCK : (c + 1) * BLOCK]
                    more = more + jnp.where(slots[c] == t, piece, 0.0)
                acc[t, k] = more

        each(0, 2 * tiles_here, spread)

    tile_work(u)
    out_own(2).start()

    def step(s):
        @pl.when(s + LOOK < n_uly)
        def _():
            send_rows(s + LOOK)

        inward(2, s).wait_recv()
        inward(3, s).wait_recv()
        inward(4, s).wait_recv()
        tile_work(peer_of(s))
        outward(2, s).start()

    each(1, n_uly, step)

    @pl.when(has_prev)
    def _():
        def give_back(s):
            a = peer_of(s)
            back[a] = acc[a].astype(back.dtype)
            backward(a).start()

        each(0, n_uly, give_back)

    def settle(s):
        a = peer_of(s)

        @pl.when(has_next)
        def _():
            backward(a).wait_recv()
            total[a] = (acc[tiles_here + a] + returned[a].astype(f32)).astype(total.dtype)

        @pl.when(b == n_blk - 1)
        def _():
            total[a] = acc[tiles_here + a].astype(total.dtype)

    settle(0)
    out_own(0).start()
    out_own(1).start()

    def settle_and_send(s):
        settle(s)
        outward(0, s).start()
        outward(1, s).start()

    each(1, n_uly, settle_and_send)

    for kind in range(3):
        out_own(kind).wait()

    def finish(s):
        for kind in range(3):
            outward(kind, s).wait_recv()
        for kind in range(5):
            inward(kind, s).wait_send()
        for kind in range(3):
            outward(kind, s).wait_send()

    each(1, n_uly, finish)

    @pl.when(has_next)
    def _():
        each(0, n_uly, lambda a: forward(a).wait_send())

    @pl.when(has_prev)
    def _():
        each(0, n_uly, lambda a: backward(a).wait_send())

    if not direct:
        for kind, out in ((0, dk_ref), (1, dv_ref)):
            for g in range(n_uly // copies):
                summed = landing[kind, g * copies].astype(f32)
                for r in range(1, copies):
                    summed = summed + landing[kind, g * copies + r].astype(f32)
                out[:, g * DH : (g + 1) * DH] = summed.astype(out.dtype)


def split_kernel(
    n_blk,
    list_count,
    list_hbm,
    lang_hbm,
    docs_hbm,
    q_ref,
    do_ref,
    k_ref,
    v_ref,
    dl_ref,
    dq_ref,
    dk_ref,
    dv_ref,
    q_all,
    do_all,
    dl_all,
    window_row,
    window_column,
    list_ref,
    lang_ref,
    order_ref,
    same_ref,
    place_ref,
    code_ref,
    key_codes,
    acc,
    entries,
    sums,
    dq_all,
    back,
    returned,
    across_out,
    across_in,
    total,
    in_send,
    in_recv,
    local_sem,
    relay_send,
    relay_recv,
    z_send,
    z_recv,
    back_send,
    back_recv,
    across_send,
    across_recv,
    out_send,
    out_recv,
    out_local,
    table_sem,
):
    b, u = lax.axis_index("blk"), lax.axis_index("uly")
    y, x, c = lax.div(u, 4), lax.rem(lax.div(u, 2), 2), lax.rem(u, 2)
    tiles_here = SPLIT
    width = HALF * DH
    f32 = jnp.float32
    windows = (window_row, window_column)
    has_next = b < n_blk - 1
    has_prev = b > 0

    def member(j, s, far):
        along, near = lax.div(s, 2), lax.rem(s, 2)
        row = lax.rem(y + (along if j == 1 else far), 2)
        column = lax.rem(x + (along if j == 0 else far), 2)
        return 4 * row + 2 * column + lax.rem(c + near, 2)

    def peer_of(j, s):
        return member(j, s, 0)

    def far_of(j, s):
        return member(j, s, 1)

    def group_of(j, s):
        along, near = lax.div(s, 2), lax.rem(s, 2)
        return HALF * j + 2 * lax.rem((x if j == 0 else y) + along, 2) + lax.rem(c + near, 2)

    def pieces(j, s):
        group = group_of(j, s)
        kv_cols = aligned(group * DH, DH)
        q_cols = aligned(group * width, width)
        return (
            (k_ref.at[:, kv_cols], windows[j].at[tiles_here + u, 0]),
            (v_ref.at[:, kv_cols], windows[j].at[tiles_here + u, 1]),
            (dl_ref.at[group], dl_all.at[j, s]),
            (q_ref.at[:, q_cols], q_all.at[j, s]),
            (do_ref.at[:, q_cols], do_all.at[j, s]),
        )

    def out_pieces(j, s):
        group = group_of(j, 0)
        kv_cols = aligned(group * DH, DH)
        return (
            (total.at[j, s, 0], dk_ref.at[:, kv_cols]),
            (total.at[j, s, 1], dv_ref.at[:, kv_cols]),
            (dq_all.at[j, s], dq_ref.at[:, aligned(group * width, width)]),
        )

    def remote(src, dst, send, recv, device):
        return pltpu.make_async_remote_copy(
            src_ref=src, dst_ref=dst, send_sem=send, recv_sem=recv, device_id=device, device_id_type=MESH
        )

    def inward(j, kind, s):
        src, dst = pieces(j, s)[kind]
        return remote(src, dst, in_send.at[j, kind, s], in_recv.at[j, kind, s], (b, peer_of(j, s)))

    def outward(j, kind, s):
        src, dst = out_pieces(j, s)[kind]
        return remote(src, dst, out_send.at[j, kind, s], out_recv.at[j, kind, s], (b, peer_of(j, s)))

    def local(j, kind):
        src, dst = pieces(j, 0)[kind]
        return pltpu.make_async_copy(src, dst, local_sem.at[j, kind])

    def out_own(j, kind):
        src, dst = out_pieces(j, 0)[kind]
        return pltpu.make_async_copy(src, dst, out_local.at[j, kind])

    def relay(j, s):
        held = windows[j].at[tiles_here + peer_of(j, s)]
        return remote(held, held, relay_send.at[j, s], relay_recv.at[j, s], (b, far_of(j, 0)))

    def forward(j, a):
        return remote(
            windows[j].at[tiles_here + a],
            windows[j].at[a],
            z_send.at[j, a],
            z_recv.at[j, a],
            (lax.rem(b + 1, n_blk), u),
        )

    def backward(j, a):
        return remote(
            back.at[j, a],
            returned.at[j, a],
            back_send.at[j, a],
            back_recv.at[j, a],
            (lax.rem(b + n_blk - 1, n_blk), u),
        )

    def over(j, s):
        return remote(
            across_out.at[j, s],
            across_in.at[j, s],
            across_send.at[j, s],
            across_recv.at[j, s],
            (b, far_of(j, 0)),
        )

    def each(first, last, body):
        lax.fori_loop(first, last, lambda s, _: (body(s), 0)[1], 0)

    def send_on(j, a):
        @pl.when(has_next)
        def _():
            forward(j, a).start()

    tables = (
        pltpu.make_async_copy(list_hbm, list_ref, table_sem.at[0]),
        pltpu.make_async_copy(lang_hbm, lang_ref, table_sem.at[1]),
        pltpu.make_async_copy(
            docs_hbm.at[aligned(jnp.maximum(b - 1, 0) * tiles_here, tiles_here), :],
            code_ref.at[pl.ds(0, tiles_here), :],
            table_sem.at[2],
        ),
        pltpu.make_async_copy(
            docs_hbm.at[aligned(b * tiles_here, tiles_here), :],
            code_ref.at[pl.ds(tiles_here, tiles_here), :],
            table_sem.at[3],
        ),
    )
    for j in range(2):
        for kind in range(5):
            local(j, kind).start()
    for table in tables:
        table.start()

    barrier = pltpu.get_barrier_semaphore()
    friends = [peer_of(0, 1), peer_of(0, 2), peer_of(0, 3), peer_of(1, 2), peer_of(1, 3)]
    for friend in friends:
        pl.semaphore_signal(barrier, inc=1, device_id=(b, friend), device_id_type=MESH)

    @pl.when(has_prev)
    def _():
        pl.semaphore_signal(barrier, inc=1, device_id=(b - 1, u), device_id_type=MESH)

    @pl.when(has_next)
    def _():
        pl.semaphore_signal(barrier, inc=1, device_id=(b + 1, u), device_id_type=MESH)

    ends = jnp.where(has_prev, 1, 0) + jnp.where(has_next, 1, 0)
    pl.semaphore_wait(barrier, len(friends) + ends)

    def start_keys(j):
        def body(s):
            inward(j, 0, s).start()
            inward(j, 1, s).start()

        each(1, HALF, body)

    def start_rows(j):
        def body(s):
            for kind in (2, 3, 4):
                inward(j, kind, s).start()

        each(1, HALF, body)

    def keys_here(j, s):
        inward(j, 0, s).wait_recv()
        inward(j, 1, s).wait_recv()

    start_keys(0)
    start_keys(1)
    start_rows(0)
    local(0, 0).wait()
    local(0, 1).wait()
    relay(0, 0).start()
    send_on(0, u)

    def pass_first(s):
        keys_here(0, s)
        relay(0, s).start()
        send_on(0, peer_of(0, s))

    each(1, HALF, pass_first)
    start_rows(1)
    local(1, 0).wait()
    local(1, 1).wait()
    relay(1, 0).start()

    def pass_second(s):
        keys_here(1, s)
        relay(1, s).start()

    each(1, HALF, pass_second)

    for table in tables:
        table.wait()
    docs = code_ref[...]

    def look_up(d, lang):
        return lang + jnp.where(docs == d, lang_ref[d], 0)

    lang = lax.fori_loop(0, lang_ref.shape[0], look_up, jnp.zeros_like(docs))
    code_ref[...] = docs * LANGS + lang

    def pass_far(s):
        relay(0, s).wait_recv()
        send_on(0, far_of(0, s))

    each(0, HALF, pass_far)
    each(0, HALF, lambda s: send_on(1, peer_of(1, s)))

    window_first = (b - 1) * tiles_here

    def slot_of(cand):
        return jnp.clip(cand - window_first, 0, 2 * tiles_here - 1)

    def plan(j):
        group = group_of(j, 0)
        count = HALF * list_count
        slots = [
            slot_of(list_ref[group, l, b * tiles_here + peer_of(j, s)]) for s in range(HALF) for l in range(list_count)
        ]
        ranks = []
        for e in range(count):
            rank = 0
            for other in range(count):
                if other < e:
                    rank = rank + jnp.where(slots[other] <= slots[e], 1, 0)
                elif other > e:
                    rank = rank + jnp.where(slots[other] < slots[e], 1, 0)
            ranks.append(rank)
        before = -1
        for i in range(count):
            entry, slot = 0, 0
            for e in range(count):
                entry = entry + jnp.where(ranks[e] == i, e, 0)
                slot = slot + jnp.where(ranks[e] == i, slots[e], 0)
            order_ref[j, i] = entry
            same_ref[j, i] = jnp.where(slot == before, 1, 0)
            before = slot
        for t in range(2 * tiles_here):
            upto, here = 0, 0
            for slot in slots:
                upto = upto + jnp.where(slot <= t, 1, 0)
                here = here + jnp.where(slot == t, 1, 0)
            place_ref[j, t] = jnp.where(here > 0, upto - 1, count)

    def prepare(t):
        key_codes[t] = jnp.broadcast_to(code_ref[pl.ds(t, 1), :], (BLOCK, BLOCK)).T
        acc[0, t] = jnp.zeros(acc.shape[2:], f32)
        acc[1, t] = jnp.zeros(acc.shape[2:], f32)

    each(0, 2 * tiles_here, prepare)
    for j in range(2):
        plan(j)
        sums[j, HALF * list_count] = jnp.zeros(sums.shape[2:], f32)

    @pl.when(b == 0)
    def _():
        for window in windows:
            window[0:tiles_here] = jnp.zeros((tiles_here,) + window.shape[1:], window.dtype)

    scaling = float(DH) ** (-0.5)
    across = (((1,), (1,)), ((), ()))
    gap = lax.broadcasted_iota(jnp.int32, (BLOCK, BLOCK), 0) - lax.broadcasted_iota(
        jnp.int32, (BLOCK, BLOCK), 1
    )

    def tile_work(j, s):
        group = group_of(j, 0)
        place = peer_of(j, s)
        tile = b * tiles_here + place
        listed = [list_ref[group, l, tile] for l in range(list_count)]
        cands = [tile - 1, tile] + listed
        own_slot = tiles_here + place
        query_code = code_ref[pl.ds(own_slot, 1), :]
        query_lang = query_code & (LANGS - 1)
        slots = []
        biases = []
        for n, cand in enumerate(cands):
            usable = cand >= 0
            for other in cands[: n if n >= 2 else 0]:
                usable = usable & (cand != other)
            marked = cand == listed[0]
            for other in listed[1:]:
                marked = marked | (cand == other)
            slot = own_slot - 1 + n if n < 2 else slot_of(cand)
            limit = jnp.where(usable, (tile - cand) * BLOCK, -2 * BLOCK)
            seen_lang = jnp.where(marked, query_lang, -1)
            key_code = key_codes[slot]
            allowed = (gap <= limit) & (
                (key_code == query_code) | ((key_code & (LANGS - 1)) == seen_lang)
            )
            slots.append(slot)
            biases.append(jnp.where(allowed, 0.0, MASKED))

        def stacked(rows):
            return jnp.concatenate([rows[:, h * DH : (h + 1) * DH] for h in range(HALF)], 0)

        bias = jnp.concatenate(biases, axis=0)
        bias = jnp.concatenate([bias] * HALF, axis=1)
        key_part = jnp.concatenate([windows[j][t, 0] for t in slots], axis=0)
        value_part = jnp.concatenate([windows[j][t, 1] for t in slots], axis=0)
        query_part = stacked(q_all[j, s])
        dout_part = stacked(do_all[j, s])
        delta_tile = dl_all[j, s]
        delta = jnp.concatenate([delta_tile[h : h + 1, :] for h in range(HALF)], axis=1)
        scores = lax.dot_general(key_part, query_part, across, preferred_element_type=f32)
        scores = scores * (scaling * LOG2_E) + bias
        top = jnp.max(scores, axis=0, keepdims=True)
        raised = jnp.exp2(scores - top)
        weights = raised * (1.0 / jnp.sum(raised, axis=0, keepdims=True))
        grad_weights = lax.dot_general(value_part, dout_part, across, preferred_element_type=f32)
        grad_scores = (weights * (grad_weights - delta)).astype(jnp.bfloat16)
        grad_query = scaling * lax.dot_general(
            grad_scores, key_part, (((0,), (0,)), ((), ())), preferred_element_type=f32
        )
        for h in range(HALF):
            dq_all[j, s, :, h * DH : (h + 1) * DH] = grad_query[h * BLOCK : (h + 1) * BLOCK].astype(
                dq_all.dtype
            )
        grad_key = scaling * jnp.dot(grad_scores, query_part, preferred_element_type=f32)
        grad_value = jnp.dot(weights.astype(jnp.bfloat16), dout_part, preferred_element_type=f32)
        for k, part in ((0, grad_key), (1, grad_value)):
            for n in range(2):
                acc[j, slots[n], k] += part[n * BLOCK : (n + 1) * BLOCK]
            for l in range(list_count):
                first = (2 + l) * BLOCK
                entries[s * list_count + l, k] = part[first : first + BLOCK]

    def add_listed(j):
        sums[j, 0] = entries[order_ref[j, 0]]

        def body(i):
            earlier = jnp.where(same_ref[j, i] == 1, sums[j, i - 1], 0.0)
            sums[j, i] = entries[order_ref[j, i]] + earlier

        each(1, HALF * list_count, body)

    def slot_sum(j, t):
        return acc[j, t] + sums[j, place_ref[j, t]]

    def arrived(j):
        @pl.when(has_prev)
        def _():
            each(0, tiles_here, lambda a: forward(j, a).wait_recv())

    def give_back(j):
        add_listed(j)

        @pl.when(has_prev)
        def _():
            def body(s):
                for a in (far_of(j, s), peer_of(j, s)):
                    back[j, a] = slot_sum(j, a).astype(back.dtype)
                    backward(j, a).start()

            each(0, HALF, body)

    def work(j, s):
        @pl.when(s > 0)
        def _():
            for kind in (2, 3, 4):
                inward(j, kind, s).wait_recv()

        tile_work(j, s)

        @pl.when(s > 0)
        def _():
            outward(j, 2, s).start()

        @pl.when(s == 0)
        def _():
            out_own(j, 2).start()

    arrived(0)
    for kind in (2, 3, 4):
        local(0, kind).wait()

    def first_step(s):
        work(0, s)
        relay(1, s).wait_recv()
        send_on(1, far_of(1, s))

    each(0, HALF, first_step)
    give_back(0)
    arrived(1)
    for kind in (2, 3, 4):
        local(1, kind).wait()
    each(0, HALF, lambda s: work(1, s))
    give_back(1)

    def with_returned(j, a, then):
        @pl.when(has_next)
        def _():
            backward(j, a).wait_recv()
            then(slot_sum(j, tiles_here + a) + returned[j, a].astype(f32))

        @pl.when(b == n_blk - 1)
        def _():
            then(slot_sum(j, tiles_here + a))

    def settle_far(j, s):
        def then(value):
            across_out[j, s] = value.astype(across_out.dtype)

        with_returned(j, far_of(j, s), then)
        over(j, s).start()

    def settle(j, s):
        over(j, s).wait_recv()

        def then(value):
            total[j, s] = (value + across_in[j, s].astype(f32)).astype(total.dtype)

        with_returned(j, peer_of(j, s), then)

        @pl.when(s > 0)
        def _():
            outward(j, 0, s).start()
            outward(j, 1, s).start()

        @pl.when(s == 0)
        def _():
            out_own(j, 0).start()
            out_own(j, 1).start()

    for j in range(2):
        each(0, HALF, lambda s: settle_far(j, s))
        each(0, HALF, lambda s: settle(j, s))

    for j in range(2):
        for kind in range(3):
            out_own(j, kind).wait()

        def finish(s):
            for kind in range(3):
                outward(j, kind, s).wait_recv()
            for kind in range(5):
                inward(j, kind, s).wait_send()
            for kind in range(3):
                outward(j, kind, s).wait_send()

        each(1, HALF, finish)

        def finish_far(s):
            relay(j, s).wait_send()
            over(j, s).wait_send()

        each(0, HALF, finish_far)

        @pl.when(has_next)
        def _():
            each(0, tiles_here, lambda a: forward(j, a).wait_send())

        @pl.when(has_prev)
        def _():
            each(0, tiles_here, lambda a: backward(j, a).wait_send())


def split_grads(lists, doc_lang, docs, queries, grad_out, keys, values, delta_rows, n_blk):
    list_count = lists.shape[1]
    width = HALF * DH
    anywhere = pl.BlockSpec(memory_space=pl.ANY)
    bf16, f32 = jnp.bfloat16, jnp.float32
    pair = (2, BLOCK, DH)
    dma = pltpu.SemaphoreType.DMA
    entry_count = HALF * list_count
    return pl.pallas_call(
        functools.partial(split_kernel, n_blk, list_count),
        out_shape=(
            jax.ShapeDtypeStruct(queries.shape, bf16),
            jax.ShapeDtypeStruct(keys.shape, bf16),
            jax.ShapeDtypeStruct(values.shape, bf16),
        ),
        in_specs=[anywhere] * 8,
        out_specs=(anywhere,) * 3,
        scratch_shapes=[
            pltpu.VMEM((2, HALF, BLOCK, width), bf16),
            pltpu.VMEM((2, HALF, BLOCK, width), bf16),
            pltpu.VMEM((2, HALF, HALF, BLOCK), f32),
            pltpu.VMEM((2 * SPLIT,) + pair, bf16),
            pltpu.VMEM((2 * SPLIT,) + pair, bf16),
            pltpu.SMEM(lists.shape, jnp.int32),
            pltpu.SMEM(doc_lang.shape, jnp.int32),
            pltpu.SMEM((2, entry_count), jnp.int32),
            pltpu.SMEM((2, entry_count), jnp.int32),
            pltpu.SMEM((2, 2 * SPLIT), jnp.int32),
            pltpu.VMEM((2 * SPLIT, BLOCK), jnp.int32),
            pltpu.VMEM((2 * SPLIT, BLOCK, BLOCK), jnp.int32),
            pltpu.VMEM((2, 2 * SPLIT) + pair, f32),
            pltpu.VMEM((entry_count,) + pair, f32),
            pltpu.VMEM((2, entry_count + 1) + pair, f32),
            pltpu.VMEM((2, HALF, BLOCK, width), bf16),
            pltpu.VMEM((2, SPLIT) + pair, bf16),
            pltpu.VMEM((2, SPLIT) + pair, bf16),
            pltpu.VMEM((2, HALF) + pair, bf16),
            pltpu.VMEM((2, HALF) + pair, bf16),
            pltpu.VMEM((2, HALF) + pair, bf16),
            dma((2, 5, HALF)),
            dma((2, 5, HALF)),
            dma((2, 5)),
            dma((2, HALF)),
            dma((2, HALF)),
            dma((2, SPLIT)),
            dma((2, SPLIT)),
            dma((2, SPLIT)),
            dma((2, SPLIT)),
            dma((2, HALF)),
            dma((2, HALF)),
            dma((2, 3, HALF)),
            dma((2, 3, HALF)),
            dma((2, 3)),
            dma((4,)),
        ],
        compiler_params=pltpu.CompilerParams(
            collective_id=0, has_side_effects=True, vmem_limit_bytes=VMEM_LIMIT
        ),
        name="split_grads",
    )(lists, doc_lang, docs, queries, grad_out, keys, values, delta_rows)


def hand_over_kernel(*refs):
    count = (len(refs) - 2) // 3
    in_sem, out_sem = refs[-2:]
    moves = []
    for k in range(count):
        src, dst, held = refs[k], refs[count + k], refs[2 * count + k]
        part = src.shape[0] // CHUNKS
        for c in range(CHUNKS):
            rows = pl.ds(c * part, part)
            moves.append(
                (
                    pltpu.make_async_copy(src.at[rows, :], held.at[rows, :], in_sem.at[k, c]),
                    pltpu.make_async_copy(held.at[rows, :], dst.at[rows, :], out_sem.at[k, c]),
                )
            )
    for fetch, _ in moves:
        fetch.start()
    for fetch, store in moves:
        fetch.wait()
        store.start()
    for _, store in moves:
        store.wait()


def handed_over(arrays):
    anywhere = pl.BlockSpec(memory_space=pl.ANY)
    count = len(arrays)
    return pl.pallas_call(
        hand_over_kernel,
        out_shape=tuple(jax.ShapeDtypeStruct(x.shape, x.dtype) for x in arrays),
        in_specs=[anywhere] * count,
        out_specs=(anywhere,) * count,
        scratch_shapes=[pltpu.VMEM(x.shape, x.dtype) for x in arrays]
        + [pltpu.SemaphoreType.DMA((count, CHUNKS)), pltpu.SemaphoreType.DMA((count, CHUNKS))],
        name="hand_over",
    )(*arrays)


def shards(queries, keys, values, grad_out, row_delta, doc_ids, doc_lang, tile_list):
    tok_count, full_width = queries.shape
    heads_all = full_width // DH
    groups_all = keys.shape[1] // DH
    repeat_count = heads_all // groups_all
    n_uly = lax.axis_size("uly")
    n_blk = lax.axis_size("blk")
    heads_here = heads_all // n_uly
    width = heads_here * DH
    copies = repeat_count // heads_here
    lists = tile_list.transpose(0, 2, 1)
    docs = doc_ids.reshape(-1, BLOCK)
    delta_rows = row_delta.T.reshape(n_uly, heads_here, tok_count)
    if n_uly == SPLIT and groups_all == SPLIT and repeat_count == HALF and tok_count == BLOCK:
        return handed_over(
            split_grads(lists, doc_lang, docs, queries, grad_out, keys, values, delta_rows, n_blk)
        )
    anywhere = pl.BlockSpec(memory_space=pl.ANY)
    in_vmem = pl.BlockSpec(memory_space=pltpu.VMEM)
    kv_spec = in_vmem if copies > 1 else anywhere
    bf16, f32 = jnp.bfloat16, jnp.float32
    pair = (2, BLOCK, DH)
    dma = pltpu.SemaphoreType.DMA
    outs = pl.pallas_call(
        functools.partial(
            fused_kernel,
            n_blk,
            n_uly,
            tile_list.shape[2],
            heads_here,
            repeat_count,
        ),
        out_shape=(
            jax.ShapeDtypeStruct(queries.shape, bf16),
            jax.ShapeDtypeStruct(keys.shape, bf16),
            jax.ShapeDtypeStruct(values.shape, bf16),
        ),
        in_specs=[anywhere] * 8,
        out_specs=(anywhere, kv_spec, kv_spec),
        scratch_shapes=[
            pltpu.VMEM((n_uly, BLOCK, width), bf16),
            pltpu.VMEM((n_uly, BLOCK, width), bf16),
            pltpu.VMEM((n_uly, heads_here, BLOCK), f32),
            pltpu.VMEM((2 * n_uly,) + pair, bf16),
            pltpu.SMEM(lists.shape, jnp.int32),
            pltpu.SMEM(doc_lang.shape, jnp.int32),
            pltpu.VMEM((2 * n_uly, BLOCK), jnp.int32),
            pltpu.VMEM((2 * n_uly, BLOCK, BLOCK), jnp.int32),
            pltpu.VMEM((2 * n_uly,) + pair, f32),
            pltpu.VMEM((n_uly, BLOCK, width), bf16),
            pltpu.VMEM((n_uly,) + pair, bf16),
            pltpu.VMEM((n_uly,) + pair, bf16),
            pltpu.VMEM((n_uly,) + pair, bf16),
            pltpu.VMEM((2, n_uly if copies > 1 else 1, BLOCK, DH), bf16),
            dma((5, n_uly)),
            dma((5, n_uly)),
            dma((5,)),
            dma((n_uly,)),
            dma((n_uly,)),
            dma((n_uly,)),
            dma((n_uly,)),
            dma((3, n_uly)),
            dma((3, n_uly)),
            dma((3,)),
            dma((4,)),
        ],
        compiler_params=pltpu.CompilerParams(
            collective_id=0, has_side_effects=True, vmem_limit_bytes=VMEM_LIMIT
        ),
        name="attention_grads",
    )(lists, doc_lang, docs, queries, grad_out, keys, values, delta_rows)
    return handed_over(outs)


def solution(mesh):
    placed = (
        P(("blk", "uly"), None),
        P(("blk", "uly"), None),
        P(("blk", "uly"), None),
        P(("blk", "uly"), None),
        P(("blk", "uly"), None),
        P(),
        P(),
        P(),
    )
    return jax.shard_map(
        shards,
        mesh=mesh,
        in_specs=placed,
        out_specs=(P(("blk", "uly"), None), P(("blk", "uly"), None), P(("blk", "uly"), None)),
        check_vma=False,
    )
```

```python
import functools

import jax
import jax.numpy as jnp
from jax import lax
from jax.experimental import pallas as pl
from jax.experimental.pallas import tpu as pltpu
from jax.sharding import PartitionSpec as P

DH = 128
BLOCK = 128
LANGS = 4
MASKED = -1e30
MESH = pl.DeviceIdType.MESH
LOOK = 7
CHUNKS = 4
SPLIT = 8
HALF = 4
SLACK = 2
LOG2_E = 1.4426950408889634
VMEM_LIMIT = 56 * 1024 * 1024


def greet(b, u, n_blk, n_uly):
    barrier = pltpu.get_barrier_semaphore()
    for p in range(1, n_uly):
        pl.semaphore_signal(
            barrier, inc=1, device_id=(b, lax.rem(u + p, n_uly)), device_id_type=MESH
        )

    @pl.when(b > 0)
    def _():
        pl.semaphore_signal(barrier, inc=1, device_id=(b - 1, u), device_id_type=MESH)

    @pl.when(b < n_blk - 1)
    def _():
        pl.semaphore_signal(barrier, inc=1, device_id=(b + 1, u), device_id_type=MESH)

    ends = jnp.where(b > 0, 1, 0) + jnp.where(b < n_blk - 1, 1, 0)
    pl.semaphore_wait(barrier, n_uly - 1 + ends)


def aligned(start, size):
    return pl.ds(pl.multiple_of(start, size), size)


def partner(u, s, n):
    found, bit = 0, 1
    while bit < n:
        found = found + bit * lax.rem(lax.div(u, bit) + lax.div(s, bit), 2)
        bit *= 2
    return found


def fused_kernel(
    n_blk,
    n_uly,
    list_count,
    heads_here,
    repeat_count,
    list_hbm,
    lang_hbm,
    docs_hbm,
    q_ref,
    do_ref,
    k_ref,
    v_ref,
    dl_ref,
    dq_ref,
    dk_ref,
    dv_ref,
    q_all,
    do_all,
    dl_all,
    window,
    list_ref,
    lang_ref,
    code_ref,
    key_codes,
    acc,
    dq_all,
    back,
    returned,
    total,
    landing,
    in_send,
    in_recv,
    local_sem,
    z_send,
    z_recv,
    back_send,
    back_recv,
    out_send,
    out_recv,
    out_local,
    table_sem,
):
    b, u = lax.axis_index("blk"), lax.axis_index("uly")
    tiles_here = n_uly
    width = heads_here * DH
    copies = repeat_count // heads_here
    direct = copies == 1
    f32 = jnp.float32
    my_cols = aligned(u * width, width)
    my_group = aligned(u * DH, DH)
    peer_of = functools.partial(partner, u, n=n_uly)

    def pieces(peer):
        group = lax.div(peer * heads_here, repeat_count)
        kv_cols = aligned(group * DH, DH)
        q_cols = aligned(peer * width, width)
        return (
            (k_ref.at[:, kv_cols], window.at[tiles_here + u, 0]),
            (v_ref.at[:, kv_cols], window.at[tiles_here + u, 1]),
            (dl_ref.at[peer], dl_all.at[u]),
            (q_ref.at[:, q_cols], q_all.at[u]),
            (do_ref.at[:, q_cols], do_all.at[u]),
        )

    def out_pieces(peer):
        if direct:
            ends = (dk_ref.at[:, my_group], dv_ref.at[:, my_group])
        else:
            ends = (landing.at[0, u], landing.at[1, u])
        return (
            (total.at[peer, 0], ends[0]),
            (total.at[peer, 1], ends[1]),
            (dq_all.at[peer], dq_ref.at[:, my_cols]),
        )

    def remote(parts, kind, s, send, recv):
        peer = peer_of(s)
        src, dst = parts(peer)[kind]
        return pltpu.make_async_remote_copy(
            src_ref=src,
            dst_ref=dst,
            send_sem=send.at[kind, s],
            recv_sem=recv.at[kind, s],
            device_id=(b, peer),
            device_id_type=MESH,
        )

    def inward(kind, s):
        return remote(pieces, kind, s, in_send, in_recv)

    def outward(kind, s):
        return remote(out_pieces, kind, s, out_send, out_recv)

    def local(kind):
        src, dst = pieces(u)[kind]
        return pltpu.make_async_copy(src, dst, local_sem.at[kind])

    def out_own(kind):
        src, dst = out_pieces(u)[kind]
        return pltpu.make_async_copy(src, dst, out_local.at[kind])

    def forward(a):
        return pltpu.make_async_remote_copy(
            src_ref=window.at[tiles_here + a],
            dst_ref=window.at[a],
            send_sem=z_send.at[a],
            recv_sem=z_recv.at[a],
            device_id=(lax.rem(b + 1, n_blk), u),
            device_id_type=MESH,
        )

    def backward(a):
        return pltpu.make_async_remote_copy(
            src_ref=back.at[a],
            dst_ref=returned.at[a],
            send_sem=back_send.at[a],
            recv_sem=back_recv.at[a],
            device_id=(lax.rem(b + n_blk - 1, n_blk), u),
            device_id_type=MESH,
        )

    def each(first, last, body):
        lax.fori_loop(first, last, lambda s, _: (body(s), 0)[1], 0)

    has_next = b < n_blk - 1
    has_prev = b > 0

    tables = (
        pltpu.make_async_copy(list_hbm, list_ref, table_sem.at[0]),
        pltpu.make_async_copy(lang_hbm, lang_ref, table_sem.at[1]),
        pltpu.make_async_copy(
            docs_hbm.at[aligned(jnp.maximum(b - 1, 0) * tiles_here, tiles_here), :],
            code_ref.at[pl.ds(0, tiles_here), :],
            table_sem.at[2],
        ),
        pltpu.make_async_copy(
            docs_hbm.at[aligned(b * tiles_here, tiles_here), :],
            code_ref.at[pl.ds(tiles_here, tiles_here), :],
            table_sem.at[3],
        ),
    )
    for kind in range(5):
        local(kind).start()
    for table in tables:
        table.start()
    greet(b, u, n_blk, n_uly)

    def send_keys(s):
        inward(0, s).start()
        inward(1, s).start()

    def send_rows(s):
        inward(2, s).start()
        inward(3, s).start()
        inward(4, s).start()

    each(1, n_uly, send_keys)
    each(1, min(LOOK, n_uly - 1) + 1, send_rows)
    local(0).wait()
    local(1).wait()

    @pl.when(has_next)
    def _():
        forward(u).start()

    for table in tables:
        table.wait()
    docs = code_ref[...]

    def look_up(d, lang):
        return lang + jnp.where(docs == d, lang_ref[d], 0)

    lang = lax.fori_loop(0, lang_ref.shape[0], look_up, jnp.zeros_like(docs))
    code_ref[...] = docs * LANGS + lang

    def prepare(t):
        key_codes[t] = jnp.broadcast_to(code_ref[pl.ds(t, 1), :], (BLOCK, BLOCK)).T
        acc[t] = jnp.zeros(acc.shape[1:], f32)

    each(0, 2 * tiles_here, prepare)

    @pl.when(b == 0)
    def _():
        window[0:tiles_here] = jnp.zeros((tiles_here,) + window.shape[1:], window.dtype)

    def pass_on(s):
        inward(0, s).wait_recv()
        inward(1, s).wait_recv()

        @pl.when(has_next)
        def _():
            forward(peer_of(s)).start()

    each(1, n_uly, pass_on)

    @pl.when(has_prev)
    def _():
        each(0, tiles_here, lambda a: forward(a).wait_recv())

    local(2).wait()
    local(3).wait()
    local(4).wait()

    scaling = float(DH) ** (-0.5)
    across = (((1,), (1,)), ((), ()))
    gap = lax.broadcasted_iota(jnp.int32, (BLOCK, BLOCK), 0) - lax.broadcasted_iota(
        jnp.int32, (BLOCK, BLOCK), 1
    )
    group_here = lax.div(u * heads_here, repeat_count)

    def tile_work(a):
        tile = b * tiles_here + a
        listed = [list_ref[group_here, l, tile] for l in range(list_count)]
        cands = [tile - 1, tile] + listed
        own_slot = tiles_here + a
        window_first = (b - 1) * tiles_here
        query_code = code_ref[pl.ds(own_slot, 1), :]
        query_lang = query_code & (LANGS - 1)
        slots = []
        biases = []
        for c, cand in enumerate(cands):
            usable = cand >= 0
            for other in cands[: c if c >= 2 else 0]:
                usable = usable & (cand != other)
            marked = cand == listed[0]
            for other in listed[1:]:
                marked = marked | (cand == other)
            if c < 2:
                slot = own_slot - 1 + c
            else:
                slot = jnp.clip(cand - window_first, 0, 2 * tiles_here - 1)
            limit = jnp.where(usable, (tile - cand) * BLOCK, -2 * BLOCK)
            seen_lang = jnp.where(marked, query_lang, -1)
            key_code = key_codes[slot]
            allowed = (gap <= limit) & (
                (key_code == query_code) | ((key_code & (LANGS - 1)) == seen_lang)
            )
            slots.append(slot)
            biases.append(jnp.where(allowed, 0.0, MASKED))

        def stacked(rows):
            return jnp.concatenate([rows[:, h * DH : (h + 1) * DH] for h in range(heads_here)], 0)

        bias = jnp.concatenate(biases, axis=0)
        bias = jnp.concatenate([bias] * heads_here, axis=1)
        key_part = jnp.concatenate([window[s, 0] for s in slots], axis=0)
        value_part = jnp.concatenate([window[s, 1] for s in slots], axis=0)
        query_part = stacked(q_all[a])
        dout_part = stacked(do_all[a])
        delta_tile = dl_all[a]
        delta = jnp.concatenate([delta_tile[h : h + 1, :] for h in range(heads_here)], axis=1)
        scores = lax.dot_general(key_part, query_part, across, preferred_element_type=f32)
        scores = scores * scaling + bias
        top = jnp.max(scores, axis=0, keepdims=True)
        raised = jnp.exp(scores - top)
        weights = raised * (1.0 / jnp.sum(raised, axis=0, keepdims=True))
        grad_weights = lax.dot_general(value_part, dout_part, across, preferred_element_type=f32)
        grad_scores = (weights * (grad_weights - delta)).astype(jnp.bfloat16)
        grad_query = scaling * lax.dot_general(
            grad_scores, key_part, (((0,), (0,)), ((), ())), preferred_element_type=f32
        )
        for h in range(heads_here):
            dq_all[a, :, h * DH : (h + 1) * DH] = grad_query[h * BLOCK : (h + 1) * BLOCK].astype(
                dq_all.dtype
            )
        grad_key = scaling * jnp.dot(grad_scores, query_part, preferred_element_type=f32)
        grad_value = jnp.dot(weights.astype(jnp.bfloat16), dout_part, preferred_element_type=f32)
        parts = (grad_key, grad_value)
        for c in range(2):
            for k in range(2):
                acc[slots[c], k] += parts[k][c * BLOCK : (c + 1) * BLOCK]

        def spread(t):
            for k in range(2):
                more = acc[t, k]
                for c in range(2, 2 + list_count):
                    piece = parts[k][c * BLOCK : (c + 1) * BLOCK]
                    more = more + jnp.where(slots[c] == t, piece, 0.0)
                acc[t, k] = more

        each(0, 2 * tiles_here, spread)

    tile_work(u)
    out_own(2).start()

    def step(s):
        @pl.when(s + LOOK < n_uly)
        def _():
            send_rows(s + LOOK)

        inward(2, s).wait_recv()
        inward(3, s).wait_recv()
        inward(4, s).wait_recv()
        tile_work(peer_of(s))
        outward(2, s).start()

    each(1, n_uly, step)

    @pl.when(has_prev)
    def _():
        def give_back(s):
            a = peer_of(s)
            back[a] = acc[a].astype(back.dtype)
            backward(a).start()

        each(0, n_uly, give_back)

    def settle(s):
        a = peer_of(s)

        @pl.when(has_next)
        def _():
            backward(a).wait_recv()
            total[a] = (acc[tiles_here + a] + returned[a].astype(f32)).astype(total.dtype)

        @pl.when(b == n_blk - 1)
        def _():
            total[a] = acc[tiles_here + a].astype(total.dtype)

    settle(0)
    out_own(0).start()
    out_own(1).start()

    def settle_and_send(s):
        settle(s)
        outward(0, s).start()
        outward(1, s).start()

    each(1, n_uly, settle_and_send)

    for kind in range(3):
        out_own(kind).wait()

    def finish(s):
        for kind in range(3):
            outward(kind, s).wait_recv()
        for kind in range(5):
            inward(kind, s).wait_send()
        for kind in range(3):
            outward(kind, s).wait_send()

    each(1, n_uly, finish)

    @pl.when(has_next)
    def _():
        each(0, n_uly, lambda a: forward(a).wait_send())

    @pl.when(has_prev)
    def _():
        each(0, n_uly, lambda a: backward(a).wait_send())

    if not direct:
        for kind, out in ((0, dk_ref), (1, dv_ref)):
            for g in range(n_uly // copies):
                summed = landing[kind, g * copies].astype(f32)
                for r in range(1, copies):
                    summed = summed + landing[kind, g * copies + r].astype(f32)
                out[:, g * DH : (g + 1) * DH] = summed.astype(out.dtype)


def split_kernel(
    n_blk,
    list_count,
    list_hbm,
    lang_hbm,
    docs_hbm,
    q_ref,
    do_ref,
    k_ref,
    v_ref,
    dl_ref,
    dq_ref,
    dk_ref,
    dv_ref,
    q_all,
    do_all,
    dl_all,
    window_row,
    window_column,
    list_ref,
    lang_ref,
    order_ref,
    same_ref,
    place_ref,
    code_ref,
    key_codes,
    acc,
    entries,
    sums,
    dq_all,
    back,
    returned,
    across_out,
    across_in,
    total,
    in_send,
    in_recv,
    local_sem,
    far_send,
    far_recv,
    relay_send,
    relay_recv,
    z_send,
    z_recv,
    back_send,
    back_recv,
    across_send,
    across_recv,
    out_send,
    out_recv,
    out_local,
    table_sem,
    gate,
):
    b, u = lax.axis_index("blk"), lax.axis_index("uly")
    y, x, c = lax.div(u, 4), lax.rem(lax.div(u, 2), 2), lax.rem(u, 2)
    tiles_here = SPLIT
    width = HALF * DH
    f32 = jnp.float32
    windows = (window_row, window_column)
    has_next = b < n_blk - 1
    has_prev = b > 0

    def job_of(f, near):
        return lax.rem(f + c + near, 2)

    def member(j, s, far):
        along, near = lax.div(s, 2), lax.rem(s, 2)
        row = lax.rem(y + along * j + far * (1 - j), 2)
        column = lax.rem(x + along * (1 - j) + far * j, 2)
        return 4 * row + 2 * column + lax.rem(c + near, 2)

    def peer_of(f, s):
        return member(job_of(f, 0), s, 0)

    def far_of(f, s):
        return member(job_of(f, 0), s, 1)

    def position(j, s):
        return HALF * j + 2 * lax.rem(x * (1 - j) + y * j + lax.div(s, 2), 2) + lax.rem(c + lax.rem(s, 2), 2)

    def group_of(f):
        return position(job_of(f, 0), 0)

    def target_of(f, s):
        return member(job_of(f, lax.rem(s, 2)), s, 0)

    def pieces(f, s):
        group = position(job_of(f, lax.rem(s, 2)), s)
        kv_cols = aligned(group * DH, DH)
        q_cols = aligned(group * width, width)
        return (
            (k_ref.at[:, kv_cols], windows[f].at[tiles_here + u, 0]),
            (v_ref.at[:, kv_cols], windows[f].at[tiles_here + u, 1]),
            (dl_ref.at[group], dl_all.at[f, s]),
            (q_ref.at[:, q_cols], q_all.at[f, s]),
            (do_ref.at[:, q_cols], do_all.at[f, s]),
        )

    def out_pieces(f, s):
        group = group_of(f)
        kv_cols = aligned(group * DH, DH)
        return (
            (total.at[f, s, 0], dk_ref.at[:, kv_cols]),
            (total.at[f, s, 1], dv_ref.at[:, kv_cols]),
            (dq_all.at[f, s], dq_ref.at[:, aligned(group * width, width)]),
        )

    def remote(src, dst, send, recv, device):
        return pltpu.make_async_remote_copy(
            src_ref=src, dst_ref=dst, send_sem=send, recv_sem=recv, device_id=device, device_id_type=MESH
        )

    def inward(j, kind, s):
        src, dst = pieces(j, s)[kind]
        return remote(src, dst, in_send.at[j, kind, s], in_recv.at[j, kind, s], (b, target_of(j, s)))

    def direct(kind, s):
        src, dst = pieces(0, s)[kind]
        return remote(
            src, dst, far_send.at[kind, s], far_recv.at[kind, s], (b, member(job_of(0, lax.rem(s, 2)), s, 1))
        )

    def outward(j, kind, s):
        src, dst = out_pieces(j, s)[kind]
        return remote(src, dst, out_send.at[j, kind, s], out_recv.at[j, kind, s], (b, peer_of(j, s)))

    def local(j, kind):
        src, dst = pieces(j, 0)[kind]
        return pltpu.make_async_copy(src, dst, local_sem.at[j, kind])

    def out_own(j, kind):
        src, dst = out_pieces(j, 0)[kind]
        return pltpu.make_async_copy(src, dst, out_local.at[j, kind])

    def relay(s):
        held = windows[1].at[tiles_here + peer_of(1, s)]
        return remote(held, held, relay_send.at[s], relay_recv.at[s], (b, far_of(1, 0)))

    def forward(j, a):
        return remote(
            windows[j].at[tiles_here + a],
            windows[j].at[a],
            z_send.at[j, a],
            z_recv.at[j, a],
            (lax.rem(b + 1, n_blk), u),
        )

    def backward(j, a):
        return remote(
            back.at[j, a],
            returned.at[j, a],
            back_send.at[j, a],
            back_recv.at[j, a],
            (lax.rem(b + n_blk - 1, n_blk), u),
        )

    def over(j, s):
        return remote(
            across_out.at[j, s],
            across_in.at[j, s],
            across_send.at[j, s],
            across_recv.at[j, s],
            (b, far_of(j, 0)),
        )

    def each(first, last, body):
        lax.fori_loop(first, last, lambda s, _: (body(s), 0)[1], 0)

    def last_first(body):
        each(0, HALF, lambda n: body(HALF - 1 - n))

    def send_on(j, a):
        @pl.when(has_next)
        def _():
            forward(j, a).start()

    tables = (
        pltpu.make_async_copy(list_hbm, list_ref, table_sem.at[0]),
        pltpu.make_async_copy(lang_hbm, lang_ref, table_sem.at[1]),
        pltpu.make_async_copy(
            docs_hbm.at[aligned(jnp.maximum(b - 1, 0) * tiles_here, tiles_here), :],
            code_ref.at[pl.ds(0, tiles_here), :],
            table_sem.at[2],
        ),
        pltpu.make_async_copy(
            docs_hbm.at[aligned(b * tiles_here, tiles_here), :],
            code_ref.at[pl.ds(tiles_here, tiles_here), :],
            table_sem.at[3],
        ),
    )
    for j in range(2):
        for kind in range(5):
            local(j, kind).start()
    for table in tables:
        table.start()

    barrier = pltpu.get_barrier_semaphore()
    friends = [member(0, s, far) for far in range(2) for s in range(HALF) if s + far > 0]
    for friend in friends:
        pl.semaphore_signal(barrier, inc=1, device_id=(b, friend), device_id_type=MESH)

    @pl.when(has_prev)
    def _():
        pl.semaphore_signal(barrier, inc=1, device_id=(b - 1, u), device_id_type=MESH)

    @pl.when(has_next)
    def _():
        pl.semaphore_signal(barrier, inc=1, device_id=(b + 1, u), device_id_type=MESH)

    ends = jnp.where(has_prev, 1, 0) + jnp.where(has_next, 1, 0)
    pl.semaphore_wait(barrier, len(friends) + ends)

    def start_keys(j):
        def body(s):
            inward(j, 0, s).start()
            inward(j, 1, s).start()

        each(1, HALF, body)

    def start_rows(j):
        def body(s):
            for kind in (2, 3, 4):
                inward(j, kind, s).start()

        each(1, HALF, body)

    def keys_here(j, s):
        inward(j, 0, s).wait_recv()
        inward(j, 1, s).wait_recv()

    def drained(j):
        @pl.when(has_next)
        def _():
            each(0, HALF, lambda s: forward(j, peer_of(j, s)).wait_send())
            each(0, HALF - SLACK, lambda s: forward(j, far_of(j, s)).wait_send())

    def let_go(n):
        pl.semaphore_signal(gate.at[n], inc=1, device_id=(b, member(0, 1, 0)), device_id_type=MESH)

    def start_far(s):
        direct(0, s).start()
        direct(1, s).start()

    def pass_near(s):
        keys_here(0, s)

        @pl.when(c == 0)
        def _():
            send_on(0, peer_of(0, s))

    def pass_far(s):
        direct(0, s).wait_recv()
        direct(1, s).wait_recv()

        @pl.when(c == 0)
        def _():
            send_on(0, far_of(0, s))

    start_keys(0)
    each(0, HALF, start_far)
    start_keys(1)
    start_rows(0)
    local(0, 0).wait()
    local(0, 1).wait()

    send_on(0, u)
    keys_here(0, 1)
    send_on(0, peer_of(0, 1))

    for table in tables:
        table.wait()
    docs = code_ref[...]

    def look_up(d, lang):
        return lang + jnp.where(docs == d, lang_ref[d], 0)

    lang = lax.fori_loop(0, lang_ref.shape[0], look_up, jnp.zeros_like(docs))
    code_ref[...] = docs * LANGS + lang

    window_first = (b - 1) * tiles_here

    def slot_of(cand):
        return jnp.clip(cand - window_first, 0, 2 * tiles_here - 1)

    def plan(j):
        group = group_of(j)
        count = HALF * list_count
        slots = [
            slot_of(list_ref[group, l, b * tiles_here + peer_of(j, s)]) for s in range(HALF) for l in range(list_count)
        ]
        ranks = []
        for e in range(count):
            rank = 0
            for other in range(count):
                if other < e:
                    rank = rank + jnp.where(slots[other] <= slots[e], 1, 0)
                elif other > e:
                    rank = rank + jnp.where(slots[other] < slots[e], 1, 0)
            ranks.append(rank)
        before = -1
        for i in range(count):
            entry, slot = 0, 0
            for e in range(count):
                entry = entry + jnp.where(ranks[e] == i, e, 0)
                slot = slot + jnp.where(ranks[e] == i, slots[e], 0)
            order_ref[j, i] = entry
            same_ref[j, i] = jnp.where(slot == before, 1, 0)
            before = slot
        for t in range(2 * tiles_here):
            upto, here = 0, 0
            for slot in slots:
                upto = upto + jnp.where(slot <= t, 1, 0)
                here = here + jnp.where(slot == t, 1, 0)
            place_ref[j, t] = jnp.where(here > 0, upto - 1, count)

    def prepare(t):
        key_codes[t] = jnp.broadcast_to(code_ref[pl.ds(t, 1), :], (BLOCK, BLOCK)).T
        acc[0, t] = jnp.zeros(acc.shape[2:], f32)
        acc[1, t] = jnp.zeros(acc.shape[2:], f32)

    each(0, 2 * tiles_here, prepare)
    for j in range(2):
        plan(j)
        sums[j, HALF * list_count] = jnp.zeros(sums.shape[2:], f32)

    @pl.when(b == 0)
    def _():
        for window in windows:
            window[0:tiles_here] = jnp.zeros((tiles_here,) + window.shape[1:], window.dtype)

    scaling = float(DH) ** (-0.5)
    across = (((1,), (1,)), ((), ()))
    gap = lax.broadcasted_iota(jnp.int32, (BLOCK, BLOCK), 0) - lax.broadcasted_iota(
        jnp.int32, (BLOCK, BLOCK), 1
    )

    def tile_work(j, s):
        group = group_of(j)
        place = peer_of(j, s)
        tile = b * tiles_here + place
        listed = [list_ref[group, l, tile] for l in range(list_count)]
        cands = [tile - 1, tile] + listed
        own_slot = tiles_here + place
        query_code = code_ref[pl.ds(own_slot, 1), :]
        query_lang = query_code & (LANGS - 1)
        slots = []
        biases = []
        for n, cand in enumerate(cands):
            usable = cand >= 0
            for other in cands[: n if n >= 2 else 0]:
                usable = usable & (cand != other)
            marked = cand == listed[0]
            for other in listed[1:]:
                marked = marked | (cand == other)
            slot = own_slot - 1 + n if n < 2 else slot_of(cand)
            limit = jnp.where(usable, (tile - cand) * BLOCK, -2 * BLOCK)
            seen_lang = jnp.where(marked, query_lang, -1)
            key_code = key_codes[slot]
            allowed = (gap <= limit) & (
                (key_code == query_code) | ((key_code & (LANGS - 1)) == seen_lang)
            )
            slots.append(slot)
            biases.append(jnp.where(allowed, 0.0, MASKED))

        def stacked(rows):
            return jnp.concatenate([rows[:, h * DH : (h + 1) * DH] for h in range(HALF)], 0)

        bias = jnp.concatenate(biases, axis=0)
        bias = jnp.concatenate([bias] * HALF, axis=1)
        key_part = jnp.concatenate([windows[j][t, 0] for t in slots], axis=0)
        value_part = jnp.concatenate([windows[j][t, 1] for t in slots], axis=0)
        query_part = stacked(q_all[j, s])
        dout_part = stacked(do_all[j, s])
        delta_tile = dl_all[j, s]
        delta = jnp.concatenate([delta_tile[h : h + 1, :] for h in range(HALF)], axis=1)
        scores = lax.dot_general(key_part, query_part, across, preferred_element_type=f32)
        scores = scores * (scaling * LOG2_E) + bias
        top = jnp.max(scores, axis=0, keepdims=True)
        raised = jnp.exp2(scores - top)
        weights = raised * (1.0 / jnp.sum(raised, axis=0, keepdims=True))
        grad_weights = lax.dot_general(value_part, dout_part, across, preferred_element_type=f32)
        grad_scores = (weights * (grad_weights - delta)).astype(jnp.bfloat16)
        grad_query = scaling * lax.dot_general(
            key_part, grad_scores, (((0,), (0,)), ((), ())), preferred_element_type=f32
        )
        for h in range(HALF):
            turned = grad_query[:, h * BLOCK : (h + 1) * BLOCK].T
            dq_all[j, s, :, h * DH : (h + 1) * DH] = turned.astype(dq_all.dtype)
        grad_key = scaling * jnp.dot(grad_scores, query_part, preferred_element_type=f32)
        grad_value = jnp.dot(weights.astype(jnp.bfloat16), dout_part, preferred_element_type=f32)
        for k, part in ((0, grad_key), (1, grad_value)):
            for n in range(2):
                acc[j, slots[n], k] += part[n * BLOCK : (n + 1) * BLOCK]
            for l in range(list_count):
                first = (2 + l) * BLOCK
                entries[s * list_count + l, k] = part[first : first + BLOCK]

    def add_listed(j):
        sums[j, 0] = entries[order_ref[j, 0]]

        def body(i):
            earlier = jnp.where(same_ref[j, i] == 1, sums[j, i - 1], 0.0)
            sums[j, i] = entries[order_ref[j, i]] + earlier

        each(1, HALF * list_count, body)

    def slot_sum(j, t):
        return acc[j, t] + sums[j, place_ref[j, t]]

    def arrived(j):
        @pl.when(has_prev)
        def _():
            each(0, tiles_here, lambda a: forward(j, a).wait_recv())

    def give_back(j):
        add_listed(j)

        @pl.when(has_prev)
        def _():
            def body(a):
                back[j, a] = slot_sum(j, a).astype(back.dtype)
                backward(j, a).start()

            last_first(lambda s: body(far_of(j, s)))
            last_first(lambda s: body(peer_of(j, s)))

    def work(j, s):
        @pl.when(s > 0)
        def _():
            for kind in (2, 3, 4):
                inward(j, kind, s).wait_recv()

        tile_work(j, s)

        @pl.when(s > 0)
        def _():
            outward(j, 2, s).start()

        @pl.when(s == 0)
        def _():
            out_own(j, 2).start()

    def with_returned(j, a, then):
        @pl.when(has_next)
        def _():
            backward(j, a).wait_recv()
            then(slot_sum(j, tiles_here + a) + returned[j, a].astype(f32))

        @pl.when(b == n_blk - 1)
        def _():
            then(slot_sum(j, tiles_here + a))

    def settle_far(j, s):
        def then(value):
            across_out[j, s] = value.astype(across_out.dtype)

        with_returned(j, far_of(j, s), then)
        over(j, s).start()

    def settle(j, s):
        over(j, s).wait_recv()

        def then(value):
            total[j, s] = (value + across_in[j, s].astype(f32)).astype(total.dtype)

        with_returned(j, peer_of(j, s), then)

        @pl.when(s > 0)
        def _():
            outward(j, 0, s).start()
            outward(j, 1, s).start()

        @pl.when(s == 0)
        def _():
            out_own(j, 0).start()
            out_own(j, 1).start()

    each(2, HALF, pass_near)
    each(0, HALF, pass_far)
    local(1, 0).wait()
    local(1, 1).wait()
    relay(0).start()

    def relay_keys(s):
        keys_here(1, s)
        relay(s).start()

    each(1, HALF, relay_keys)
    start_rows(1)

    @pl.when(c == 1)
    def _():
        pl.semaphore_wait(gate.at[0], 1)
        each(2, HALF, lambda s: send_on(0, peer_of(0, s)))
        each(0, HALF, lambda s: send_on(0, far_of(0, s)))
        drained(0)
        let_go(1)

    @pl.when(c == 0)
    def _():
        drained(0)
        let_go(0)

    arrived(0)
    for kind in (2, 3, 4):
        local(0, kind).wait()

    def first_step(s):
        work(0, s)

    each(0, HALF, first_step)
    give_back(0)

    @pl.when(c == 0)
    def _():
        pl.semaphore_wait(gate.at[1], 1)

    @pl.when(c == 1)
    def _():
        pl.semaphore_wait(gate.at[2], 1)

    each(0, HALF, lambda s: send_on(1, peer_of(1, s)))

    def pass_far_second(s):
        relay(s).wait_recv()
        send_on(1, far_of(1, s))

    each(0, HALF, pass_far_second)

    @pl.when(c == 0)
    def _():
        drained(1)
        let_go(2)

    last_first(lambda s: settle_far(0, s))
    arrived(1)
    for kind in (2, 3, 4):
        local(1, kind).wait()

    last_first(lambda s: work(1, s))
    give_back(1)
    last_first(lambda s: settle(0, s))
    last_first(lambda s: settle_far(1, s))
    last_first(lambda s: settle(1, s))

    for j in range(2):
        for kind in range(3):
            out_own(j, kind).wait()

        def finish(s):
            for kind in range(3):
                outward(j, kind, s).wait_recv()
            for kind in range(5):
                inward(j, kind, s).wait_send()
            for kind in range(3):
                outward(j, kind, s).wait_send()

        each(1, HALF, finish)

        def finish_far(s):
            over(j, s).wait_send()
            if j == 0:
                direct(0, s).wait_send()
                direct(1, s).wait_send()
            else:
                relay(s).wait_send()

        each(0, HALF, finish_far)

        @pl.when(has_next)
        def _():
            if j == 0:
                each(HALF - SLACK, HALF, lambda s: forward(j, far_of(j, s)).wait_send())
            else:

                @pl.when(c == 0)
                def _():
                    each(HALF - SLACK, HALF, lambda s: forward(j, far_of(j, s)).wait_send())

                @pl.when(c == 1)
                def _():
                    each(0, tiles_here, lambda a: forward(j, a).wait_send())

        @pl.when(has_prev)
        def _():
            each(0, tiles_here, lambda a: backward(j, a).wait_send())


def split_grads(lists, doc_lang, docs, queries, grad_out, keys, values, delta_rows, n_blk):
    list_count = lists.shape[1]
    width = HALF * DH
    anywhere = pl.BlockSpec(memory_space=pl.ANY)
    bf16, f32 = jnp.bfloat16, jnp.float32
    pair = (2, BLOCK, DH)
    dma = pltpu.SemaphoreType.DMA
    entry_count = HALF * list_count
    return pl.pallas_call(
        functools.partial(split_kernel, n_blk, list_count),
        out_shape=(
            jax.ShapeDtypeStruct(queries.shape, bf16),
            jax.ShapeDtypeStruct(keys.shape, bf16),
            jax.ShapeDtypeStruct(values.shape, bf16),
        ),
        in_specs=[anywhere] * 8,
        out_specs=(anywhere,) * 3,
        scratch_shapes=[
            pltpu.VMEM((2, HALF, BLOCK, width), bf16),
            pltpu.VMEM((2, HALF, BLOCK, width), bf16),
            pltpu.VMEM((2, HALF, HALF, BLOCK), f32),
            pltpu.VMEM((2 * SPLIT,) + pair, bf16),
            pltpu.VMEM((2 * SPLIT,) + pair, bf16),
            pltpu.SMEM(lists.shape, jnp.int32),
            pltpu.SMEM(doc_lang.shape, jnp.int32),
            pltpu.SMEM((2, entry_count), jnp.int32),
            pltpu.SMEM((2, entry_count), jnp.int32),
            pltpu.SMEM((2, 2 * SPLIT), jnp.int32),
            pltpu.VMEM((2 * SPLIT, BLOCK), jnp.int32),
            pltpu.VMEM((2 * SPLIT, BLOCK, BLOCK), jnp.int32),
            pltpu.VMEM((2, 2 * SPLIT) + pair, f32),
            pltpu.VMEM((entry_count,) + pair, f32),
            pltpu.VMEM((2, entry_count + 1) + pair, f32),
            pltpu.VMEM((2, HALF, BLOCK, width), bf16),
            pltpu.VMEM((2, SPLIT) + pair, bf16),
            pltpu.VMEM((2, SPLIT) + pair, bf16),
            pltpu.VMEM((2, HALF) + pair, bf16),
            pltpu.VMEM((2, HALF) + pair, bf16),
            pltpu.VMEM((2, HALF) + pair, bf16),
            dma((2, 5, HALF)),
            dma((2, 5, HALF)),
            dma((2, 5)),
            dma((2, HALF)),
            dma((2, HALF)),
            dma((HALF,)),
            dma((HALF,)),
            dma((2, SPLIT)),
            dma((2, SPLIT)),
            dma((2, SPLIT)),
            dma((2, SPLIT)),
            dma((2, HALF)),
            dma((2, HALF)),
            dma((2, 3, HALF)),
            dma((2, 3, HALF)),
            dma((2, 3)),
            dma((4,)),
            pltpu.SemaphoreType.REGULAR((3,)),
        ],
        compiler_params=pltpu.CompilerParams(
            collective_id=0, has_side_effects=True, vmem_limit_bytes=VMEM_LIMIT
        ),
        name="split_grads",
    )(lists, doc_lang, docs, queries, grad_out, keys, values, delta_rows)


def hand_over_kernel(*refs):
    count = (len(refs) - 2) // 3
    in_sem, out_sem = refs[-2:]
    moves = []
    for k in range(count):
        src, dst, held = refs[k], refs[count + k], refs[2 * count + k]
        part = src.shape[0] // CHUNKS
        for c in range(CHUNKS):
            rows = pl.ds(c * part, part)
            moves.append(
                (
                    pltpu.make_async_copy(src.at[rows, :], held.at[rows, :], in_sem.at[k, c]),
                    pltpu.make_async_copy(held.at[rows, :], dst.at[rows, :], out_sem.at[k, c]),
                )
            )
    for fetch, _ in moves:
        fetch.start()
    for fetch, store in moves:
        fetch.wait()
        store.start()
    for _, store in moves:
        store.wait()


def handed_over(arrays):
    anywhere = pl.BlockSpec(memory_space=pl.ANY)
    count = len(arrays)
    return pl.pallas_call(
        hand_over_kernel,
        out_shape=tuple(jax.ShapeDtypeStruct(x.shape, x.dtype) for x in arrays),
        in_specs=[anywhere] * count,
        out_specs=(anywhere,) * count,
        scratch_shapes=[pltpu.VMEM(x.shape, x.dtype) for x in arrays]
        + [pltpu.SemaphoreType.DMA((count, CHUNKS)), pltpu.SemaphoreType.DMA((count, CHUNKS))],
        name="hand_over",
    )(*arrays)


def shards(queries, keys, values, grad_out, row_delta, doc_ids, doc_lang, tile_list):
    tok_count, full_width = queries.shape
    heads_all = full_width // DH
    groups_all = keys.shape[1] // DH
    repeat_count = heads_all // groups_all
    n_uly = lax.axis_size("uly")
    n_blk = lax.axis_size("blk")
    heads_here = heads_all // n_uly
    width = heads_here * DH
    copies = repeat_count // heads_here
    lists = tile_list.transpose(0, 2, 1)
    docs = doc_ids.reshape(-1, BLOCK)
    delta_rows = row_delta.T.reshape(n_uly, heads_here, tok_count)
    if n_uly == SPLIT and groups_all == SPLIT and repeat_count == HALF and tok_count == BLOCK:
        return handed_over(
            split_grads(lists, doc_lang, docs, queries, grad_out, keys, values, delta_rows, n_blk)
        )
    anywhere = pl.BlockSpec(memory_space=pl.ANY)
    in_vmem = pl.BlockSpec(memory_space=pltpu.VMEM)
    kv_spec = in_vmem if copies > 1 else anywhere
    bf16, f32 = jnp.bfloat16, jnp.float32
    pair = (2, BLOCK, DH)
    dma = pltpu.SemaphoreType.DMA
    outs = pl.pallas_call(
        functools.partial(
            fused_kernel,
            n_blk,
            n_uly,
            tile_list.shape[2],
            heads_here,
            repeat_count,
        ),
        out_shape=(
            jax.ShapeDtypeStruct(queries.shape, bf16),
            jax.ShapeDtypeStruct(keys.shape, bf16),
            jax.ShapeDtypeStruct(values.shape, bf16),
        ),
        in_specs=[anywhere] * 8,
        out_specs=(anywhere, kv_spec, kv_spec),
        scratch_shapes=[
            pltpu.VMEM((n_uly, BLOCK, width), bf16),
            pltpu.VMEM((n_uly, BLOCK, width), bf16),
            pltpu.VMEM((n_uly, heads_here, BLOCK), f32),
            pltpu.VMEM((2 * n_uly,) + pair, bf16),
            pltpu.SMEM(lists.shape, jnp.int32),
            pltpu.SMEM(doc_lang.shape, jnp.int32),
            pltpu.VMEM((2 * n_uly, BLOCK), jnp.int32),
            pltpu.VMEM((2 * n_uly, BLOCK, BLOCK), jnp.int32),
            pltpu.VMEM((2 * n_uly,) + pair, f32),
            pltpu.VMEM((n_uly, BLOCK, width), bf16),
            pltpu.VMEM((n_uly,) + pair, bf16),
            pltpu.VMEM((n_uly,) + pair, bf16),
            pltpu.VMEM((n_uly,) + pair, bf16),
            pltpu.VMEM((2, n_uly if copies > 1 else 1, BLOCK, DH), bf16),
            dma((5, n_uly)),
            dma((5, n_uly)),
            dma((5,)),
            dma((n_uly,)),
            dma((n_uly,)),
            dma((n_uly,)),
            dma((n_uly,)),
            dma((3, n_uly)),
            dma((3, n_uly)),
            dma((3,)),
            dma((4,)),
        ],
        compiler_params=pltpu.CompilerParams(
            collective_id=0, has_side_effects=True, vmem_limit_bytes=VMEM_LIMIT
        ),
        name="attention_grads",
    )(lists, doc_lang, docs, queries, grad_out, keys, values, delta_rows)
    return handed_over(outs)


def solution(mesh):
    placed = (
        P(("blk", "uly"), None),
        P(("blk", "uly"), None),
        P(("blk", "uly"), None),
        P(("blk", "uly"), None),
        P(("blk", "uly"), None),
        P(),
        P(),
        P(),
    )
    return jax.shard_map(
        shards,
        mesh=mesh,
        in_specs=placed,
        out_specs=(P(("blk", "uly"), None), P(("blk", "uly"), None), P(("blk", "uly"), None)),
        check_vma=False,
    )
```

```python
import functools

import jax
import jax.numpy as jnp
from jax import lax
from jax.experimental import pallas as pl
from jax.experimental.pallas import tpu as pltpu
from jax.sharding import PartitionSpec as P

DH = 128
BLOCK = 128
LANGS = 4
MASKED = -1e30
MESH = pl.DeviceIdType.MESH
LOOK = 7
CHUNKS = 2
SPLIT = 8
HALF = 4
SLACK = 1
LOG2_E = 1.4426950408889634
VMEM_LIMIT = 56 * 1024 * 1024


def greet(b, u, n_blk, n_uly):
    barrier = pltpu.get_barrier_semaphore()
    for p in range(1, n_uly):
        pl.semaphore_signal(
            barrier, inc=1, device_id=(b, lax.rem(u + p, n_uly)), device_id_type=MESH
        )

    @pl.when(b > 0)
    def _():
        pl.semaphore_signal(barrier, inc=1, device_id=(b - 1, u), device_id_type=MESH)

    @pl.when(b < n_blk - 1)
    def _():
        pl.semaphore_signal(barrier, inc=1, device_id=(b + 1, u), device_id_type=MESH)

    ends = jnp.where(b > 0, 1, 0) + jnp.where(b < n_blk - 1, 1, 0)
    pl.semaphore_wait(barrier, n_uly - 1 + ends)


def aligned(start, size):
    return pl.ds(pl.multiple_of(start, size), size)


def partner(u, s, n):
    found, bit = 0, 1
    while bit < n:
        found = found + bit * lax.rem(lax.div(u, bit) + lax.div(s, bit), 2)
        bit *= 2
    return found


def fused_kernel(
    n_blk,
    n_uly,
    list_count,
    heads_here,
    repeat_count,
    list_hbm,
    lang_hbm,
    docs_hbm,
    q_ref,
    do_ref,
    k_ref,
    v_ref,
    dl_ref,
    dq_ref,
    dk_ref,
    dv_ref,
    q_all,
    do_all,
    dl_all,
    window,
    list_ref,
    lang_ref,
    code_ref,
    key_codes,
    acc,
    dq_all,
    back,
    returned,
    total,
    landing,
    in_send,
    in_recv,
    local_sem,
    z_send,
    z_recv,
    back_send,
    back_recv,
    out_send,
    out_recv,
    out_local,
    table_sem,
):
    b, u = lax.axis_index("blk"), lax.axis_index("uly")
    tiles_here = n_uly
    width = heads_here * DH
    copies = repeat_count // heads_here
    direct = copies == 1
    f32 = jnp.float32
    my_cols = aligned(u * width, width)
    my_group = aligned(u * DH, DH)
    peer_of = functools.partial(partner, u, n=n_uly)

    def pieces(peer):
        group = lax.div(peer * heads_here, repeat_count)
        kv_cols = aligned(group * DH, DH)
        q_cols = aligned(peer * width, width)
        return (
            (k_ref.at[:, kv_cols], window.at[tiles_here + u, 0]),
            (v_ref.at[:, kv_cols], window.at[tiles_here + u, 1]),
            (dl_ref.at[peer], dl_all.at[u]),
            (q_ref.at[:, q_cols], q_all.at[u]),
            (do_ref.at[:, q_cols], do_all.at[u]),
        )

    def out_pieces(peer):
        if direct:
            ends = (dk_ref.at[:, my_group], dv_ref.at[:, my_group])
        else:
            ends = (landing.at[0, u], landing.at[1, u])
        return (
            (total.at[peer, 0], ends[0]),
            (total.at[peer, 1], ends[1]),
            (dq_all.at[peer], dq_ref.at[:, my_cols]),
        )

    def remote(parts, kind, s, send, recv):
        peer = peer_of(s)
        src, dst = parts(peer)[kind]
        return pltpu.make_async_remote_copy(
            src_ref=src,
            dst_ref=dst,
            send_sem=send.at[kind, s],
            recv_sem=recv.at[kind, s],
            device_id=(b, peer),
            device_id_type=MESH,
        )

    def inward(kind, s):
        return remote(pieces, kind, s, in_send, in_recv)

    def outward(kind, s):
        return remote(out_pieces, kind, s, out_send, out_recv)

    def local(kind):
        src, dst = pieces(u)[kind]
        return pltpu.make_async_copy(src, dst, local_sem.at[kind])

    def out_own(kind):
        src, dst = out_pieces(u)[kind]
        return pltpu.make_async_copy(src, dst, out_local.at[kind])

    def forward(a):
        return pltpu.make_async_remote_copy(
            src_ref=window.at[tiles_here + a],
            dst_ref=window.at[a],
            send_sem=z_send.at[a],
            recv_sem=z_recv.at[a],
            device_id=(lax.rem(b + 1, n_blk), u),
            device_id_type=MESH,
        )

    def backward(a):
        return pltpu.make_async_remote_copy(
            src_ref=back.at[a],
            dst_ref=returned.at[a],
            send_sem=back_send.at[a],
            recv_sem=back_recv.at[a],
            device_id=(lax.rem(b + n_blk - 1, n_blk), u),
            device_id_type=MESH,
        )

    def each(first, last, body):
        lax.fori_loop(first, last, lambda s, _: (body(s), 0)[1], 0)

    has_next = b < n_blk - 1
    has_prev = b > 0

    tables = (
        pltpu.make_async_copy(list_hbm, list_ref, table_sem.at[0]),
        pltpu.make_async_copy(lang_hbm, lang_ref, table_sem.at[1]),
        pltpu.make_async_copy(
            docs_hbm.at[aligned(jnp.maximum(b - 1, 0) * tiles_here, tiles_here), :],
            code_ref.at[pl.ds(0, tiles_here), :],
            table_sem.at[2],
        ),
        pltpu.make_async_copy(
            docs_hbm.at[aligned(b * tiles_here, tiles_here), :],
            code_ref.at[pl.ds(tiles_here, tiles_here), :],
            table_sem.at[3],
        ),
    )
    for kind in range(5):
        local(kind).start()
    for table in tables:
        table.start()
    greet(b, u, n_blk, n_uly)

    def send_keys(s):
        inward(0, s).start()
        inward(1, s).start()

    def send_rows(s):
        inward(2, s).start()
        inward(3, s).start()
        inward(4, s).start()

    each(1, n_uly, send_keys)
    each(1, min(LOOK, n_uly - 1) + 1, send_rows)
    local(0).wait()
    local(1).wait()

    @pl.when(has_next)
    def _():
        forward(u).start()

    for table in tables:
        table.wait()
    docs = code_ref[...]

    def look_up(d, lang):
        return lang + jnp.where(docs == d, lang_ref[d], 0)

    lang = lax.fori_loop(0, lang_ref.shape[0], look_up, jnp.zeros_like(docs))
    code_ref[...] = docs * LANGS + lang

    def prepare(t):
        key_codes[t] = jnp.broadcast_to(code_ref[pl.ds(t, 1), :], (BLOCK, BLOCK)).T
        acc[t] = jnp.zeros(acc.shape[1:], f32)

    each(0, 2 * tiles_here, prepare)

    @pl.when(b == 0)
    def _():
        window[0:tiles_here] = jnp.zeros((tiles_here,) + window.shape[1:], window.dtype)

    def pass_on(s):
        inward(0, s).wait_recv()
        inward(1, s).wait_recv()

        @pl.when(has_next)
        def _():
            forward(peer_of(s)).start()

    each(1, n_uly, pass_on)

    @pl.when(has_prev)
    def _():
        each(0, tiles_here, lambda a: forward(a).wait_recv())

    local(2).wait()
    local(3).wait()
    local(4).wait()

    scaling = float(DH) ** (-0.5)
    across = (((1,), (1,)), ((), ()))
    gap = lax.broadcasted_iota(jnp.int32, (BLOCK, BLOCK), 0) - lax.broadcasted_iota(
        jnp.int32, (BLOCK, BLOCK), 1
    )
    group_here = lax.div(u * heads_here, repeat_count)

    def tile_work(a):
        tile = b * tiles_here + a
        listed = [list_ref[group_here, l, tile] for l in range(list_count)]
        cands = [tile - 1, tile] + listed
        own_slot = tiles_here + a
        window_first = (b - 1) * tiles_here
        query_code = code_ref[pl.ds(own_slot, 1), :]
        query_lang = query_code & (LANGS - 1)
        slots = []
        biases = []
        for c, cand in enumerate(cands):
            usable = cand >= 0
            for other in cands[: c if c >= 2 else 0]:
                usable = usable & (cand != other)
            marked = cand == listed[0]
            for other in listed[1:]:
                marked = marked | (cand == other)
            if c < 2:
                slot = own_slot - 1 + c
            else:
                slot = jnp.clip(cand - window_first, 0, 2 * tiles_here - 1)
            limit = jnp.where(usable, (tile - cand) * BLOCK, -2 * BLOCK)
            seen_lang = jnp.where(marked, query_lang, -1)
            key_code = key_codes[slot]
            allowed = (gap <= limit) & (
                (key_code == query_code) | ((key_code & (LANGS - 1)) == seen_lang)
            )
            slots.append(slot)
            biases.append(jnp.where(allowed, 0.0, MASKED))

        def stacked(rows):
            return jnp.concatenate([rows[:, h * DH : (h + 1) * DH] for h in range(heads_here)], 0)

        bias = jnp.concatenate(biases, axis=0)
        bias = jnp.concatenate([bias] * heads_here, axis=1)
        key_part = jnp.concatenate([window[s, 0] for s in slots], axis=0)
        value_part = jnp.concatenate([window[s, 1] for s in slots], axis=0)
        query_part = stacked(q_all[a])
        dout_part = stacked(do_all[a])
        delta_tile = dl_all[a]
        delta = jnp.concatenate([delta_tile[h : h + 1, :] for h in range(heads_here)], axis=1)
        scores = lax.dot_general(key_part, query_part, across, preferred_element_type=f32)
        scores = scores * scaling + bias
        top = jnp.max(scores, axis=0, keepdims=True)
        raised = jnp.exp(scores - top)
        weights = raised * (1.0 / jnp.sum(raised, axis=0, keepdims=True))
        grad_weights = lax.dot_general(value_part, dout_part, across, preferred_element_type=f32)
        grad_scores = (weights * (grad_weights - delta)).astype(jnp.bfloat16)
        grad_query = scaling * lax.dot_general(
            grad_scores, key_part, (((0,), (0,)), ((), ())), preferred_element_type=f32
        )
        for h in range(heads_here):
            dq_all[a, :, h * DH : (h + 1) * DH] = grad_query[h * BLOCK : (h + 1) * BLOCK].astype(
                dq_all.dtype
            )
        grad_key = scaling * jnp.dot(grad_scores, query_part, preferred_element_type=f32)
        grad_value = jnp.dot(weights.astype(jnp.bfloat16), dout_part, preferred_element_type=f32)
        parts = (grad_key, grad_value)
        for c in range(2):
            for k in range(2):
                acc[slots[c], k] += parts[k][c * BLOCK : (c + 1) * BLOCK]

        def spread(t):
            for k in range(2):
                more = acc[t, k]
                for c in range(2, 2 + list_count):
                    piece = parts[k][c * BLOCK : (c + 1) * BLOCK]
                    more = more + jnp.where(slots[c] == t, piece, 0.0)
                acc[t, k] = more

        each(0, 2 * tiles_here, spread)

    tile_work(u)
    out_own(2).start()

    def step(s):
        @pl.when(s + LOOK < n_uly)
        def _():
            send_rows(s + LOOK)

        inward(2, s).wait_recv()
        inward(3, s).wait_recv()
        inward(4, s).wait_recv()
        tile_work(peer_of(s))
        outward(2, s).start()

    each(1, n_uly, step)

    @pl.when(has_prev)
    def _():
        def give_back(s):
            a = peer_of(s)
            back[a] = acc[a].astype(back.dtype)
            backward(a).start()

        each(0, n_uly, give_back)

    def settle(s):
        a = peer_of(s)

        @pl.when(has_next)
        def _():
            backward(a).wait_recv()
            total[a] = (acc[tiles_here + a] + returned[a].astype(f32)).astype(total.dtype)

        @pl.when(b == n_blk - 1)
        def _():
            total[a] = acc[tiles_here + a].astype(total.dtype)

    settle(0)
    out_own(0).start()
    out_own(1).start()

    def settle_and_send(s):
        settle(s)
        outward(0, s).start()
        outward(1, s).start()

    each(1, n_uly, settle_and_send)

    for kind in range(3):
        out_own(kind).wait()

    def finish(s):
        for kind in range(3):
            outward(kind, s).wait_recv()
        for kind in range(5):
            inward(kind, s).wait_send()
        for kind in range(3):
            outward(kind, s).wait_send()

    each(1, n_uly, finish)

    @pl.when(has_next)
    def _():
        each(0, n_uly, lambda a: forward(a).wait_send())

    @pl.when(has_prev)
    def _():
        each(0, n_uly, lambda a: backward(a).wait_send())

    if not direct:
        for kind, out in ((0, dk_ref), (1, dv_ref)):
            for g in range(n_uly // copies):
                summed = landing[kind, g * copies].astype(f32)
                for r in range(1, copies):
                    summed = summed + landing[kind, g * copies + r].astype(f32)
                out[:, g * DH : (g + 1) * DH] = summed.astype(out.dtype)


def split_kernel(
    n_blk,
    list_count,
    list_hbm,
    lang_hbm,
    docs_hbm,
    q_ref,
    do_ref,
    k_ref,
    v_ref,
    dl_ref,
    dq_ref,
    dk_ref,
    dv_ref,
    q_all,
    do_all,
    dl_all,
    window_row,
    window_column,
    list_ref,
    lang_ref,
    order_ref,
    same_ref,
    place_ref,
    code_ref,
    key_codes,
    acc,
    entries,
    sums,
    scores_held,
    dq_all,
    back,
    returned,
    across_out,
    across_in,
    total,
    in_send,
    in_recv,
    local_sem,
    far_send,
    far_recv,
    relay_send,
    relay_recv,
    z_send,
    z_recv,
    back_send,
    back_recv,
    across_send,
    across_recv,
    out_send,
    out_recv,
    out_local,
    table_sem,
    gate,
):
    b, u = lax.axis_index("blk"), lax.axis_index("uly")
    y, x, c = lax.div(u, 4), lax.rem(lax.div(u, 2), 2), lax.rem(u, 2)
    tiles_here = SPLIT
    width = HALF * DH
    f32 = jnp.float32
    windows = (window_row, window_column)
    has_next = b < n_blk - 1
    has_prev = b > 0

    def job_of(f, near):
        return lax.rem(f + c + near, 2)

    def member(j, s, far):
        along, near = lax.div(s, 2), lax.rem(s, 2)
        row = lax.rem(y + along * j + far * (1 - j), 2)
        column = lax.rem(x + along * (1 - j) + far * j, 2)
        return 4 * row + 2 * column + lax.rem(c + near, 2)

    def peer_of(f, s):
        return member(job_of(f, 0), s, 0)

    def far_of(f, s):
        return member(job_of(f, 0), s, 1)

    def position(j, s):
        return HALF * j + 2 * lax.rem(x * (1 - j) + y * j + lax.div(s, 2), 2) + lax.rem(c + lax.rem(s, 2), 2)

    def group_of(f):
        return position(job_of(f, 0), 0)

    def target_of(f, s):
        return member(job_of(f, lax.rem(s, 2)), s, 0)

    def pieces(f, s):
        group = position(job_of(f, lax.rem(s, 2)), s)
        kv_cols = aligned(group * DH, DH)
        q_cols = aligned(group * width, width)
        return (
            (k_ref.at[:, kv_cols], windows[f].at[tiles_here + u, 0]),
            (v_ref.at[:, kv_cols], windows[f].at[tiles_here + u, 1]),
            (dl_ref.at[group], dl_all.at[f, s]),
            (q_ref.at[:, q_cols], q_all.at[f, s]),
            (do_ref.at[:, q_cols], do_all.at[f, s]),
        )

    def out_pieces(f, s):
        group = group_of(f)
        kv_cols = aligned(group * DH, DH)
        return (
            (total.at[f, s, 0], dk_ref.at[:, kv_cols]),
            (total.at[f, s, 1], dv_ref.at[:, kv_cols]),
            (dq_all.at[f, s], dq_ref.at[:, aligned(group * width, width)]),
        )

    def remote(src, dst, send, recv, device):
        return pltpu.make_async_remote_copy(
            src_ref=src, dst_ref=dst, send_sem=send, recv_sem=recv, device_id=device, device_id_type=MESH
        )

    def inward(j, kind, s):
        src, dst = pieces(j, s)[kind]
        return remote(src, dst, in_send.at[j, kind, s], in_recv.at[j, kind, s], (b, target_of(j, s)))

    def direct(kind, s):
        src, dst = pieces(0, s)[kind]
        return remote(
            src, dst, far_send.at[kind, s], far_recv.at[kind, s], (b, member(job_of(0, lax.rem(s, 2)), s, 1))
        )

    def outward(j, kind, s):
        src, dst = out_pieces(j, s)[kind]
        return remote(src, dst, out_send.at[j, kind, s], out_recv.at[j, kind, s], (b, peer_of(j, s)))

    def local(j, kind):
        src, dst = pieces(j, 0)[kind]
        return pltpu.make_async_copy(src, dst, local_sem.at[j, kind])

    def out_own(j, kind):
        src, dst = out_pieces(j, 0)[kind]
        return pltpu.make_async_copy(src, dst, out_local.at[j, kind])

    def relay(s):
        held = windows[1].at[tiles_here + peer_of(1, s)]
        return remote(held, held, relay_send.at[s], relay_recv.at[s], (b, far_of(1, 0)))

    def forward(j, a):
        return remote(
            windows[j].at[tiles_here + a],
            windows[j].at[a],
            z_send.at[j, a],
            z_recv.at[j, a],
            (lax.rem(b + 1, n_blk), u),
        )

    def backward(j, a):
        return remote(
            back.at[j, a],
            returned.at[j, a],
            back_send.at[j, a],
            back_recv.at[j, a],
            (lax.rem(b + n_blk - 1, n_blk), u),
        )

    def over(j, s):
        return remote(
            across_out.at[j, s],
            across_in.at[j, s],
            across_send.at[j, s],
            across_recv.at[j, s],
            (b, far_of(j, 0)),
        )

    def each(first, last, body):
        lax.fori_loop(first, last, lambda s, _: (body(s), 0)[1], 0)

    def last_first(body):
        each(0, HALF, lambda n: body(HALF - 1 - n))

    def send_on(j, a):
        @pl.when(has_next)
        def _():
            forward(j, a).start()

    tables = (
        pltpu.make_async_copy(list_hbm, list_ref, table_sem.at[0]),
        pltpu.make_async_copy(lang_hbm, lang_ref, table_sem.at[1]),
        pltpu.make_async_copy(
            docs_hbm.at[aligned(jnp.maximum(b - 1, 0) * tiles_here, tiles_here), :],
            code_ref.at[pl.ds(0, tiles_here), :],
            table_sem.at[2],
        ),
        pltpu.make_async_copy(
            docs_hbm.at[aligned(b * tiles_here, tiles_here), :],
            code_ref.at[pl.ds(tiles_here, tiles_here), :],
            table_sem.at[3],
        ),
    )
    for j in range(2):
        for kind in range(5):
            local(j, kind).start()
    for table in tables:
        table.start()

    barrier = pltpu.get_barrier_semaphore()
    friends = [member(0, s, far) for far in range(2) for s in range(HALF) if s + far > 0]
    for friend in friends:
        pl.semaphore_signal(barrier, inc=1, device_id=(b, friend), device_id_type=MESH)

    @pl.when(has_prev)
    def _():
        pl.semaphore_signal(barrier, inc=1, device_id=(b - 1, u), device_id_type=MESH)

    @pl.when(has_next)
    def _():
        pl.semaphore_signal(barrier, inc=1, device_id=(b + 1, u), device_id_type=MESH)

    ends = jnp.where(has_prev, 1, 0) + jnp.where(has_next, 1, 0)
    pl.semaphore_wait(barrier, len(friends) + ends)

    def start_keys(j):
        def body(s):
            inward(j, 0, s).start()
            inward(j, 1, s).start()

        each(1, HALF, body)

    def start_rows(j):
        def body(s):
            for kind in (2, 3, 4):
                inward(j, kind, s).start()

        each(1, HALF, body)

    def start_rows_of(j, core):
        def body(n):
            s = lax.rem(c + core, 2) + 2 * n

            @pl.when(s > 0)
            def _():
                for kind in (2, 3, 4):
                    inward(j, kind, s).start()

        each(0, 2, body)

    def keys_here(j, s):
        inward(j, 0, s).wait_recv()
        inward(j, 1, s).wait_recv()

    def drained(j):
        @pl.when(has_next)
        def _():
            each(0, HALF, lambda s: forward(j, peer_of(j, s)).wait_send())
            each(0, HALF - SLACK, lambda s: forward(j, far_of(j, s)).wait_send())

    def let_go(n):
        pl.semaphore_signal(gate.at[n], inc=1, device_id=(b, member(0, 1, 0)), device_id_type=MESH)

    def start_far(s):
        direct(0, s).start()
        direct(1, s).start()

    def pass_near(s):
        keys_here(0, s)

        @pl.when(c == 0)
        def _():
            send_on(0, peer_of(0, s))

    def pass_far(s):
        direct(0, s).wait_recv()
        direct(1, s).wait_recv()

        @pl.when(c == 0)
        def _():
            send_on(0, far_of(0, s))

    start_keys(0)
    each(0, HALF, start_far)
    start_keys(1)
    start_rows_of(0, 0)
    local(0, 0).wait()
    local(0, 1).wait()

    send_on(0, u)
    keys_here(0, 1)
    send_on(0, peer_of(0, 1))

    for table in tables:
        table.wait()
    docs = code_ref[...]

    def look_up(d, lang):
        return lang + jnp.where(docs == d, lang_ref[d], 0)

    lang = lax.fori_loop(0, lang_ref.shape[0], look_up, jnp.zeros_like(docs))
    code_ref[...] = docs * LANGS + lang

    window_first = (b - 1) * tiles_here

    def slot_of(cand):
        return jnp.clip(cand - window_first, 0, 2 * tiles_here - 1)

    def plan(j):
        group = group_of(j)
        count = HALF * list_count
        slots = [
            slot_of(list_ref[group, l, b * tiles_here + peer_of(j, s)]) for s in range(HALF) for l in range(list_count)
        ]
        ranks = []
        for e in range(count):
            rank = 0
            for other in range(count):
                if other < e:
                    rank = rank + jnp.where(slots[other] <= slots[e], 1, 0)
                elif other > e:
                    rank = rank + jnp.where(slots[other] < slots[e], 1, 0)
            ranks.append(rank)
        before = -1
        for i in range(count):
            entry, slot = 0, 0
            for e in range(count):
                entry = entry + jnp.where(ranks[e] == i, e, 0)
                slot = slot + jnp.where(ranks[e] == i, slots[e], 0)
            order_ref[j, i] = entry
            same_ref[j, i] = jnp.where(slot == before, 1, 0)
            before = slot
        for t in range(2 * tiles_here):
            upto, here = 0, 0
            for slot in slots:
                upto = upto + jnp.where(slot <= t, 1, 0)
                here = here + jnp.where(slot == t, 1, 0)
            place_ref[j, t] = jnp.where(here > 0, upto - 1, count)

    def prepare(t):
        key_codes[t] = jnp.broadcast_to(code_ref[pl.ds(t, 1), :], (BLOCK, BLOCK)).T
        acc[0, t] = jnp.zeros(acc.shape[2:], f32)
        acc[1, t] = jnp.zeros(acc.shape[2:], f32)

    each(0, 2 * tiles_here, prepare)
    for j in range(2):
        plan(j)
        sums[j, HALF * list_count] = jnp.zeros(sums.shape[2:], f32)

    @pl.when(b == 0)
    def _():
        for window in windows:
            window[0:tiles_here] = jnp.zeros((tiles_here,) + window.shape[1:], window.dtype)

    scaling = float(DH) ** (-0.5)
    across = (((1,), (1,)), ((), ()))
    gap = lax.broadcasted_iota(jnp.int32, (BLOCK, BLOCK), 0) - lax.broadcasted_iota(
        jnp.int32, (BLOCK, BLOCK), 1
    )

    def query_work(j, s, grad_scores, key_part):
        grad_query = scaling * lax.dot_general(
            key_part, grad_scores, (((0,), (0,)), ((), ())), preferred_element_type=f32
        )
        for h in range(HALF):
            turned = grad_query[:, h * BLOCK : (h + 1) * BLOCK].T
            dq_all[j, s, :, h * DH : (h + 1) * DH] = turned.astype(dq_all.dtype)

    def tile_work(j, s):
        group = group_of(j)
        place = peer_of(j, s)
        tile = b * tiles_here + place
        listed = [list_ref[group, l, tile] for l in range(list_count)]
        cands = [tile - 1, tile] + listed
        own_slot = tiles_here + place
        query_code = code_ref[pl.ds(own_slot, 1), :]
        query_lang = query_code & (LANGS - 1)
        slots = []
        biases = []
        for n, cand in enumerate(cands):
            usable = cand >= 0
            for other in cands[: n if n >= 2 else 0]:
                usable = usable & (cand != other)
            marked = cand == listed[0]
            for other in listed[1:]:
                marked = marked | (cand == other)
            slot = own_slot - 1 + n if n < 2 else slot_of(cand)
            limit = jnp.where(usable, (tile - cand) * BLOCK, -2 * BLOCK)
            seen_lang = jnp.where(marked, query_lang, -1)
            key_code = key_codes[slot]
            allowed = (gap <= limit) & (
                (key_code == query_code) | ((key_code & (LANGS - 1)) == seen_lang)
            )
            slots.append(slot)
            biases.append(jnp.where(allowed, 0.0, MASKED))

        def stacked(rows):
            return jnp.concatenate([rows[:, h * DH : (h + 1) * DH] for h in range(HALF)], 0)

        bias = jnp.concatenate(biases, axis=0)
        bias = jnp.concatenate([bias] * HALF, axis=1)
        key_part = jnp.concatenate([windows[j][t, 0] for t in slots], axis=0)
        value_part = jnp.concatenate([windows[j][t, 1] for t in slots], axis=0)
        query_part = stacked(q_all[j, s])
        dout_part = stacked(do_all[j, s])
        delta_tile = dl_all[j, s]
        delta = jnp.concatenate([delta_tile[h : h + 1, :] for h in range(HALF)], axis=1)
        scores = lax.dot_general(key_part, query_part, across, preferred_element_type=f32)
        scores = scores * (scaling * LOG2_E) + bias
        top = jnp.max(scores, axis=0, keepdims=True)
        raised = jnp.exp2(scores - top)
        weights = raised * (1.0 / jnp.sum(raised, axis=0, keepdims=True))
        grad_weights = lax.dot_general(value_part, dout_part, across, preferred_element_type=f32)
        grad_scores = (weights * (grad_weights - delta)).astype(jnp.bfloat16)
        if j == 1:
            scores_held[s] = grad_scores
        else:
            query_work(j, s, grad_scores, key_part)
        grad_key = scaling * jnp.dot(grad_scores, query_part, preferred_element_type=f32)
        grad_value = jnp.dot(weights.astype(jnp.bfloat16), dout_part, preferred_element_type=f32)
        for k, part in ((0, grad_key), (1, grad_value)):
            for n in range(2):
                acc[j, slots[n], k] += part[n * BLOCK : (n + 1) * BLOCK]
            for l in range(list_count):
                first = (2 + l) * BLOCK
                entries[s * list_count + l, k] = part[first : first + BLOCK]

    def add_listed(j):
        sums[j, 0] = entries[order_ref[j, 0]]

        def body(i):
            earlier = jnp.where(same_ref[j, i] == 1, sums[j, i - 1], 0.0)
            sums[j, i] = entries[order_ref[j, i]] + earlier

        each(1, HALF * list_count, body)

    def slot_sum(j, t):
        return acc[j, t] + sums[j, place_ref[j, t]]

    def arrived(j):
        @pl.when(has_prev)
        def _():
            each(0, tiles_here, lambda a: forward(j, a).wait_recv())

    def give_back(j):
        add_listed(j)

        @pl.when(has_prev)
        def _():
            def body(a):
                back[j, a] = slot_sum(j, a).astype(back.dtype)
                backward(j, a).start()

            last_first(lambda s: body(far_of(j, s)))
            last_first(lambda s: body(peer_of(j, s)))

    def send_queries(j, s):
        @pl.when(s > 0)
        def _():
            outward(j, 2, s).start()

        @pl.when(s == 0)
        def _():
            out_own(j, 2).start()

    def late_queries(s):
        place = tiles_here + peer_of(1, s)
        slots = [place - 1, place] + [
            slot_of(list_ref[group_of(1), l, b * tiles_here + peer_of(1, s)]) for l in range(list_count)
        ]
        query_work(1, s, scores_held[s], jnp.concatenate([windows[1][t, 0] for t in slots], axis=0))
        send_queries(1, s)

    def work(j, s):
        @pl.when(s > 0)
        def _():
            for kind in (2, 3, 4):
                inward(j, kind, s).wait_recv()

        tile_work(j, s)

        if j == 0:
            send_queries(j, s)

    def with_returned(j, a, then):
        @pl.when(has_next)
        def _():
            backward(j, a).wait_recv()
            then(slot_sum(j, tiles_here + a) + returned[j, a].astype(f32))

        @pl.when(b == n_blk - 1)
        def _():
            then(slot_sum(j, tiles_here + a))

    def settle_far(j, s):
        def then(value):
            across_out[j, s] = value.astype(across_out.dtype)

        with_returned(j, far_of(j, s), then)
        over(j, s).start()

    def settle(j, s):
        over(j, s).wait_recv()

        def then(value):
            total[j, s] = (value + across_in[j, s].astype(f32)).astype(total.dtype)

        with_returned(j, peer_of(j, s), then)

        @pl.when(s > 0)
        def _():
            outward(j, 0, s).start()
            outward(j, 1, s).start()

        @pl.when(s == 0)
        def _():
            out_own(j, 0).start()
            out_own(j, 1).start()

    each(2, HALF, pass_near)
    each(0, HALF, pass_far)
    local(1, 0).wait()
    local(1, 1).wait()
    relay(0).start()

    def relay_keys(s):
        keys_here(1, s)
        relay(s).start()

    each(1, HALF, relay_keys)
    start_rows_of(0, 1)
    start_rows(1)

    @pl.when(c == 1)
    def _():
        pl.semaphore_wait(gate.at[0], 1)
        each(2, HALF, lambda s: send_on(0, peer_of(0, s)))
        each(0, HALF, lambda s: send_on(0, far_of(0, s)))
        drained(0)
        let_go(1)

    @pl.when(c == 0)
    def _():
        drained(0)
        let_go(0)

    arrived(0)
    for kind in (2, 3, 4):
        local(0, kind).wait()

    def first_step(s):
        work(0, s)

    each(0, HALF, first_step)
    give_back(0)

    @pl.when(c == 0)
    def _():
        pl.semaphore_wait(gate.at[1], 1)

    @pl.when(c == 1)
    def _():
        pl.semaphore_wait(gate.at[2], 1)

    each(0, HALF, lambda s: send_on(1, peer_of(1, s)))

    def pass_far_second(s):
        relay(s).wait_recv()
        send_on(1, far_of(1, s))

    each(0, HALF, pass_far_second)

    @pl.when(c == 0)
    def _():
        drained(1)
        let_go(2)

    last_first(lambda s: settle_far(0, s))
    arrived(1)
    for kind in (2, 3, 4):
        local(1, kind).wait()

    last_first(lambda s: work(1, s))
    give_back(1)
    last_first(late_queries)
    last_first(lambda s: settle(0, s))
    last_first(lambda s: settle_far(1, s))
    last_first(lambda s: settle(1, s))

    for j in range(2):
        for kind in range(3):
            out_own(j, kind).wait()

        def finish(s):
            for kind in range(3):
                outward(j, kind, s).wait_recv()
            for kind in range(5):
                inward(j, kind, s).wait_send()
            for kind in range(3):
                outward(j, kind, s).wait_send()

        each(1, HALF, finish)

        def finish_far(s):
            over(j, s).wait_send()
            if j == 0:
                direct(0, s).wait_send()
                direct(1, s).wait_send()
            else:
                relay(s).wait_send()

        each(0, HALF, finish_far)

        @pl.when(has_next)
        def _():
            if j == 0:
                each(HALF - SLACK, HALF, lambda s: forward(j, far_of(j, s)).wait_send())
            else:

                @pl.when(c == 0)
                def _():
                    each(HALF - SLACK, HALF, lambda s: forward(j, far_of(j, s)).wait_send())

                @pl.when(c == 1)
                def _():
                    each(0, tiles_here, lambda a: forward(j, a).wait_send())

        @pl.when(has_prev)
        def _():
            each(0, tiles_here, lambda a: backward(j, a).wait_send())


def split_grads(lists, doc_lang, docs, queries, grad_out, keys, values, delta_rows, n_blk):
    list_count = lists.shape[1]
    width = HALF * DH
    anywhere = pl.BlockSpec(memory_space=pl.ANY)
    bf16, f32 = jnp.bfloat16, jnp.float32
    pair = (2, BLOCK, DH)
    dma = pltpu.SemaphoreType.DMA
    entry_count = HALF * list_count
    return pl.pallas_call(
        functools.partial(split_kernel, n_blk, list_count),
        out_shape=(
            jax.ShapeDtypeStruct(queries.shape, bf16),
            jax.ShapeDtypeStruct(keys.shape, bf16),
            jax.ShapeDtypeStruct(values.shape, bf16),
        ),
        in_specs=[anywhere] * 8,
        out_specs=(anywhere,) * 3,
        scratch_shapes=[
            pltpu.VMEM((2, HALF, BLOCK, width), bf16),
            pltpu.VMEM((2, HALF, BLOCK, width), bf16),
            pltpu.VMEM((2, HALF, HALF, BLOCK), f32),
            pltpu.VMEM((2 * SPLIT,) + pair, bf16),
            pltpu.VMEM((2 * SPLIT,) + pair, bf16),
            pltpu.SMEM(lists.shape, jnp.int32),
            pltpu.SMEM(doc_lang.shape, jnp.int32),
            pltpu.SMEM((2, entry_count), jnp.int32),
            pltpu.SMEM((2, entry_count), jnp.int32),
            pltpu.SMEM((2, 2 * SPLIT), jnp.int32),
            pltpu.VMEM((2 * SPLIT, BLOCK), jnp.int32),
            pltpu.VMEM((2 * SPLIT, BLOCK, BLOCK), jnp.int32),
            pltpu.VMEM((2, 2 * SPLIT) + pair, f32),
            pltpu.VMEM((entry_count,) + pair, f32),
            pltpu.VMEM((2, entry_count + 1) + pair, f32),
            pltpu.VMEM((HALF, (2 + list_count) * BLOCK, width), bf16),
            pltpu.VMEM((2, HALF, BLOCK, width), bf16),
            pltpu.VMEM((2, SPLIT) + pair, bf16),
            pltpu.VMEM((2, SPLIT) + pair, bf16),
            pltpu.VMEM((2, HALF) + pair, bf16),
            pltpu.VMEM((2, HALF) + pair, bf16),
            pltpu.VMEM((2, HALF) + pair, bf16),
            dma((2, 5, HALF)),
            dma((2, 5, HALF)),
            dma((2, 5)),
            dma((2, HALF)),
            dma((2, HALF)),
            dma((HALF,)),
            dma((HALF,)),
            dma((2, SPLIT)),
            dma((2, SPLIT)),
            dma((2, SPLIT)),
            dma((2, SPLIT)),
            dma((2, HALF)),
            dma((2, HALF)),
            dma((2, 3, HALF)),
            dma((2, 3, HALF)),
            dma((2, 3)),
            dma((4,)),
            pltpu.SemaphoreType.REGULAR((3,)),
        ],
        compiler_params=pltpu.CompilerParams(
            collective_id=0, has_side_effects=True, vmem_limit_bytes=VMEM_LIMIT
        ),
        name="split_grads",
    )(lists, doc_lang, docs, queries, grad_out, keys, values, delta_rows)


def hand_over_kernel(*refs):
    count = (len(refs) - 2) // 3
    in_sem, out_sem = refs[-2:]
    moves = []
    for k in range(count):
        src, dst, held = refs[k], refs[count + k], refs[2 * count + k]
        part = src.shape[0] // CHUNKS
        for c in range(CHUNKS):
            rows = pl.ds(c * part, part)
            moves.append(
                (
                    pltpu.make_async_copy(src.at[rows, :], held.at[rows, :], in_sem.at[k, c]),
                    pltpu.make_async_copy(held.at[rows, :], dst.at[rows, :], out_sem.at[k, c]),
                )
            )
    for fetch, _ in moves:
        fetch.start()
    for fetch, store in moves:
        fetch.wait()
        store.start()
    for _, store in moves:
        store.wait()


def handed_over(arrays):
    anywhere = pl.BlockSpec(memory_space=pl.ANY)
    count = len(arrays)
    return pl.pallas_call(
        hand_over_kernel,
        out_shape=tuple(jax.ShapeDtypeStruct(x.shape, x.dtype) for x in arrays),
        in_specs=[anywhere] * count,
        out_specs=(anywhere,) * count,
        scratch_shapes=[pltpu.VMEM(x.shape, x.dtype) for x in arrays]
        + [pltpu.SemaphoreType.DMA((count, CHUNKS)), pltpu.SemaphoreType.DMA((count, CHUNKS))],
        name="hand_over",
    )(*arrays)


def shards(queries, keys, values, grad_out, row_delta, doc_ids, doc_lang, tile_list):
    tok_count, full_width = queries.shape
    heads_all = full_width // DH
    groups_all = keys.shape[1] // DH
    repeat_count = heads_all // groups_all
    n_uly = lax.axis_size("uly")
    n_blk = lax.axis_size("blk")
    heads_here = heads_all // n_uly
    width = heads_here * DH
    copies = repeat_count // heads_here
    lists = tile_list.transpose(0, 2, 1)
    docs = doc_ids.reshape(-1, BLOCK)
    delta_rows = row_delta.T.reshape(n_uly, heads_here, tok_count)
    if n_uly == SPLIT and groups_all == SPLIT and repeat_count == HALF and tok_count == BLOCK:
        return handed_over(
            split_grads(lists, doc_lang, docs, queries, grad_out, keys, values, delta_rows, n_blk)
        )
    anywhere = pl.BlockSpec(memory_space=pl.ANY)
    in_vmem = pl.BlockSpec(memory_space=pltpu.VMEM)
    kv_spec = in_vmem if copies > 1 else anywhere
    bf16, f32 = jnp.bfloat16, jnp.float32
    pair = (2, BLOCK, DH)
    dma = pltpu.SemaphoreType.DMA
    outs = pl.pallas_call(
        functools.partial(
            fused_kernel,
            n_blk,
            n_uly,
            tile_list.shape[2],
            heads_here,
            repeat_count,
        ),
        out_shape=(
            jax.ShapeDtypeStruct(queries.shape, bf16),
            jax.ShapeDtypeStruct(keys.shape, bf16),
            jax.ShapeDtypeStruct(values.shape, bf16),
        ),
        in_specs=[anywhere] * 8,
        out_specs=(anywhere, kv_spec, kv_spec),
        scratch_shapes=[
            pltpu.VMEM((n_uly, BLOCK, width), bf16),
            pltpu.VMEM((n_uly, BLOCK, width), bf16),
            pltpu.VMEM((n_uly, heads_here, BLOCK), f32),
            pltpu.VMEM((2 * n_uly,) + pair, bf16),
            pltpu.SMEM(lists.shape, jnp.int32),
            pltpu.SMEM(doc_lang.shape, jnp.int32),
            pltpu.VMEM((2 * n_uly, BLOCK), jnp.int32),
            pltpu.VMEM((2 * n_uly, BLOCK, BLOCK), jnp.int32),
            pltpu.VMEM((2 * n_uly,) + pair, f32),
            pltpu.VMEM((n_uly, BLOCK, width), bf16),
            pltpu.VMEM((n_uly,) + pair, bf16),
            pltpu.VMEM((n_uly,) + pair, bf16),
            pltpu.VMEM((n_uly,) + pair, bf16),
            pltpu.VMEM((2, n_uly if copies > 1 else 1, BLOCK, DH), bf16),
            dma((5, n_uly)),
            dma((5, n_uly)),
            dma((5,)),
            dma((n_uly,)),
            dma((n_uly,)),
            dma((n_uly,)),
            dma((n_uly,)),
            dma((3, n_uly)),
            dma((3, n_uly)),
            dma((3,)),
            dma((4,)),
        ],
        compiler_params=pltpu.CompilerParams(
            collective_id=0, has_side_effects=True, vmem_limit_bytes=VMEM_LIMIT
        ),
        name="attention_grads",
    )(lists, doc_lang, docs, queries, grad_out, keys, values, delta_rows)
    return handed_over(outs)


def solution(mesh):
    placed = (
        P(("blk", "uly"), None),
        P(("blk", "uly"), None),
        P(("blk", "uly"), None),
        P(("blk", "uly"), None),
        P(("blk", "uly"), None),
        P(),
        P(),
        P(),
    )
    return jax.shard_map(
        shards,
        mesh=mesh,
        in_specs=placed,
        out_specs=(P(("blk", "uly"), None), P(("blk", "uly"), None), P(("blk", "uly"), None)),
        check_vma=False,
    )
```

```python
import functools

import jax
import jax.numpy as jnp
from jax import lax
from jax.experimental import pallas as pl
from jax.experimental.pallas import tpu as pltpu
from jax.sharding import PartitionSpec as P

DH = 128
BLOCK = 128
LANGS = 4
MASKED = -1e30
MESH = pl.DeviceIdType.MESH
LOOK = 7
CHUNKS = 2
SPLIT = 8
HALF = 4
SLACK = 1
LOG2_E = 1.4426950408889634
VMEM_LIMIT = 56 * 1024 * 1024


def greet(b, u, n_blk, n_uly):
    barrier = pltpu.get_barrier_semaphore()
    for p in range(1, n_uly):
        pl.semaphore_signal(
            barrier, inc=1, device_id=(b, lax.rem(u + p, n_uly)), device_id_type=MESH
        )

    @pl.when(b > 0)
    def _():
        pl.semaphore_signal(barrier, inc=1, device_id=(b - 1, u), device_id_type=MESH)

    @pl.when(b < n_blk - 1)
    def _():
        pl.semaphore_signal(barrier, inc=1, device_id=(b + 1, u), device_id_type=MESH)

    ends = jnp.where(b > 0, 1, 0) + jnp.where(b < n_blk - 1, 1, 0)
    pl.semaphore_wait(barrier, n_uly - 1 + ends)


def aligned(start, size):
    return pl.ds(pl.multiple_of(start, size), size)


def partner(u, s, n):
    found, bit = 0, 1
    while bit < n:
        found = found + bit * lax.rem(lax.div(u, bit) + lax.div(s, bit), 2)
        bit *= 2
    return found


def fused_kernel(
    n_blk,
    n_uly,
    list_count,
    heads_here,
    repeat_count,
    list_hbm,
    lang_hbm,
    docs_hbm,
    q_ref,
    do_ref,
    k_ref,
    v_ref,
    dl_ref,
    dq_ref,
    dk_ref,
    dv_ref,
    q_all,
    do_all,
    dl_all,
    window,
    list_ref,
    lang_ref,
    code_ref,
    key_codes,
    acc,
    dq_all,
    back,
    returned,
    total,
    landing,
    in_send,
    in_recv,
    local_sem,
    z_send,
    z_recv,
    back_send,
    back_recv,
    out_send,
    out_recv,
    out_local,
    table_sem,
):
    b, u = lax.axis_index("blk"), lax.axis_index("uly")
    tiles_here = n_uly
    width = heads_here * DH
    copies = repeat_count // heads_here
    direct = copies == 1
    f32 = jnp.float32
    my_cols = aligned(u * width, width)
    my_group = aligned(u * DH, DH)
    peer_of = functools.partial(partner, u, n=n_uly)

    def pieces(peer):
        group = lax.div(peer * heads_here, repeat_count)
        kv_cols = aligned(group * DH, DH)
        q_cols = aligned(peer * width, width)
        return (
            (k_ref.at[:, kv_cols], window.at[tiles_here + u, 0]),
            (v_ref.at[:, kv_cols], window.at[tiles_here + u, 1]),
            (dl_ref.at[peer], dl_all.at[u]),
            (q_ref.at[:, q_cols], q_all.at[u]),
            (do_ref.at[:, q_cols], do_all.at[u]),
        )

    def out_pieces(peer):
        if direct:
            ends = (dk_ref.at[:, my_group], dv_ref.at[:, my_group])
        else:
            ends = (landing.at[0, u], landing.at[1, u])
        return (
            (total.at[peer, 0], ends[0]),
            (total.at[peer, 1], ends[1]),
            (dq_all.at[peer], dq_ref.at[:, my_cols]),
        )

    def remote(parts, kind, s, send, recv):
        peer = peer_of(s)
        src, dst = parts(peer)[kind]
        return pltpu.make_async_remote_copy(
            src_ref=src,
            dst_ref=dst,
            send_sem=send.at[kind, s],
            recv_sem=recv.at[kind, s],
            device_id=(b, peer),
            device_id_type=MESH,
        )

    def inward(kind, s):
        return remote(pieces, kind, s, in_send, in_recv)

    def outward(kind, s):
        return remote(out_pieces, kind, s, out_send, out_recv)

    def local(kind):
        src, dst = pieces(u)[kind]
        return pltpu.make_async_copy(src, dst, local_sem.at[kind])

    def out_own(kind):
        src, dst = out_pieces(u)[kind]
        return pltpu.make_async_copy(src, dst, out_local.at[kind])

    def forward(a):
        return pltpu.make_async_remote_copy(
            src_ref=window.at[tiles_here + a],
            dst_ref=window.at[a],
            send_sem=z_send.at[a],
            recv_sem=z_recv.at[a],
            device_id=(lax.rem(b + 1, n_blk), u),
            device_id_type=MESH,
        )

    def backward(a):
        return pltpu.make_async_remote_copy(
            src_ref=back.at[a],
            dst_ref=returned.at[a],
            send_sem=back_send.at[a],
            recv_sem=back_recv.at[a],
            device_id=(lax.rem(b + n_blk - 1, n_blk), u),
            device_id_type=MESH,
        )

    def each(first, last, body):
        lax.fori_loop(first, last, lambda s, _: (body(s), 0)[1], 0)

    has_next = b < n_blk - 1
    has_prev = b > 0

    tables = (
        pltpu.make_async_copy(list_hbm, list_ref, table_sem.at[0]),
        pltpu.make_async_copy(lang_hbm, lang_ref, table_sem.at[1]),
        pltpu.make_async_copy(
            docs_hbm.at[aligned(jnp.maximum(b - 1, 0) * tiles_here, tiles_here), :],
            code_ref.at[pl.ds(0, tiles_here), :],
            table_sem.at[2],
        ),
        pltpu.make_async_copy(
            docs_hbm.at[aligned(b * tiles_here, tiles_here), :],
            code_ref.at[pl.ds(tiles_here, tiles_here), :],
            table_sem.at[3],
        ),
    )
    for kind in range(5):
        local(kind).start()
    for table in tables:
        table.start()
    greet(b, u, n_blk, n_uly)

    def send_keys(s):
        inward(0, s).start()
        inward(1, s).start()

    def send_rows(s):
        inward(2, s).start()
        inward(3, s).start()
        inward(4, s).start()

    each(1, n_uly, send_keys)
    each(1, min(LOOK, n_uly - 1) + 1, send_rows)
    local(0).wait()
    local(1).wait()

    @pl.when(has_next)
    def _():
        forward(u).start()

    for table in tables:
        table.wait()
    docs = code_ref[...]

    def look_up(d, lang):
        return lang + jnp.where(docs == d, lang_ref[d], 0)

    lang = lax.fori_loop(0, lang_ref.shape[0], look_up, jnp.zeros_like(docs))
    code_ref[...] = docs * LANGS + lang

    def prepare(t):
        key_codes[t] = jnp.broadcast_to(code_ref[pl.ds(t, 1), :], (BLOCK, BLOCK)).T
        acc[t] = jnp.zeros(acc.shape[1:], f32)

    each(0, 2 * tiles_here, prepare)

    @pl.when(b == 0)
    def _():
        window[0:tiles_here] = jnp.zeros((tiles_here,) + window.shape[1:], window.dtype)

    def pass_on(s):
        inward(0, s).wait_recv()
        inward(1, s).wait_recv()

        @pl.when(has_next)
        def _():
            forward(peer_of(s)).start()

    each(1, n_uly, pass_on)

    @pl.when(has_prev)
    def _():
        each(0, tiles_here, lambda a: forward(a).wait_recv())

    local(2).wait()
    local(3).wait()
    local(4).wait()

    scaling = float(DH) ** (-0.5)
    across = (((1,), (1,)), ((), ()))
    gap = lax.broadcasted_iota(jnp.int32, (BLOCK, BLOCK), 0) - lax.broadcasted_iota(
        jnp.int32, (BLOCK, BLOCK), 1
    )
    group_here = lax.div(u * heads_here, repeat_count)

    def tile_work(a):
        tile = b * tiles_here + a
        listed = [list_ref[group_here, l, tile] for l in range(list_count)]
        cands = [tile - 1, tile] + listed
        own_slot = tiles_here + a
        window_first = (b - 1) * tiles_here
        query_code = code_ref[pl.ds(own_slot, 1), :]
        query_lang = query_code & (LANGS - 1)
        slots = []
        biases = []
        for c, cand in enumerate(cands):
            usable = cand >= 0
            for other in cands[: c if c >= 2 else 0]:
                usable = usable & (cand != other)
            marked = cand == listed[0]
            for other in listed[1:]:
                marked = marked | (cand == other)
            if c < 2:
                slot = own_slot - 1 + c
            else:
                slot = jnp.clip(cand - window_first, 0, 2 * tiles_here - 1)
            limit = jnp.where(usable, (tile - cand) * BLOCK, -2 * BLOCK)
            seen_lang = jnp.where(marked, query_lang, -1)
            key_code = key_codes[slot]
            allowed = (gap <= limit) & (
                (key_code == query_code) | ((key_code & (LANGS - 1)) == seen_lang)
            )
            slots.append(slot)
            biases.append(jnp.where(allowed, 0.0, MASKED))

        def stacked(rows):
            return jnp.concatenate([rows[:, h * DH : (h + 1) * DH] for h in range(heads_here)], 0)

        bias = jnp.concatenate(biases, axis=0)
        bias = jnp.concatenate([bias] * heads_here, axis=1)
        key_part = jnp.concatenate([window[s, 0] for s in slots], axis=0)
        value_part = jnp.concatenate([window[s, 1] for s in slots], axis=0)
        query_part = stacked(q_all[a])
        dout_part = stacked(do_all[a])
        delta_tile = dl_all[a]
        delta = jnp.concatenate([delta_tile[h : h + 1, :] for h in range(heads_here)], axis=1)
        scores = lax.dot_general(key_part, query_part, across, preferred_element_type=f32)
        scores = scores * scaling + bias
        top = jnp.max(scores, axis=0, keepdims=True)
        raised = jnp.exp(scores - top)
        weights = raised * (1.0 / jnp.sum(raised, axis=0, keepdims=True))
        grad_weights = lax.dot_general(value_part, dout_part, across, preferred_element_type=f32)
        grad_scores = (weights * (grad_weights - delta)).astype(jnp.bfloat16)
        grad_query = scaling * lax.dot_general(
            grad_scores, key_part, (((0,), (0,)), ((), ())), preferred_element_type=f32
        )
        for h in range(heads_here):
            dq_all[a, :, h * DH : (h + 1) * DH] = grad_query[h * BLOCK : (h + 1) * BLOCK].astype(
                dq_all.dtype
            )
        grad_key = scaling * jnp.dot(grad_scores, query_part, preferred_element_type=f32)
        grad_value = jnp.dot(weights.astype(jnp.bfloat16), dout_part, preferred_element_type=f32)
        parts = (grad_key, grad_value)
        for c in range(2):
            for k in range(2):
                acc[slots[c], k] += parts[k][c * BLOCK : (c + 1) * BLOCK]

        def spread(t):
            for k in range(2):
                more = acc[t, k]
                for c in range(2, 2 + list_count):
                    piece = parts[k][c * BLOCK : (c + 1) * BLOCK]
                    more = more + jnp.where(slots[c] == t, piece, 0.0)
                acc[t, k] = more

        each(0, 2 * tiles_here, spread)

    tile_work(u)
    out_own(2).start()

    def step(s):
        @pl.when(s + LOOK < n_uly)
        def _():
            send_rows(s + LOOK)

        inward(2, s).wait_recv()
        inward(3, s).wait_recv()
        inward(4, s).wait_recv()
        tile_work(peer_of(s))
        outward(2, s).start()

    each(1, n_uly, step)

    @pl.when(has_prev)
    def _():
        def give_back(s):
            a = peer_of(s)
            back[a] = acc[a].astype(back.dtype)
            backward(a).start()

        each(0, n_uly, give_back)

    def settle(s):
        a = peer_of(s)

        @pl.when(has_next)
        def _():
            backward(a).wait_recv()
            total[a] = (acc[tiles_here + a] + returned[a].astype(f32)).astype(total.dtype)

        @pl.when(b == n_blk - 1)
        def _():
            total[a] = acc[tiles_here + a].astype(total.dtype)

    settle(0)
    out_own(0).start()
    out_own(1).start()

    def settle_and_send(s):
        settle(s)
        outward(0, s).start()
        outward(1, s).start()

    each(1, n_uly, settle_and_send)

    for kind in range(3):
        out_own(kind).wait()

    def finish(s):
        for kind in range(3):
            outward(kind, s).wait_recv()
        for kind in range(5):
            inward(kind, s).wait_send()
        for kind in range(3):
            outward(kind, s).wait_send()

    each(1, n_uly, finish)

    @pl.when(has_next)
    def _():
        each(0, n_uly, lambda a: forward(a).wait_send())

    @pl.when(has_prev)
    def _():
        each(0, n_uly, lambda a: backward(a).wait_send())

    if not direct:
        for kind, out in ((0, dk_ref), (1, dv_ref)):
            for g in range(n_uly // copies):
                summed = landing[kind, g * copies].astype(f32)
                for r in range(1, copies):
                    summed = summed + landing[kind, g * copies + r].astype(f32)
                out[:, g * DH : (g + 1) * DH] = summed.astype(out.dtype)


def split_kernel(
    n_blk,
    list_count,
    list_hbm,
    lang_hbm,
    docs_hbm,
    q_ref,
    do_ref,
    k_ref,
    v_ref,
    dl_ref,
    dq_ref,
    dk_ref,
    dv_ref,
    q_all,
    do_all,
    dl_all,
    window_row,
    window_column,
    list_ref,
    lang_ref,
    order_ref,
    same_ref,
    place_ref,
    code_ref,
    key_codes,
    acc,
    entries,
    sums,
    scores_held,
    dq_all,
    back,
    returned,
    across_out,
    across_in,
    total,
    in_send,
    in_recv,
    local_sem,
    far_send,
    far_recv,
    relay_send,
    relay_recv,
    z_send,
    z_recv,
    back_send,
    back_recv,
    across_send,
    across_recv,
    out_send,
    out_recv,
    out_local,
    table_sem,
    gate,
):
    b, u = lax.axis_index("blk"), lax.axis_index("uly")
    y, x, c = lax.div(u, 4), lax.rem(lax.div(u, 2), 2), lax.rem(u, 2)
    tiles_here = SPLIT
    width = HALF * DH
    f32 = jnp.float32
    windows = (window_row, window_column)
    has_next = b < n_blk - 1
    has_prev = b > 0

    def job_of(f, near):
        return lax.rem(f + c + near, 2)

    def member(j, s, far):
        along, near = lax.div(s, 2), lax.rem(s, 2)
        row = lax.rem(y + along * j + far * (1 - j), 2)
        column = lax.rem(x + along * (1 - j) + far * j, 2)
        return 4 * row + 2 * column + lax.rem(c + near, 2)

    def peer_of(f, s):
        return member(job_of(f, 0), s, 0)

    def far_of(f, s):
        return member(job_of(f, 0), s, 1)

    def position(j, s):
        return HALF * j + 2 * lax.rem(x * (1 - j) + y * j + lax.div(s, 2), 2) + lax.rem(c + lax.rem(s, 2), 2)

    def group_of(f):
        return position(job_of(f, 0), 0)

    def target_of(f, s):
        return member(job_of(f, lax.rem(s, 2)), s, 0)

    def pieces(f, s):
        group = position(job_of(f, lax.rem(s, 2)), s)
        kv_cols = aligned(group * DH, DH)
        q_cols = aligned(group * width, width)
        return (
            (k_ref.at[:, kv_cols], windows[f].at[tiles_here + u, 0]),
            (v_ref.at[:, kv_cols], windows[f].at[tiles_here + u, 1]),
            (dl_ref.at[group], dl_all.at[f, s]),
            (q_ref.at[:, q_cols], q_all.at[f, s]),
            (do_ref.at[:, q_cols], do_all.at[f, s]),
        )

    def out_pieces(f, s):
        group = group_of(f)
        kv_cols = aligned(group * DH, DH)
        return (
            (total.at[f, s, 0], dk_ref.at[:, kv_cols]),
            (total.at[f, s, 1], dv_ref.at[:, kv_cols]),
            (dq_all.at[f, s], dq_ref.at[:, aligned(group * width, width)]),
        )

    def remote(src, dst, send, recv, device):
        return pltpu.make_async_remote_copy(
            src_ref=src, dst_ref=dst, send_sem=send, recv_sem=recv, device_id=device, device_id_type=MESH
        )

    def inward(j, kind, s):
        src, dst = pieces(j, s)[kind]
        return remote(src, dst, in_send.at[j, kind, s], in_recv.at[j, kind, s], (b, target_of(j, s)))

    def direct(kind, s):
        src, dst = pieces(0, s)[kind]
        return remote(
            src, dst, far_send.at[kind, s], far_recv.at[kind, s], (b, member(job_of(0, lax.rem(s, 2)), s, 1))
        )

    def outward(j, kind, s):
        src, dst = out_pieces(j, s)[kind]
        return remote(src, dst, out_send.at[j, kind, s], out_recv.at[j, kind, s], (b, peer_of(j, s)))

    def local(j, kind):
        src, dst = pieces(j, 0)[kind]
        return pltpu.make_async_copy(src, dst, local_sem.at[j, kind])

    def out_own(j, kind):
        src, dst = out_pieces(j, 0)[kind]
        return pltpu.make_async_copy(src, dst, out_local.at[j, kind])

    def relay(s):
        held = windows[1].at[tiles_here + peer_of(1, s)]
        return remote(held, held, relay_send.at[s], relay_recv.at[s], (b, far_of(1, 0)))

    def forward(j, a):
        return remote(
            windows[j].at[tiles_here + a],
            windows[j].at[a],
            z_send.at[j, a],
            z_recv.at[j, a],
            (lax.rem(b + 1, n_blk), u),
        )

    def backward(j, a):
        return remote(
            back.at[j, a],
            returned.at[j, a],
            back_send.at[j, a],
            back_recv.at[j, a],
            (lax.rem(b + n_blk - 1, n_blk), u),
        )

    def over(j, s):
        return remote(
            across_out.at[j, s],
            across_in.at[j, s],
            across_send.at[j, s],
            across_recv.at[j, s],
            (b, far_of(j, 0)),
        )

    def each(first, last, body):
        lax.fori_loop(first, last, lambda s, _: (body(s), 0)[1], 0)

    def last_first(body):
        each(0, HALF, lambda n: body(HALF - 1 - n))

    def send_on(j, a):
        @pl.when(has_next)
        def _():
            forward(j, a).start()

    tables = (
        pltpu.make_async_copy(list_hbm, list_ref, table_sem.at[0]),
        pltpu.make_async_copy(lang_hbm, lang_ref, table_sem.at[1]),
        pltpu.make_async_copy(
            docs_hbm.at[aligned(jnp.maximum(b - 1, 0) * tiles_here, tiles_here), :],
            code_ref.at[pl.ds(0, tiles_here), :],
            table_sem.at[2],
        ),
        pltpu.make_async_copy(
            docs_hbm.at[aligned(b * tiles_here, tiles_here), :],
            code_ref.at[pl.ds(tiles_here, tiles_here), :],
            table_sem.at[3],
        ),
    )
    for j in range(2):
        for kind in range(5):
            local(j, kind).start()
    for table in tables:
        table.start()

    barrier = pltpu.get_barrier_semaphore()
    friends = [member(0, s, far) for far in range(2) for s in range(HALF) if s + far > 0]
    for friend in friends:
        pl.semaphore_signal(barrier, inc=1, device_id=(b, friend), device_id_type=MESH)

    @pl.when(has_prev)
    def _():
        pl.semaphore_signal(barrier, inc=1, device_id=(b - 1, u), device_id_type=MESH)

    @pl.when(has_next)
    def _():
        pl.semaphore_signal(barrier, inc=1, device_id=(b + 1, u), device_id_type=MESH)

    ends = jnp.where(has_prev, 1, 0) + jnp.where(has_next, 1, 0)
    pl.semaphore_wait(barrier, len(friends) + ends)

    def start_keys(j):
        def body(s):
            inward(j, 0, s).start()
            inward(j, 1, s).start()

        each(1, HALF, body)

    def start_rows(j):
        def body(s):
            for kind in (2, 3, 4):
                inward(j, kind, s).start()

        each(1, HALF, body)

    def start_rows_of(j, core):
        def body(n):
            s = lax.rem(c + core, 2) + 2 * n

            @pl.when(s > 0)
            def _():
                for kind in (2, 3, 4):
                    inward(j, kind, s).start()

        each(0, 2, body)

    def keys_here(j, s):
        inward(j, 0, s).wait_recv()
        inward(j, 1, s).wait_recv()

    def drained(j):
        @pl.when(has_next)
        def _():
            each(0, HALF, lambda s: forward(j, peer_of(j, s)).wait_send())
            each(0, HALF - SLACK, lambda s: forward(j, far_of(j, s)).wait_send())

    def let_go(n):
        pl.semaphore_signal(gate.at[n], inc=1, device_id=(b, member(0, 1, 0)), device_id_type=MESH)

    def start_far(s):
        direct(0, s).start()
        direct(1, s).start()

    def pass_near(s):
        keys_here(0, s)

        @pl.when(c == 0)
        def _():
            send_on(0, peer_of(0, s))

    def pass_far(s):
        direct(0, s).wait_recv()
        direct(1, s).wait_recv()

        @pl.when(c == 0)
        def _():
            send_on(0, far_of(0, s))

    start_keys(0)
    each(0, HALF, start_far)
    start_keys(1)
    start_rows_of(0, 0)
    local(0, 0).wait()
    local(0, 1).wait()

    send_on(0, u)
    keys_here(0, 1)
    send_on(0, peer_of(0, 1))

    for table in tables:
        table.wait()
    docs = code_ref[...]

    def look_up(d, lang):
        return lang + jnp.where(docs == d, lang_ref[d], 0)

    lang = lax.fori_loop(0, lang_ref.shape[0], look_up, jnp.zeros_like(docs))
    code_ref[...] = docs * LANGS + lang

    window_first = (b - 1) * tiles_here

    def slot_of(cand):
        return jnp.clip(cand - window_first, 0, 2 * tiles_here - 1)

    def plan(j):
        group = group_of(j)
        count = HALF * list_count
        slots = [
            slot_of(list_ref[group, l, b * tiles_here + peer_of(j, s)]) for s in range(HALF) for l in range(list_count)
        ]
        ranks = []
        for e in range(count):
            rank = 0
            for other in range(count):
                if other < e:
                    rank = rank + jnp.where(slots[other] <= slots[e], 1, 0)
                elif other > e:
                    rank = rank + jnp.where(slots[other] < slots[e], 1, 0)
            ranks.append(rank)
        before = -1
        for i in range(count):
            entry, slot = 0, 0
            for e in range(count):
                entry = entry + jnp.where(ranks[e] == i, e, 0)
                slot = slot + jnp.where(ranks[e] == i, slots[e], 0)
            order_ref[j, i] = entry
            same_ref[j, i] = jnp.where(slot == before, 1, 0)
            before = slot
        for t in range(2 * tiles_here):
            upto, here = 0, 0
            for slot in slots:
                upto = upto + jnp.where(slot <= t, 1, 0)
                here = here + jnp.where(slot == t, 1, 0)
            place_ref[j, t] = jnp.where(here > 0, upto - 1, count)

    def prepare(t):
        key_codes[t] = jnp.broadcast_to(code_ref[pl.ds(t, 1), :], (BLOCK, BLOCK)).T
        acc[0, t] = jnp.zeros(acc.shape[2:], f32)
        acc[1, t] = jnp.zeros(acc.shape[2:], f32)

    each(0, 2 * tiles_here, prepare)
    for j in range(2):
        plan(j)
        sums[j, HALF * list_count] = jnp.zeros(sums.shape[2:], f32)

    @pl.when(b == 0)
    def _():
        for window in windows:
            window[0:tiles_here] = jnp.zeros((tiles_here,) + window.shape[1:], window.dtype)

    scaling = float(DH) ** (-0.5)
    across = (((1,), (1,)), ((), ()))
    gap = lax.broadcasted_iota(jnp.int32, (BLOCK, BLOCK), 0) - lax.broadcasted_iota(
        jnp.int32, (BLOCK, BLOCK), 1
    )

    def query_work(j, s, grad_scores, key_part):
        grad_query = scaling * lax.dot_general(
            key_part, grad_scores, (((0,), (0,)), ((), ())), preferred_element_type=f32
        )
        for h in range(HALF):
            turned = grad_query[:, h * BLOCK : (h + 1) * BLOCK].T
            dq_all[j, s, :, h * DH : (h + 1) * DH] = turned.astype(dq_all.dtype)

    def tile_work(j, s):
        group = group_of(j)
        place = peer_of(j, s)
        tile = b * tiles_here + place
        listed = [list_ref[group, l, tile] for l in range(list_count)]
        cands = [tile - 1, tile] + listed
        own_slot = tiles_here + place
        query_code = code_ref[pl.ds(own_slot, 1), :]
        query_lang = query_code & (LANGS - 1)
        slots = []
        biases = []
        for n, cand in enumerate(cands):
            usable = cand >= 0
            for other in cands[: n if n >= 2 else 0]:
                usable = usable & (cand != other)
            marked = cand == listed[0]
            for other in listed[1:]:
                marked = marked | (cand == other)
            slot = own_slot - 1 + n if n < 2 else slot_of(cand)
            limit = jnp.where(usable, (tile - cand) * BLOCK, -2 * BLOCK)
            seen_lang = jnp.where(marked, query_lang, -1)
            key_code = key_codes[slot]
            allowed = (gap <= limit) & (
                (key_code == query_code) | ((key_code & (LANGS - 1)) == seen_lang)
            )
            slots.append(slot)
            biases.append(jnp.where(allowed, 0.0, MASKED))

        def stacked(rows):
            return jnp.concatenate([rows[:, h * DH : (h + 1) * DH] for h in range(HALF)], 0)

        bias = jnp.concatenate(biases, axis=0)
        bias = jnp.concatenate([bias] * HALF, axis=1)
        key_part = jnp.concatenate([windows[j][t, 0] for t in slots], axis=0)
        value_part = jnp.concatenate([windows[j][t, 1] for t in slots], axis=0)
        query_part = stacked(q_all[j, s])
        dout_part = stacked(do_all[j, s])
        delta_tile = dl_all[j, s]
        delta = jnp.concatenate([delta_tile[h : h + 1, :] for h in range(HALF)], axis=1)
        scores = lax.dot_general(key_part, query_part, across, preferred_element_type=f32)
        scores = scores * (scaling * LOG2_E) + bias
        top = jnp.max(scores, axis=0, keepdims=True)
        raised = jnp.exp2(scores - top)
        weights = raised * (1.0 / jnp.sum(raised, axis=0, keepdims=True))
        grad_weights = lax.dot_general(value_part, dout_part, across, preferred_element_type=f32)
        grad_scores = (weights * (grad_weights - delta)).astype(jnp.bfloat16)
        if j == 1:
            scores_held[s] = grad_scores
        else:
            query_work(j, s, grad_scores, key_part)
        grad_key = scaling * jnp.dot(grad_scores, query_part, preferred_element_type=f32)
        grad_value = jnp.dot(weights.astype(jnp.bfloat16), dout_part, preferred_element_type=f32)
        for k, part in ((0, grad_key), (1, grad_value)):
            for n in range(2):
                acc[j, slots[n], k] += part[n * BLOCK : (n + 1) * BLOCK]
            for l in range(list_count):
                first = (2 + l) * BLOCK
                entries[s * list_count + l, k] = part[first : first + BLOCK]

    def add_listed(j):
        sums[j, 0] = entries[order_ref[j, 0]]

        def body(i):
            earlier = jnp.where(same_ref[j, i] == 1, sums[j, i - 1], 0.0)
            sums[j, i] = entries[order_ref[j, i]] + earlier

        each(1, HALF * list_count, body)

    def slot_sum(j, t):
        return acc[j, t] + sums[j, place_ref[j, t]]

    def arrived(j):
        @pl.when(has_prev)
        def _():
            each(0, tiles_here, lambda a: forward(j, a).wait_recv())

    def give_back(j):
        add_listed(j)

        @pl.when(has_prev)
        def _():
            def body(a):
                back[j, a] = slot_sum(j, a).astype(back.dtype)
                backward(j, a).start()

            last_first(lambda s: body(far_of(j, s)))
            last_first(lambda s: body(peer_of(j, s)))

    def send_queries(j, s):
        @pl.when(s > 0)
        def _():
            outward(j, 2, s).start()

        @pl.when(s == 0)
        def _():
            out_own(j, 2).start()

    def late_queries(s):
        place = tiles_here + peer_of(1, s)
        slots = [place - 1, place] + [
            slot_of(list_ref[group_of(1), l, b * tiles_here + peer_of(1, s)]) for l in range(list_count)
        ]
        query_work(1, s, scores_held[s], jnp.concatenate([windows[1][t, 0] for t in slots], axis=0))
        send_queries(1, s)

    def work(j, s):
        @pl.when(s > 0)
        def _():
            for kind in (2, 3, 4):
                inward(j, kind, s).wait_recv()

        tile_work(j, s)

        if j == 0:
            send_queries(j, s)

    def with_returned(j, a, then):
        @pl.when(has_next)
        def _():
            backward(j, a).wait_recv()
            then(slot_sum(j, tiles_here + a) + returned[j, a].astype(f32))

        @pl.when(b == n_blk - 1)
        def _():
            then(slot_sum(j, tiles_here + a))

    def settle_far(j, s):
        def then(value):
            across_out[j, s] = value.astype(across_out.dtype)

        with_returned(j, far_of(j, s), then)
        over(j, s).start()

    def settle(j, s):
        over(j, s).wait_recv()

        def then(value):
            total[j, s] = (value + across_in[j, s].astype(f32)).astype(total.dtype)

        with_returned(j, peer_of(j, s), then)

        @pl.when(s > 0)
        def _():
            outward(j, 0, s).start()
            outward(j, 1, s).start()

        @pl.when(s == 0)
        def _():
            out_own(j, 0).start()
            out_own(j, 1).start()

    each(2, HALF, pass_near)
    each(0, HALF, pass_far)
    local(1, 0).wait()
    local(1, 1).wait()
    relay(0).start()

    def relay_keys(s):
        keys_here(1, s)
        relay(s).start()

    each(1, HALF, relay_keys)
    start_rows_of(0, 1)
    start_rows(1)

    @pl.when(c == 1)
    def _():
        pl.semaphore_wait(gate.at[0], 1)
        each(2, HALF, lambda s: send_on(0, peer_of(0, s)))
        each(0, HALF, lambda s: send_on(0, far_of(0, s)))
        drained(0)
        let_go(1)

    @pl.when(c == 0)
    def _():
        drained(0)
        let_go(0)

    arrived(0)
    for kind in (2, 3, 4):
        local(0, kind).wait()

    def first_step(s):
        work(0, s)

    each(0, HALF, first_step)
    give_back(0)

    @pl.when(c == 0)
    def _():
        pl.semaphore_wait(gate.at[1], 1)

    @pl.when(c == 1)
    def _():
        pl.semaphore_wait(gate.at[2], 1)

    each(0, HALF, lambda s: send_on(1, peer_of(1, s)))

    def pass_far_second(s):
        relay(s).wait_recv()
        send_on(1, far_of(1, s))

    each(0, HALF, pass_far_second)

    @pl.when(c == 0)
    def _():
        drained(1)
        let_go(2)

    last_first(lambda s: settle_far(0, s))
    arrived(1)
    for kind in (2, 3, 4):
        local(1, kind).wait()

    last_first(lambda s: work(1, s))
    give_back(1)
    last_first(lambda s: settle(0, s))
    last_first(late_queries)
    last_first(lambda s: settle_far(1, s))
    last_first(lambda s: settle(1, s))

    for j in range(2):
        for kind in range(3):
            out_own(j, kind).wait()

        def finish(s):
            for kind in range(3):
                outward(j, kind, s).wait_recv()
            for kind in range(5):
                inward(j, kind, s).wait_send()
            for kind in range(3):
                outward(j, kind, s).wait_send()

        each(1, HALF, finish)

        def finish_far(s):
            over(j, s).wait_send()
            if j == 0:
                direct(0, s).wait_send()
                direct(1, s).wait_send()
            else:
                relay(s).wait_send()

        each(0, HALF, finish_far)

        @pl.when(has_next)
        def _():
            if j == 0:
                each(HALF - SLACK, HALF, lambda s: forward(j, far_of(j, s)).wait_send())
            else:

                @pl.when(c == 0)
                def _():
                    each(HALF - SLACK, HALF, lambda s: forward(j, far_of(j, s)).wait_send())

                @pl.when(c == 1)
                def _():
                    each(0, tiles_here, lambda a: forward(j, a).wait_send())

        @pl.when(has_prev)
        def _():
            each(0, tiles_here, lambda a: backward(j, a).wait_send())


def split_grads(lists, doc_lang, docs, queries, grad_out, keys, values, delta_rows, n_blk):
    list_count = lists.shape[1]
    width = HALF * DH
    anywhere = pl.BlockSpec(memory_space=pl.ANY)
    bf16, f32 = jnp.bfloat16, jnp.float32
    pair = (2, BLOCK, DH)
    dma = pltpu.SemaphoreType.DMA
    entry_count = HALF * list_count
    return pl.pallas_call(
        functools.partial(split_kernel, n_blk, list_count),
        out_shape=(
            jax.ShapeDtypeStruct(queries.shape, bf16),
            jax.ShapeDtypeStruct(keys.shape, bf16),
            jax.ShapeDtypeStruct(values.shape, bf16),
        ),
        in_specs=[anywhere] * 8,
        out_specs=(anywhere,) * 3,
        scratch_shapes=[
            pltpu.VMEM((2, HALF, BLOCK, width), bf16),
            pltpu.VMEM((2, HALF, BLOCK, width), bf16),
            pltpu.VMEM((2, HALF, HALF, BLOCK), f32),
            pltpu.VMEM((2 * SPLIT,) + pair, bf16),
            pltpu.VMEM((2 * SPLIT,) + pair, bf16),
            pltpu.SMEM(lists.shape, jnp.int32),
            pltpu.SMEM(doc_lang.shape, jnp.int32),
            pltpu.SMEM((2, entry_count), jnp.int32),
            pltpu.SMEM((2, entry_count), jnp.int32),
            pltpu.SMEM((2, 2 * SPLIT), jnp.int32),
            pltpu.VMEM((2 * SPLIT, BLOCK), jnp.int32),
            pltpu.VMEM((2 * SPLIT, BLOCK, BLOCK), jnp.int32),
            pltpu.VMEM((2, 2 * SPLIT) + pair, f32),
            pltpu.VMEM((entry_count,) + pair, f32),
            pltpu.VMEM((2, entry_count + 1) + pair, f32),
            pltpu.VMEM((HALF, (2 + list_count) * BLOCK, width), bf16),
            pltpu.VMEM((2, HALF, BLOCK, width), bf16),
            pltpu.VMEM((2, SPLIT) + pair, bf16),
            pltpu.VMEM((2, SPLIT) + pair, bf16),
            pltpu.VMEM((2, HALF) + pair, bf16),
            pltpu.VMEM((2, HALF) + pair, bf16),
            pltpu.VMEM((2, HALF) + pair, bf16),
            dma((2, 5, HALF)),
            dma((2, 5, HALF)),
            dma((2, 5)),
            dma((2, HALF)),
            dma((2, HALF)),
            dma((HALF,)),
            dma((HALF,)),
            dma((2, SPLIT)),
            dma((2, SPLIT)),
            dma((2, SPLIT)),
            dma((2, SPLIT)),
            dma((2, HALF)),
            dma((2, HALF)),
            dma((2, 3, HALF)),
            dma((2, 3, HALF)),
            dma((2, 3)),
            dma((4,)),
            pltpu.SemaphoreType.REGULAR((3,)),
        ],
        compiler_params=pltpu.CompilerParams(
            collective_id=0, has_side_effects=True, vmem_limit_bytes=VMEM_LIMIT
        ),
        name="split_grads",
    )(lists, doc_lang, docs, queries, grad_out, keys, values, delta_rows)


def hand_over_kernel(*refs):
    count = (len(refs) - 2) // 3
    in_sem, out_sem = refs[-2:]
    moves = []
    for k in range(count):
        src, dst, held = refs[k], refs[count + k], refs[2 * count + k]
        part = src.shape[0] // CHUNKS
        for c in range(CHUNKS):
            rows = pl.ds(c * part, part)
            moves.append(
                (
                    pltpu.make_async_copy(src.at[rows, :], held.at[rows, :], in_sem.at[k, c]),
                    pltpu.make_async_copy(held.at[rows, :], dst.at[rows, :], out_sem.at[k, c]),
                )
            )
    for fetch, _ in moves:
        fetch.start()
    for fetch, store in moves:
        fetch.wait()
        store.start()
    for _, store in moves:
        store.wait()


def handed_over(arrays):
    anywhere = pl.BlockSpec(memory_space=pl.ANY)
    count = len(arrays)
    return pl.pallas_call(
        hand_over_kernel,
        out_shape=tuple(jax.ShapeDtypeStruct(x.shape, x.dtype) for x in arrays),
        in_specs=[anywhere] * count,
        out_specs=(anywhere,) * count,
        scratch_shapes=[pltpu.VMEM(x.shape, x.dtype) for x in arrays]
        + [pltpu.SemaphoreType.DMA((count, CHUNKS)), pltpu.SemaphoreType.DMA((count, CHUNKS))],
        name="hand_over",
    )(*arrays)


def shards(queries, keys, values, grad_out, row_delta, doc_ids, doc_lang, tile_list):
    tok_count, full_width = queries.shape
    heads_all = full_width // DH
    groups_all = keys.shape[1] // DH
    repeat_count = heads_all // groups_all
    n_uly = lax.axis_size("uly")
    n_blk = lax.axis_size("blk")
    heads_here = heads_all // n_uly
    width = heads_here * DH
    copies = repeat_count // heads_here
    lists = tile_list.transpose(0, 2, 1)
    docs = doc_ids.reshape(-1, BLOCK)
    delta_rows = row_delta.T.reshape(n_uly, heads_here, tok_count)
    if n_uly == SPLIT and groups_all == SPLIT and repeat_count == HALF and tok_count == BLOCK:
        return handed_over(
            split_grads(lists, doc_lang, docs, queries, grad_out, keys, values, delta_rows, n_blk)
        )
    anywhere = pl.BlockSpec(memory_space=pl.ANY)
    in_vmem = pl.BlockSpec(memory_space=pltpu.VMEM)
    kv_spec = in_vmem if copies > 1 else anywhere
    bf16, f32 = jnp.bfloat16, jnp.float32
    pair = (2, BLOCK, DH)
    dma = pltpu.SemaphoreType.DMA
    outs = pl.pallas_call(
        functools.partial(
            fused_kernel,
            n_blk,
            n_uly,
            tile_list.shape[2],
            heads_here,
            repeat_count,
        ),
        out_shape=(
            jax.ShapeDtypeStruct(queries.shape, bf16),
            jax.ShapeDtypeStruct(keys.shape, bf16),
            jax.ShapeDtypeStruct(values.shape, bf16),
        ),
        in_specs=[anywhere] * 8,
        out_specs=(anywhere, kv_spec, kv_spec),
        scratch_shapes=[
            pltpu.VMEM((n_uly, BLOCK, width), bf16),
            pltpu.VMEM((n_uly, BLOCK, width), bf16),
            pltpu.VMEM((n_uly, heads_here, BLOCK), f32),
            pltpu.VMEM((2 * n_uly,) + pair, bf16),
            pltpu.SMEM(lists.shape, jnp.int32),
            pltpu.SMEM(doc_lang.shape, jnp.int32),
            pltpu.VMEM((2 * n_uly, BLOCK), jnp.int32),
            pltpu.VMEM((2 * n_uly, BLOCK, BLOCK), jnp.int32),
            pltpu.VMEM((2 * n_uly,) + pair, f32),
            pltpu.VMEM((n_uly, BLOCK, width), bf16),
            pltpu.VMEM((n_uly,) + pair, bf16),
            pltpu.VMEM((n_uly,) + pair, bf16),
            pltpu.VMEM((n_uly,) + pair, bf16),
            pltpu.VMEM((2, n_uly if copies > 1 else 1, BLOCK, DH), bf16),
            dma((5, n_uly)),
            dma((5, n_uly)),
            dma((5,)),
            dma((n_uly,)),
            dma((n_uly,)),
            dma((n_uly,)),
            dma((n_uly,)),
            dma((3, n_uly)),
            dma((3, n_uly)),
            dma((3,)),
            dma((4,)),
        ],
        compiler_params=pltpu.CompilerParams(
            collective_id=0, has_side_effects=True, vmem_limit_bytes=VMEM_LIMIT
        ),
        name="attention_grads",
    )(lists, doc_lang, docs, queries, grad_out, keys, values, delta_rows)
    return handed_over(outs)


def solution(mesh):
    placed = (
        P(("blk", "uly"), None),
        P(("blk", "uly"), None),
        P(("blk", "uly"), None),
        P(("blk", "uly"), None),
        P(("blk", "uly"), None),
        P(),
        P(),
        P(),
    )
    return jax.shard_map(
        shards,
        mesh=mesh,
        in_specs=placed,
        out_specs=(P(("blk", "uly"), None), P(("blk", "uly"), None), P(("blk", "uly"), None)),
        check_vma=False,
    )
```

```python
import functools

import jax
import jax.numpy as jnp
from jax import lax
from jax.experimental import pallas as pl
from jax.experimental.pallas import tpu as pltpu
from jax.sharding import PartitionSpec as P

DH = 128
BLOCK = 128
LANGS = 4
MASKED = -1e30
MESH = pl.DeviceIdType.MESH
LOOK = 7
CHUNKS = 2
SPLIT = 8
HALF = 4
SLACK = 1
LOG2_E = 1.4426950408889634
VMEM_LIMIT = 56 * 1024 * 1024


def greet(b, u, n_blk, n_uly):
    barrier = pltpu.get_barrier_semaphore()
    for p in range(1, n_uly):
        pl.semaphore_signal(
            barrier, inc=1, device_id=(b, lax.rem(u + p, n_uly)), device_id_type=MESH
        )

    @pl.when(b > 0)
    def _():
        pl.semaphore_signal(barrier, inc=1, device_id=(b - 1, u), device_id_type=MESH)

    @pl.when(b < n_blk - 1)
    def _():
        pl.semaphore_signal(barrier, inc=1, device_id=(b + 1, u), device_id_type=MESH)

    ends = jnp.where(b > 0, 1, 0) + jnp.where(b < n_blk - 1, 1, 0)
    pl.semaphore_wait(barrier, n_uly - 1 + ends)


def aligned(start, size):
    return pl.ds(pl.multiple_of(start, size), size)


def partner(u, s, n):
    found, bit = 0, 1
    while bit < n:
        found = found + bit * lax.rem(lax.div(u, bit) + lax.div(s, bit), 2)
        bit *= 2
    return found


def fused_kernel(
    n_blk,
    n_uly,
    list_count,
    heads_here,
    repeat_count,
    list_hbm,
    lang_hbm,
    docs_hbm,
    q_ref,
    do_ref,
    k_ref,
    v_ref,
    dl_ref,
    dq_ref,
    dk_ref,
    dv_ref,
    q_all,
    do_all,
    dl_all,
    window,
    list_ref,
    lang_ref,
    code_ref,
    key_codes,
    acc,
    dq_all,
    back,
    returned,
    total,
    landing,
    in_send,
    in_recv,
    local_sem,
    z_send,
    z_recv,
    back_send,
    back_recv,
    out_send,
    out_recv,
    out_local,
    table_sem,
):
    b, u = lax.axis_index("blk"), lax.axis_index("uly")
    tiles_here = n_uly
    width = heads_here * DH
    copies = repeat_count // heads_here
    direct = copies == 1
    f32 = jnp.float32
    my_cols = aligned(u * width, width)
    my_group = aligned(u * DH, DH)
    peer_of = functools.partial(partner, u, n=n_uly)

    def pieces(peer):
        group = lax.div(peer * heads_here, repeat_count)
        kv_cols = aligned(group * DH, DH)
        q_cols = aligned(peer * width, width)
        return (
            (k_ref.at[:, kv_cols], window.at[tiles_here + u, 0]),
            (v_ref.at[:, kv_cols], window.at[tiles_here + u, 1]),
            (dl_ref.at[peer], dl_all.at[u]),
            (q_ref.at[:, q_cols], q_all.at[u]),
            (do_ref.at[:, q_cols], do_all.at[u]),
        )

    def out_pieces(peer):
        if direct:
            ends = (dk_ref.at[:, my_group], dv_ref.at[:, my_group])
        else:
            ends = (landing.at[0, u], landing.at[1, u])
        return (
            (total.at[peer, 0], ends[0]),
            (total.at[peer, 1], ends[1]),
            (dq_all.at[peer], dq_ref.at[:, my_cols]),
        )

    def remote(parts, kind, s, send, recv):
        peer = peer_of(s)
        src, dst = parts(peer)[kind]
        return pltpu.make_async_remote_copy(
            src_ref=src,
            dst_ref=dst,
            send_sem=send.at[kind, s],
            recv_sem=recv.at[kind, s],
            device_id=(b, peer),
            device_id_type=MESH,
        )

    def inward(kind, s):
        return remote(pieces, kind, s, in_send, in_recv)

    def outward(kind, s):
        return remote(out_pieces, kind, s, out_send, out_recv)

    def local(kind):
        src, dst = pieces(u)[kind]
        return pltpu.make_async_copy(src, dst, local_sem.at[kind])

    def out_own(kind):
        src, dst = out_pieces(u)[kind]
        return pltpu.make_async_copy(src, dst, out_local.at[kind])

    def forward(a):
        return pltpu.make_async_remote_copy(
            src_ref=window.at[tiles_here + a],
            dst_ref=window.at[a],
            send_sem=z_send.at[a],
            recv_sem=z_recv.at[a],
            device_id=(lax.rem(b + 1, n_blk), u),
            device_id_type=MESH,
        )

    def backward(a):
        return pltpu.make_async_remote_copy(
            src_ref=back.at[a],
            dst_ref=returned.at[a],
            send_sem=back_send.at[a],
            recv_sem=back_recv.at[a],
            device_id=(lax.rem(b + n_blk - 1, n_blk), u),
            device_id_type=MESH,
        )

    def each(first, last, body):
        lax.fori_loop(first, last, lambda s, _: (body(s), 0)[1], 0)

    has_next = b < n_blk - 1
    has_prev = b > 0

    tables = (
        pltpu.make_async_copy(list_hbm, list_ref, table_sem.at[0]),
        pltpu.make_async_copy(lang_hbm, lang_ref, table_sem.at[1]),
        pltpu.make_async_copy(
            docs_hbm.at[aligned(jnp.maximum(b - 1, 0) * tiles_here, tiles_here), :],
            code_ref.at[pl.ds(0, tiles_here), :],
            table_sem.at[2],
        ),
        pltpu.make_async_copy(
            docs_hbm.at[aligned(b * tiles_here, tiles_here), :],
            code_ref.at[pl.ds(tiles_here, tiles_here), :],
            table_sem.at[3],
        ),
    )
    for kind in range(5):
        local(kind).start()
    for table in tables:
        table.start()
    greet(b, u, n_blk, n_uly)

    def send_keys(s):
        inward(0, s).start()
        inward(1, s).start()

    def send_rows(s):
        inward(2, s).start()
        inward(3, s).start()
        inward(4, s).start()

    each(1, n_uly, send_keys)
    each(1, min(LOOK, n_uly - 1) + 1, send_rows)
    local(0).wait()
    local(1).wait()

    @pl.when(has_next)
    def _():
        forward(u).start()

    for table in tables:
        table.wait()
    docs = code_ref[...]

    def look_up(d, lang):
        return lang + jnp.where(docs == d, lang_ref[d], 0)

    lang = lax.fori_loop(0, lang_ref.shape[0], look_up, jnp.zeros_like(docs))
    code_ref[...] = docs * LANGS + lang

    def prepare(t):
        key_codes[t] = jnp.broadcast_to(code_ref[pl.ds(t, 1), :], (BLOCK, BLOCK)).T
        acc[t] = jnp.zeros(acc.shape[1:], f32)

    each(0, 2 * tiles_here, prepare)

    @pl.when(b == 0)
    def _():
        window[0:tiles_here] = jnp.zeros((tiles_here,) + window.shape[1:], window.dtype)

    def pass_on(s):
        inward(0, s).wait_recv()
        inward(1, s).wait_recv()

        @pl.when(has_next)
        def _():
            forward(peer_of(s)).start()

    each(1, n_uly, pass_on)

    @pl.when(has_prev)
    def _():
        each(0, tiles_here, lambda a: forward(a).wait_recv())

    local(2).wait()
    local(3).wait()
    local(4).wait()

    scaling = float(DH) ** (-0.5)
    across = (((1,), (1,)), ((), ()))
    gap = lax.broadcasted_iota(jnp.int32, (BLOCK, BLOCK), 0) - lax.broadcasted_iota(
        jnp.int32, (BLOCK, BLOCK), 1
    )
    group_here = lax.div(u * heads_here, repeat_count)

    def tile_work(a):
        tile = b * tiles_here + a
        listed = [list_ref[group_here, l, tile] for l in range(list_count)]
        cands = [tile - 1, tile] + listed
        own_slot = tiles_here + a
        window_first = (b - 1) * tiles_here
        query_code = code_ref[pl.ds(own_slot, 1), :]
        query_lang = query_code & (LANGS - 1)
        slots = []
        biases = []
        for c, cand in enumerate(cands):
            usable = cand >= 0
            for other in cands[: c if c >= 2 else 0]:
                usable = usable & (cand != other)
            marked = cand == listed[0]
            for other in listed[1:]:
                marked = marked | (cand == other)
            if c < 2:
                slot = own_slot - 1 + c
            else:
                slot = jnp.clip(cand - window_first, 0, 2 * tiles_here - 1)
            limit = jnp.where(usable, (tile - cand) * BLOCK, -2 * BLOCK)
            seen_lang = jnp.where(marked, query_lang, -1)
            key_code = key_codes[slot]
            allowed = (gap <= limit) & (
                (key_code == query_code) | ((key_code & (LANGS - 1)) == seen_lang)
            )
            slots.append(slot)
            biases.append(jnp.where(allowed, 0.0, MASKED))

        def stacked(rows):
            return jnp.concatenate([rows[:, h * DH : (h + 1) * DH] for h in range(heads_here)], 0)

        bias = jnp.concatenate(biases, axis=0)
        bias = jnp.concatenate([bias] * heads_here, axis=1)
        key_part = jnp.concatenate([window[s, 0] for s in slots], axis=0)
        value_part = jnp.concatenate([window[s, 1] for s in slots], axis=0)
        query_part = stacked(q_all[a])
        dout_part = stacked(do_all[a])
        delta_tile = dl_all[a]
        delta = jnp.concatenate([delta_tile[h : h + 1, :] for h in range(heads_here)], axis=1)
        scores = lax.dot_general(key_part, query_part, across, preferred_element_type=f32)
        scores = scores * scaling + bias
        top = jnp.max(scores, axis=0, keepdims=True)
        raised = jnp.exp(scores - top)
        weights = raised * (1.0 / jnp.sum(raised, axis=0, keepdims=True))
        grad_weights = lax.dot_general(value_part, dout_part, across, preferred_element_type=f32)
        grad_scores = (weights * (grad_weights - delta)).astype(jnp.bfloat16)
        grad_query = scaling * lax.dot_general(
            grad_scores, key_part, (((0,), (0,)), ((), ())), preferred_element_type=f32
        )
        for h in range(heads_here):
            dq_all[a, :, h * DH : (h + 1) * DH] = grad_query[h * BLOCK : (h + 1) * BLOCK].astype(
                dq_all.dtype
            )
        grad_key = scaling * jnp.dot(grad_scores, query_part, preferred_element_type=f32)
        grad_value = jnp.dot(weights.astype(jnp.bfloat16), dout_part, preferred_element_type=f32)
        parts = (grad_key, grad_value)
        for c in range(2):
            for k in range(2):
                acc[slots[c], k] += parts[k][c * BLOCK : (c + 1) * BLOCK]

        def spread(t):
            for k in range(2):
                more = acc[t, k]
                for c in range(2, 2 + list_count):
                    piece = parts[k][c * BLOCK : (c + 1) * BLOCK]
                    more = more + jnp.where(slots[c] == t, piece, 0.0)
                acc[t, k] = more

        each(0, 2 * tiles_here, spread)

    tile_work(u)
    out_own(2).start()

    def step(s):
        @pl.when(s + LOOK < n_uly)
        def _():
            send_rows(s + LOOK)

        inward(2, s).wait_recv()
        inward(3, s).wait_recv()
        inward(4, s).wait_recv()
        tile_work(peer_of(s))
        outward(2, s).start()

    each(1, n_uly, step)

    @pl.when(has_prev)
    def _():
        def give_back(s):
            a = peer_of(s)
            back[a] = acc[a].astype(back.dtype)
            backward(a).start()

        each(0, n_uly, give_back)

    def settle(s):
        a = peer_of(s)

        @pl.when(has_next)
        def _():
            backward(a).wait_recv()
            total[a] = (acc[tiles_here + a] + returned[a].astype(f32)).astype(total.dtype)

        @pl.when(b == n_blk - 1)
        def _():
            total[a] = acc[tiles_here + a].astype(total.dtype)

    settle(0)
    out_own(0).start()
    out_own(1).start()

    def settle_and_send(s):
        settle(s)
        outward(0, s).start()
        outward(1, s).start()

    each(1, n_uly, settle_and_send)

    for kind in range(3):
        out_own(kind).wait()

    def finish(s):
        for kind in range(3):
            outward(kind, s).wait_recv()
        for kind in range(5):
            inward(kind, s).wait_send()
        for kind in range(3):
            outward(kind, s).wait_send()

    each(1, n_uly, finish)

    @pl.when(has_next)
    def _():
        each(0, n_uly, lambda a: forward(a).wait_send())

    @pl.when(has_prev)
    def _():
        each(0, n_uly, lambda a: backward(a).wait_send())

    if not direct:
        for kind, out in ((0, dk_ref), (1, dv_ref)):
            for g in range(n_uly // copies):
                summed = landing[kind, g * copies].astype(f32)
                for r in range(1, copies):
                    summed = summed + landing[kind, g * copies + r].astype(f32)
                out[:, g * DH : (g + 1) * DH] = summed.astype(out.dtype)


def split_kernel(
    n_blk,
    list_count,
    list_hbm,
    lang_hbm,
    docs_hbm,
    q_ref,
    do_ref,
    k_ref,
    v_ref,
    dl_ref,
    dq_ref,
    dk_ref,
    dv_ref,
    q_all,
    do_all,
    dl_all,
    window_row,
    window_column,
    list_ref,
    lang_ref,
    order_ref,
    same_ref,
    place_ref,
    code_ref,
    key_codes,
    acc,
    entries,
    sums,
    scores_held,
    dq_all,
    back,
    returned,
    across_out,
    across_in,
    total,
    in_send,
    in_recv,
    local_sem,
    far_send,
    far_recv,
    relay_send,
    relay_recv,
    z_send,
    z_recv,
    back_send,
    back_recv,
    across_send,
    across_recv,
    out_send,
    out_recv,
    out_local,
    table_sem,
    gate,
):
    b, u = lax.axis_index("blk"), lax.axis_index("uly")
    y, x, c = lax.div(u, 4), lax.rem(lax.div(u, 2), 2), lax.rem(u, 2)
    tiles_here = SPLIT
    width = HALF * DH
    f32 = jnp.float32
    windows = (window_row, window_column)
    has_next = b < n_blk - 1
    has_prev = b > 0

    def job_of(f, near):
        return lax.rem(f + c + near, 2)

    def member(j, s, far):
        along, near = lax.div(s, 2), lax.rem(s, 2)
        row = lax.rem(y + along * j + far * (1 - j), 2)
        column = lax.rem(x + along * (1 - j) + far * j, 2)
        return 4 * row + 2 * column + lax.rem(c + near, 2)

    def peer_of(f, s):
        return member(job_of(f, 0), s, 0)

    def far_of(f, s):
        return member(job_of(f, 0), s, 1)

    def position(j, s):
        return HALF * j + 2 * lax.rem(x * (1 - j) + y * j + lax.div(s, 2), 2) + lax.rem(c + lax.rem(s, 2), 2)

    def group_of(f):
        return position(job_of(f, 0), 0)

    def target_of(f, s):
        return member(job_of(f, lax.rem(s, 2)), s, 0)

    def pieces(f, s):
        group = position(job_of(f, lax.rem(s, 2)), s)
        kv_cols = aligned(group * DH, DH)
        q_cols = aligned(group * width, width)
        return (
            (k_ref.at[:, kv_cols], windows[f].at[tiles_here + u, 0]),
            (v_ref.at[:, kv_cols], windows[f].at[tiles_here + u, 1]),
            (dl_ref.at[group], dl_all.at[f, s]),
            (q_ref.at[:, q_cols], q_all.at[f, s]),
            (do_ref.at[:, q_cols], do_all.at[f, s]),
        )

    def out_pieces(f, s):
        group = group_of(f)
        kv_cols = aligned(group * DH, DH)
        return (
            (total.at[f, s, 0], dk_ref.at[:, kv_cols]),
            (total.at[f, s, 1], dv_ref.at[:, kv_cols]),
            (dq_all.at[f, s], dq_ref.at[:, aligned(group * width, width)]),
        )

    def remote(src, dst, send, recv, device):
        return pltpu.make_async_remote_copy(
            src_ref=src, dst_ref=dst, send_sem=send, recv_sem=recv, device_id=device, device_id_type=MESH
        )

    def inward(j, kind, s):
        src, dst = pieces(j, s)[kind]
        return remote(src, dst, in_send.at[j, kind, s], in_recv.at[j, kind, s], (b, target_of(j, s)))

    def direct(kind, s):
        src, dst = pieces(0, s)[kind]
        return remote(
            src, dst, far_send.at[kind, s], far_recv.at[kind, s], (b, member(job_of(0, lax.rem(s, 2)), s, 1))
        )

    def outward(j, kind, s):
        src, dst = out_pieces(j, s)[kind]
        return remote(src, dst, out_send.at[j, kind, s], out_recv.at[j, kind, s], (b, peer_of(j, s)))

    def local(j, kind):
        src, dst = pieces(j, 0)[kind]
        return pltpu.make_async_copy(src, dst, local_sem.at[j, kind])

    def out_own(j, kind):
        src, dst = out_pieces(j, 0)[kind]
        return pltpu.make_async_copy(src, dst, out_local.at[j, kind])

    def relay(s):
        held = windows[1].at[tiles_here + peer_of(1, s)]
        return remote(held, held, relay_send.at[s], relay_recv.at[s], (b, far_of(1, 0)))

    def forward(j, a):
        return remote(
            windows[j].at[tiles_here + a],
            windows[j].at[a],
            z_send.at[j, a],
            z_recv.at[j, a],
            (lax.rem(b + 1, n_blk), u),
        )

    def backward(j, a):
        return remote(
            back.at[j, a],
            returned.at[j, a],
            back_send.at[j, a],
            back_recv.at[j, a],
            (lax.rem(b + n_blk - 1, n_blk), u),
        )

    def over(j, s):
        return remote(
            across_out.at[j, s],
            across_in.at[j, s],
            across_send.at[j, s],
            across_recv.at[j, s],
            (b, far_of(j, 0)),
        )

    def each(first, last, body):
        lax.fori_loop(first, last, lambda s, _: (body(s), 0)[1], 0)

    def last_first(body):
        each(0, HALF, lambda n: body(HALF - 1 - n))

    def send_on(j, a):
        @pl.when(has_next)
        def _():
            forward(j, a).start()

    tables = (
        pltpu.make_async_copy(list_hbm, list_ref, table_sem.at[0]),
        pltpu.make_async_copy(lang_hbm, lang_ref, table_sem.at[1]),
        pltpu.make_async_copy(
            docs_hbm.at[aligned(jnp.maximum(b - 1, 0) * tiles_here, tiles_here), :],
            code_ref.at[pl.ds(0, tiles_here), :],
            table_sem.at[2],
        ),
        pltpu.make_async_copy(
            docs_hbm.at[aligned(b * tiles_here, tiles_here), :],
            code_ref.at[pl.ds(tiles_here, tiles_here), :],
            table_sem.at[3],
        ),
    )
    for j in range(2):
        for kind in range(5):
            local(j, kind).start()
    for table in tables:
        table.start()

    barrier = pltpu.get_barrier_semaphore()
    friends = [member(0, s, far) for far in range(2) for s in range(HALF) if s + far > 0]
    for friend in friends:
        pl.semaphore_signal(barrier, inc=1, device_id=(b, friend), device_id_type=MESH)

    @pl.when(has_prev)
    def _():
        pl.semaphore_signal(barrier, inc=1, device_id=(b - 1, u), device_id_type=MESH)

    @pl.when(has_next)
    def _():
        pl.semaphore_signal(barrier, inc=1, device_id=(b + 1, u), device_id_type=MESH)

    ends = jnp.where(has_prev, 1, 0) + jnp.where(has_next, 1, 0)
    pl.semaphore_wait(barrier, len(friends) + ends)

    def start_keys(j):
        def body(s):
            inward(j, 0, s).start()
            inward(j, 1, s).start()

        each(1, HALF, body)

    def start_rows(j):
        def body(s):
            for kind in (2, 3, 4):
                inward(j, kind, s).start()

        each(1, HALF, body)

    def start_rows_of(j, core):
        def body(n):
            s = lax.rem(c + core, 2) + 2 * n

            @pl.when(s > 0)
            def _():
                for kind in (2, 3, 4):
                    inward(j, kind, s).start()

        each(0, 2, body)

    def keys_here(j, s):
        inward(j, 0, s).wait_recv()
        inward(j, 1, s).wait_recv()

    def drained(j):
        @pl.when(has_next)
        def _():
            each(0, HALF, lambda s: forward(j, peer_of(j, s)).wait_send())
            each(0, HALF - SLACK, lambda s: forward(j, far_of(j, s)).wait_send())

    def let_go(n):
        pl.semaphore_signal(gate.at[n], inc=1, device_id=(b, member(0, 1, 0)), device_id_type=MESH)

    def start_far(s):
        direct(0, s).start()
        direct(1, s).start()

    def pass_near(s):
        keys_here(0, s)

        @pl.when(c == 0)
        def _():
            send_on(0, peer_of(0, s))

    def pass_far(s):
        direct(0, s).wait_recv()
        direct(1, s).wait_recv()

        @pl.when(c == 0)
        def _():
            send_on(0, far_of(0, s))

    start_keys(0)
    each(0, HALF, start_far)
    start_keys(1)
    start_rows_of(0, 0)
    local(0, 0).wait()
    local(0, 1).wait()

    send_on(0, u)
    keys_here(0, 1)
    send_on(0, peer_of(0, 1))

    for table in tables:
        table.wait()
    docs = code_ref[...]

    def look_up(d, lang):
        return lang + jnp.where(docs == d, lang_ref[d], 0)

    lang = lax.fori_loop(0, lang_ref.shape[0], look_up, jnp.zeros_like(docs))
    code_ref[...] = docs * LANGS + lang

    window_first = (b - 1) * tiles_here

    def slot_of(cand):
        return jnp.clip(cand - window_first, 0, 2 * tiles_here - 1)

    def plan(j):
        group = group_of(j)
        count = HALF * list_count
        slots = [
            slot_of(list_ref[group, l, b * tiles_here + peer_of(j, s)]) for s in range(HALF) for l in range(list_count)
        ]
        ranks = []
        for e in range(count):
            rank = 0
            for other in range(count):
                if other < e:
                    rank = rank + jnp.where(slots[other] <= slots[e], 1, 0)
                elif other > e:
                    rank = rank + jnp.where(slots[other] < slots[e], 1, 0)
            ranks.append(rank)
        before = -1
        for i in range(count):
            entry, slot = 0, 0
            for e in range(count):
                entry = entry + jnp.where(ranks[e] == i, e, 0)
                slot = slot + jnp.where(ranks[e] == i, slots[e], 0)
            order_ref[j, i] = entry
            same_ref[j, i] = jnp.where(slot == before, 1, 0)
            before = slot
        for t in range(2 * tiles_here):
            upto, here = 0, 0
            for slot in slots:
                upto = upto + jnp.where(slot <= t, 1, 0)
                here = here + jnp.where(slot == t, 1, 0)
            place_ref[j, t] = jnp.where(here > 0, upto - 1, count)

    def prepare(t):
        key_codes[t] = jnp.broadcast_to(code_ref[pl.ds(t, 1), :], (BLOCK, BLOCK)).T
        acc[0, t] = jnp.zeros(acc.shape[2:], f32)
        acc[1, t] = jnp.zeros(acc.shape[2:], f32)

    each(0, 2 * tiles_here, prepare)
    for j in range(2):
        plan(j)
        sums[j, HALF * list_count] = jnp.zeros(sums.shape[2:], f32)

    @pl.when(b == 0)
    def _():
        for window in windows:
            window[0:tiles_here] = jnp.zeros((tiles_here,) + window.shape[1:], window.dtype)

    scaling = float(DH) ** (-0.5)
    across = (((1,), (1,)), ((), ()))
    gap = lax.broadcasted_iota(jnp.int32, (BLOCK, BLOCK), 0) - lax.broadcasted_iota(
        jnp.int32, (BLOCK, BLOCK), 1
    )

    def query_work(j, s, grad_scores, key_part):
        grad_query = scaling * lax.dot_general(
            key_part, grad_scores, (((0,), (0,)), ((), ())), preferred_element_type=f32
        )
        for h in range(HALF):
            turned = grad_query[:, h * BLOCK : (h + 1) * BLOCK].T
            dq_all[j, s, :, h * DH : (h + 1) * DH] = turned.astype(dq_all.dtype)

    def tile_work(j, s):
        group = group_of(j)
        place = peer_of(j, s)
        tile = b * tiles_here + place
        listed = [list_ref[group, l, tile] for l in range(list_count)]
        cands = [tile - 1, tile] + listed
        own_slot = tiles_here + place
        query_code = code_ref[pl.ds(own_slot, 1), :]
        query_lang = query_code & (LANGS - 1)
        slots = []
        biases = []
        for n, cand in enumerate(cands):
            usable = cand >= 0
            for other in cands[: n if n >= 2 else 0]:
                usable = usable & (cand != other)
            marked = cand == listed[0]
            for other in listed[1:]:
                marked = marked | (cand == other)
            slot = own_slot - 1 + n if n < 2 else slot_of(cand)
            limit = jnp.where(usable, (tile - cand) * BLOCK, -2 * BLOCK)
            seen_lang = jnp.where(marked, query_lang, -1)
            key_code = key_codes[slot]
            allowed = (gap <= limit) & (
                (key_code == query_code) | ((key_code & (LANGS - 1)) == seen_lang)
            )
            slots.append(slot)
            biases.append(jnp.where(allowed, 0.0, MASKED))

        def stacked(rows):
            return jnp.concatenate([rows[:, h * DH : (h + 1) * DH] for h in range(HALF)], 0)

        bias = jnp.concatenate(biases, axis=0)
        bias = jnp.concatenate([bias] * HALF, axis=1)
        key_part = jnp.concatenate([windows[j][t, 0] for t in slots], axis=0)
        value_part = jnp.concatenate([windows[j][t, 1] for t in slots], axis=0)
        query_part = stacked(q_all[j, s])
        dout_part = stacked(do_all[j, s])
        delta_tile = dl_all[j, s]
        delta = jnp.concatenate([delta_tile[h : h + 1, :] for h in range(HALF)], axis=1)
        scores = lax.dot_general(key_part, query_part, across, preferred_element_type=f32)
        scores = scores * (scaling * LOG2_E) + bias
        top = jnp.max(scores, axis=0, keepdims=True)
        raised = jnp.exp2(scores - top)
        weights = raised * (1.0 / jnp.sum(raised, axis=0, keepdims=True))
        grad_weights = lax.dot_general(value_part, dout_part, across, preferred_element_type=f32)
        grad_scores = (weights * (grad_weights - delta)).astype(jnp.bfloat16)
        if j == 1:
            scores_held[s] = grad_scores
        else:
            query_work(j, s, grad_scores, key_part)
        grad_key = scaling * jnp.dot(grad_scores, query_part, preferred_element_type=f32)
        grad_value = jnp.dot(weights.astype(jnp.bfloat16), dout_part, preferred_element_type=f32)
        for k, part in ((0, grad_key), (1, grad_value)):
            for n in range(2):
                acc[j, slots[n], k] += part[n * BLOCK : (n + 1) * BLOCK]
            for l in range(list_count):
                first = (2 + l) * BLOCK
                entries[s * list_count + l, k] = part[first : first + BLOCK]

    def add_listed(j):
        sums[j, 0] = entries[order_ref[j, 0]]

        def body(i):
            earlier = jnp.where(same_ref[j, i] == 1, sums[j, i - 1], 0.0)
            sums[j, i] = entries[order_ref[j, i]] + earlier

        each(1, HALF * list_count, body)

    def slot_sum(j, t):
        return acc[j, t] + sums[j, place_ref[j, t]]

    def arrived(j):
        @pl.when(has_prev)
        def _():
            each(0, tiles_here, lambda a: forward(j, a).wait_recv())

    def give_back(j):
        add_listed(j)

        @pl.when(has_prev)
        def _():
            def body(a):
                back[j, a] = slot_sum(j, a).astype(back.dtype)
                backward(j, a).start()

            last_first(lambda s: body(far_of(j, s)))
            last_first(lambda s: body(peer_of(j, s)))

    def send_queries(j, s):
        @pl.when(s > 0)
        def _():
            outward(j, 2, s).start()

        @pl.when(s == 0)
        def _():
            out_own(j, 2).start()

    def late_queries(s):
        place = tiles_here + peer_of(1, s)
        slots = [place - 1, place] + [
            slot_of(list_ref[group_of(1), l, b * tiles_here + peer_of(1, s)]) for l in range(list_count)
        ]
        query_work(1, s, scores_held[s], jnp.concatenate([windows[1][t, 0] for t in slots], axis=0))
        send_queries(1, s)

    def work(j, s):
        @pl.when(s > 0)
        def _():
            for kind in (2, 3, 4):
                inward(j, kind, s).wait_recv()

        tile_work(j, s)

        if j == 0:
            send_queries(j, s)

    def with_returned(j, a, then):
        @pl.when(has_next)
        def _():
            backward(j, a).wait_recv()
            then(slot_sum(j, tiles_here + a) + returned[j, a].astype(f32))

        @pl.when(b == n_blk - 1)
        def _():
            then(slot_sum(j, tiles_here + a))

    def settle_far(j, s):
        def then(value):
            across_out[j, s] = value.astype(across_out.dtype)

        with_returned(j, far_of(j, s), then)
        over(j, s).start()

    def settle(j, s):
        over(j, s).wait_recv()

        def then(value):
            total[j, s] = (value + across_in[j, s].astype(f32)).astype(total.dtype)

        with_returned(j, peer_of(j, s), then)

        @pl.when(s > 0)
        def _():
            outward(j, 0, s).start()
            outward(j, 1, s).start()

        @pl.when(s == 0)
        def _():
            out_own(j, 0).start()
            out_own(j, 1).start()

    each(2, HALF, pass_near)
    each(0, HALF, pass_far)
    local(1, 0).wait()
    local(1, 1).wait()
    relay(0).start()

    def relay_keys(s):
        keys_here(1, s)
        relay(s).start()

    each(1, HALF, relay_keys)
    start_rows_of(0, 1)
    start_rows(1)

    @pl.when(c == 1)
    def _():
        pl.semaphore_wait(gate.at[0], 1)
        each(2, HALF, lambda s: send_on(0, peer_of(0, s)))
        each(0, HALF, lambda s: send_on(0, far_of(0, s)))
        drained(0)
        let_go(1)

    @pl.when(c == 0)
    def _():
        drained(0)
        let_go(0)

    arrived(0)
    for kind in (2, 3, 4):
        local(0, kind).wait()

    def first_step(s):
        work(0, s)

    each(0, HALF, first_step)
    give_back(0)

    @pl.when(c == 0)
    def _():
        pl.semaphore_wait(gate.at[1], 1)

    @pl.when(c == 1)
    def _():
        pl.semaphore_wait(gate.at[2], 1)

    last_first(lambda s: send_on(1, peer_of(1, s)))

    def pass_far_second(s):
        relay(s).wait_recv()
        send_on(1, far_of(1, s))

    each(0, HALF, pass_far_second)

    @pl.when(c == 0)
    def _():
        drained(1)
        let_go(2)

    last_first(lambda s: settle_far(0, s))
    arrived(1)
    for kind in (2, 3, 4):
        local(1, kind).wait()

    last_first(lambda s: work(1, s))
    give_back(1)
    last_first(lambda s: settle(0, s))
    last_first(late_queries)
    last_first(lambda s: settle_far(1, s))
    last_first(lambda s: settle(1, s))

    for j in range(2):
        for kind in range(3):
            out_own(j, kind).wait()

        def finish(s):
            for kind in range(3):
                outward(j, kind, s).wait_recv()
            for kind in range(5):
                inward(j, kind, s).wait_send()
            for kind in range(3):
                outward(j, kind, s).wait_send()

        each(1, HALF, finish)

        def finish_far(s):
            over(j, s).wait_send()
            if j == 0:
                direct(0, s).wait_send()
                direct(1, s).wait_send()
            else:
                relay(s).wait_send()

        each(0, HALF, finish_far)

        @pl.when(has_next)
        def _():
            if j == 0:
                each(HALF - SLACK, HALF, lambda s: forward(j, far_of(j, s)).wait_send())
            else:

                @pl.when(c == 0)
                def _():
                    each(HALF - SLACK, HALF, lambda s: forward(j, far_of(j, s)).wait_send())

                @pl.when(c == 1)
                def _():
                    each(0, tiles_here, lambda a: forward(j, a).wait_send())

        @pl.when(has_prev)
        def _():
            each(0, tiles_here, lambda a: backward(j, a).wait_send())


def split_grads(lists, doc_lang, docs, queries, grad_out, keys, values, delta_rows, n_blk):
    list_count = lists.shape[1]
    width = HALF * DH
    anywhere = pl.BlockSpec(memory_space=pl.ANY)
    bf16, f32 = jnp.bfloat16, jnp.float32
    pair = (2, BLOCK, DH)
    dma = pltpu.SemaphoreType.DMA
    entry_count = HALF * list_count
    return pl.pallas_call(
        functools.partial(split_kernel, n_blk, list_count),
        out_shape=(
            jax.ShapeDtypeStruct(queries.shape, bf16),
            jax.ShapeDtypeStruct(keys.shape, bf16),
            jax.ShapeDtypeStruct(values.shape, bf16),
        ),
        in_specs=[anywhere] * 8,
        out_specs=(anywhere,) * 3,
        scratch_shapes=[
            pltpu.VMEM((2, HALF, BLOCK, width), bf16),
            pltpu.VMEM((2, HALF, BLOCK, width), bf16),
            pltpu.VMEM((2, HALF, HALF, BLOCK), f32),
            pltpu.VMEM((2 * SPLIT,) + pair, bf16),
            pltpu.VMEM((2 * SPLIT,) + pair, bf16),
            pltpu.SMEM(lists.shape, jnp.int32),
            pltpu.SMEM(doc_lang.shape, jnp.int32),
            pltpu.SMEM((2, entry_count), jnp.int32),
            pltpu.SMEM((2, entry_count), jnp.int32),
            pltpu.SMEM((2, 2 * SPLIT), jnp.int32),
            pltpu.VMEM((2 * SPLIT, BLOCK), jnp.int32),
            pltpu.VMEM((2 * SPLIT, BLOCK, BLOCK), jnp.int32),
            pltpu.VMEM((2, 2 * SPLIT) + pair, f32),
            pltpu.VMEM((entry_count,) + pair, f32),
            pltpu.VMEM((2, entry_count + 1) + pair, f32),
            pltpu.VMEM((HALF, (2 + list_count) * BLOCK, width), bf16),
            pltpu.VMEM((2, HALF, BLOCK, width), bf16),
            pltpu.VMEM((2, SPLIT) + pair, bf16),
            pltpu.VMEM((2, SPLIT) + pair, bf16),
            pltpu.VMEM((2, HALF) + pair, bf16),
            pltpu.VMEM((2, HALF) + pair, bf16),
            pltpu.VMEM((2, HALF) + pair, bf16),
            dma((2, 5, HALF)),
            dma((2, 5, HALF)),
            dma((2, 5)),
            dma((2, HALF)),
            dma((2, HALF)),
            dma((HALF,)),
            dma((HALF,)),
            dma((2, SPLIT)),
            dma((2, SPLIT)),
            dma((2, SPLIT)),
            dma((2, SPLIT)),
            dma((2, HALF)),
            dma((2, HALF)),
            dma((2, 3, HALF)),
            dma((2, 3, HALF)),
            dma((2, 3)),
            dma((4,)),
            pltpu.SemaphoreType.REGULAR((3,)),
        ],
        compiler_params=pltpu.CompilerParams(
            collective_id=0, has_side_effects=True, vmem_limit_bytes=VMEM_LIMIT
        ),
        name="split_grads",
    )(lists, doc_lang, docs, queries, grad_out, keys, values, delta_rows)


def hand_over_kernel(*refs):
    count = (len(refs) - 2) // 3
    in_sem, out_sem = refs[-2:]
    moves = []
    for k in range(count):
        src, dst, held = refs[k], refs[count + k], refs[2 * count + k]
        part = src.shape[0] // CHUNKS
        for c in range(CHUNKS):
            rows = pl.ds(c * part, part)
            moves.append(
                (
                    pltpu.make_async_copy(src.at[rows, :], held.at[rows, :], in_sem.at[k, c]),
                    pltpu.make_async_copy(held.at[rows, :], dst.at[rows, :], out_sem.at[k, c]),
                )
            )
    for fetch, _ in moves:
        fetch.start()
    for fetch, store in moves:
        fetch.wait()
        store.start()
    for _, store in moves:
        store.wait()


def handed_over(arrays):
    anywhere = pl.BlockSpec(memory_space=pl.ANY)
    count = len(arrays)
    return pl.pallas_call(
        hand_over_kernel,
        out_shape=tuple(jax.ShapeDtypeStruct(x.shape, x.dtype) for x in arrays),
        in_specs=[anywhere] * count,
        out_specs=(anywhere,) * count,
        scratch_shapes=[pltpu.VMEM(x.shape, x.dtype) for x in arrays]
        + [pltpu.SemaphoreType.DMA((count, CHUNKS)), pltpu.SemaphoreType.DMA((count, CHUNKS))],
        name="hand_over",
    )(*arrays)


def shards(queries, keys, values, grad_out, row_delta, doc_ids, doc_lang, tile_list):
    tok_count, full_width = queries.shape
    heads_all = full_width // DH
    groups_all = keys.shape[1] // DH
    repeat_count = heads_all // groups_all
    n_uly = lax.axis_size("uly")
    n_blk = lax.axis_size("blk")
    heads_here = heads_all // n_uly
    width = heads_here * DH
    copies = repeat_count // heads_here
    lists = tile_list.transpose(0, 2, 1)
    docs = doc_ids.reshape(-1, BLOCK)
    delta_rows = row_delta.T.reshape(n_uly, heads_here, tok_count)
    if n_uly == SPLIT and groups_all == SPLIT and repeat_count == HALF and tok_count == BLOCK:
        return handed_over(
            split_grads(lists, doc_lang, docs, queries, grad_out, keys, values, delta_rows, n_blk)
        )
    anywhere = pl.BlockSpec(memory_space=pl.ANY)
    in_vmem = pl.BlockSpec(memory_space=pltpu.VMEM)
    kv_spec = in_vmem if copies > 1 else anywhere
    bf16, f32 = jnp.bfloat16, jnp.float32
    pair = (2, BLOCK, DH)
    dma = pltpu.SemaphoreType.DMA
    outs = pl.pallas_call(
        functools.partial(
            fused_kernel,
            n_blk,
            n_uly,
            tile_list.shape[2],
            heads_here,
            repeat_count,
        ),
        out_shape=(
            jax.ShapeDtypeStruct(queries.shape, bf16),
            jax.ShapeDtypeStruct(keys.shape, bf16),
            jax.ShapeDtypeStruct(values.shape, bf16),
        ),
        in_specs=[anywhere] * 8,
        out_specs=(anywhere, kv_spec, kv_spec),
        scratch_shapes=[
            pltpu.VMEM((n_uly, BLOCK, width), bf16),
            pltpu.VMEM((n_uly, BLOCK, width), bf16),
            pltpu.VMEM((n_uly, heads_here, BLOCK), f32),
            pltpu.VMEM((2 * n_uly,) + pair, bf16),
            pltpu.SMEM(lists.shape, jnp.int32),
            pltpu.SMEM(doc_lang.shape, jnp.int32),
            pltpu.VMEM((2 * n_uly, BLOCK), jnp.int32),
            pltpu.VMEM((2 * n_uly, BLOCK, BLOCK), jnp.int32),
            pltpu.VMEM((2 * n_uly,) + pair, f32),
            pltpu.VMEM((n_uly, BLOCK, width), bf16),
            pltpu.VMEM((n_uly,) + pair, bf16),
            pltpu.VMEM((n_uly,) + pair, bf16),
            pltpu.VMEM((n_uly,) + pair, bf16),
            pltpu.VMEM((2, n_uly if copies > 1 else 1, BLOCK, DH), bf16),
            dma((5, n_uly)),
            dma((5, n_uly)),
            dma((5,)),
            dma((n_uly,)),
            dma((n_uly,)),
            dma((n_uly,)),
            dma((n_uly,)),
            dma((3, n_uly)),
            dma((3, n_uly)),
            dma((3,)),
            dma((4,)),
        ],
        compiler_params=pltpu.CompilerParams(
            collective_id=0, has_side_effects=True, vmem_limit_bytes=VMEM_LIMIT
        ),
        name="attention_grads",
    )(lists, doc_lang, docs, queries, grad_out, keys, values, delta_rows)
    return handed_over(outs)


def solution(mesh):
    placed = (
        P(("blk", "uly"), None),
        P(("blk", "uly"), None),
        P(("blk", "uly"), None),
        P(("blk", "uly"), None),
        P(("blk", "uly"), None),
        P(),
        P(),
        P(),
    )
    return jax.shard_map(
        shards,
        mesh=mesh,
        in_specs=placed,
        out_specs=(P(("blk", "uly"), None), P(("blk", "uly"), None), P(("blk", "uly"), None)),
        check_vma=False,
    )
```
